32 devices in a mesh: term: 8 (over z, x), sector: 4 (over y, core).
Axes of the slice: x: 2, y: 2, z: 4, core: 2. Of those that a mesh axis runs over, the one named last changes fastest.
Arguments:
- psi_start: float32 [4, 384, 384], P('sector'), may hold values from -6 to 6
- diagonal: float32 [4, 384, 384], P('sector'), may hold values from -3 to 3
- left_ops: float32 [128, 384, 384], P(('term', 'sector')), may hold values from -0.3125 to 0.3125
- right_ops: float32 [128, 384, 384], P(('term', 'sector')), may hold values from -0.078125 to 0.078125
- pair_in: int32 [32, 4], P(('term', 'sector')), may hold values from 0 to 3
- pair_out: int32 [32, 4], P(('term', 'sector')), may hold values from 0 to 3
- pair_count: int32 [32], P(('term', 'sector')), may hold values from 1 to 4, as said below
Outputs:
- psi_final: float32 [4, 384, 384], P('sector')
- energies: float32 [2], replicated
The draws below stay inside these ranges and needn't reach their ends.
Inputs may be any that keep to these rules, and one draw needn't show every extreme that they name: `pair_count`: some device has all 4 slots live in every draw.
All inputs are finite; a program needn't handle non-finite values.
Results may differ from the reference program's by a relative error of at most 0.00013.
Values sent between devices are 32-bit elements; how exact they have to be, the bound alone decides.
No kernel may reach another device: no remote copies, remote signals or barrier semaphores. Data moves between devices by JAX's collectives and lax.ppermute only.
A program may use at most 64 MiB of HBM per device.

```python
import jax
import jax.numpy as jnp
from jax import lax

B = 384
PAIRS = 4
ITERS = 2
SECTORS = 4
TERMS_SEC = 32
DEVICES = 32


def draw_pair_count(key, part):
    first_key, second_key = jax.random.split(jax.random.fold_in(key, 17))
    counts = jax.random.randint(first_key, (DEVICES,), 1, PAIRS + 1)
    chosen = jax.random.randint(second_key, (), 0, DEVICES)
    return jnp.where(jnp.arange(DEVICES) == chosen, PAIRS, counts).astype(jnp.int32)


def with_ends(drawn, stream_key, least, high):
    longest = drawn.shape.index(max(drawn.shape))
    spots = []
    for shift in (0, 1):
        where = [jax.random.randint(jax.random.fold_in(stream_key, axis), (), 0, length) for axis, length in enumerate(drawn.shape)]
        where[longest] = (where[longest] + shift) % drawn.shape[longest]
        spots.append(tuple(where))
    return drawn.at[spots[0]].set(least).at[spots[1]].set(high)


def level_of(rng, dims, cuts, low, largest):
    gain, own = 1.0, jax.random.fold_in(rng, 6)
    for position, parts in cuts:
        draws = jnp.exp(jax.random.uniform(jax.random.fold_in(own, position), (parts,), jnp.float32, low / len(cuts), largest / len(cuts)))
        gain = gain * jnp.repeat(draws, dims[position] // parts).reshape([-1 if axis == position else 1 for axis in range(len(dims))])
    return gain


def scatter_about(own_key, extent, deviation, most, shards=(), kind=jnp.bfloat16):
    values = deviation * jax.random.normal(own_key, extent, jnp.float32)
    if shards:
        values = values * level_of(own_key, extent, shards, -0.22, 0.18)
    return jnp.clip(values, -most, most).astype(kind)


def setup_inputs(seed: int = 0) -> dict:
    key_of = jax.random.split(jax.random.key(seed), 8)
    return {
        "psi_start": scatter_about(key_of[0], (SECTORS, B, B), 1.0, 6.0, ((0, 4),), jnp.float32),
        "diagonal": jnp.clip(jax.random.uniform(key_of[1], (SECTORS, B, B), jnp.float32, -3.0, 3.0) * level_of(key_of[1], (SECTORS, B, B), ((0, 4),), -0.4, 0.0), -3.0, 3.0),
        "left_ops": scatter_about(key_of[2], (DEVICES * PAIRS, B, B), B ** -0.5, 0.3125, ((0, 32),), jnp.float32),
        "right_ops": scatter_about(key_of[3], (DEVICES * PAIRS, B, B), (B * TERMS_SEC // 2) ** -0.5, 0.078125, ((0, 32),), jnp.float32),
        "pair_in": with_ends(jax.random.randint(key_of[4], (DEVICES, PAIRS), 0, SECTORS), jax.random.fold_in(key_of[4], 1), 0, SECTORS - 1).astype(jnp.int32),
        "pair_out": with_ends(jax.random.randint(key_of[5], (DEVICES, PAIRS), 0, SECTORS), jax.random.fold_in(key_of[5], 1), 0, SECTORS - 1).astype(jnp.int32),
        "pair_count": draw_pair_count(jax.random.fold_in(key_of[7], 71), 0),
    }


epsilon = 1e-06

def reference(psi_start, diagonal, left_ops, right_ops, pair_in, pair_out, pair_count):
    flat_in = pair_in.reshape(-1).astype(jnp.int32)
    flat_out = pair_out.reshape(-1).astype(jnp.int32)
    slot_ids = jnp.arange(flat_in.shape[0], dtype=jnp.int32)
    live = (slot_ids % PAIRS < jnp.repeat(pair_count, PAIRS)).astype(jnp.float32)

    def apply_all(vector):

        def one_pair(pair_slot, partial_value):
            source = lax.dynamic_index_in_dim(vector, flat_in[pair_slot], 0, keepdims=False)
            left_block = lax.dynamic_index_in_dim(left_ops, pair_slot, 0, keepdims=False)
            right_block = lax.dynamic_index_in_dim(right_ops, pair_slot, 0, keepdims=False)
            inner_prod = jnp.dot(left_block, source, precision=lax.Precision.HIGHEST)
            product = lax.dot_general(inner_prod, right_block, (((1,), (1,)), ((), ())), precision=lax.Precision.HIGHEST)
            product = product * live[pair_slot]
            target = flat_out[pair_slot]
            current = lax.dynamic_index_in_dim(partial_value, target, 0, keepdims=False)
            return lax.dynamic_update_index_in_dim(partial_value, current + product, target, 0)
        return lax.fori_loop(0, flat_in.shape[0], one_pair, jnp.zeros_like(vector))
    vector = psi_start
    energies = []
    for sweep in range(ITERS):
        mean_square = jnp.mean(vector * vector) + epsilon
        normed = vector / jnp.sqrt(mean_square)
        sigma = apply_all(normed)
        rayleigh = jnp.mean(normed * sigma)
        residual = sigma - rayleigh * normed
        correction = residual / jnp.maximum(jnp.abs(diagonal - rayleigh), 1.0)
        vector = normed - correction
        energies.append(rayleigh)
    return (vector, jnp.stack(energies))
```

```python
import functools

import jax
import jax.numpy as jnp
from jax import lax
from jax.experimental import pallas as pl
from jax.experimental.pallas import tpu as pltpu
from jax.sharding import PartitionSpec as P

ITERS = 2
AXES = ("term", "sector")
LANE_ROWS = 8

epsilon = 1e-06

VMEM = pl.BlockSpec(memory_space=pltpu.VMEM)
SMEM = pl.BlockSpec(memory_space=pltpu.SMEM)
F32 = jnp.float32
BF16 = jnp.bfloat16

ORDERS = (
    (("sector", 1), ("term", 0), ("term", 1)),
    (("term", 1), ("sector", 1), ("term", 0)),
)


def bit_of(axis, bit):
    return (lax.axis_index(axis) >> bit) & 1


def order_bits(core):
    a = [bit_of(axis, bit) for axis, bit in ORDERS[0]]
    b = [bit_of(axis, bit) for axis, bit in ORDERS[1]]
    return [jnp.where(core == 0, x, y) for x, y in zip(a, b)]


def place(core, bits, quarter):
    b1, b2, b3 = bits
    sector = jnp.where(core == 0, 2 * b1, 2 * b2 + 1)
    row = jnp.where(core == 0, 2 * b2 + b3, 2 * b1 + b3) * quarter
    return sector, pl.multiple_of(row, 8)


def split(x):
    high = x.astype(BF16)
    return high, (x - high.astype(F32)).astype(BF16)


def prep_kernel(left_ref, right_ref, lh_ref, ll_ref, rh_ref, rl_ref):
    lh_ref[...], ll_ref[...] = split(left_ref[...])
    rh_ref[...], rl_ref[...] = split(right_ref[...])


def prepare(left_ops, right_ops):
    pairs, b, _ = left_ops.shape
    spec = pl.BlockSpec((1, b, b), lambda i: (i, 0, 0))
    return pl.pallas_call(
        prep_kernel,
        grid=(pairs,),
        in_specs=[spec] * 2,
        out_specs=[spec] * 4,
        out_shape=[jax.ShapeDtypeStruct(left_ops.shape, BF16)] * 4,
        cost_estimate=pl.CostEstimate(
            flops=4 * left_ops.size, bytes_accessed=16 * left_ops.size, transcendentals=0
        ),
    )(left_ops, right_ops)


def apply_kernel(first, cells, *refs):
    (in_ref, out_ref, count_ref, p0, p1, p2, p3, lh, ll, rh, rl,
     send_ref, keep_ref, inv_ref, vec, vh, vl, acc) = refs
    sectors, b, _ = vec.shape
    quarter = b // 4
    me = lax.axis_index("sector")
    core = me & 1
    total = jnp.zeros((1, b), F32)
    for number, piece in enumerate((p0, p1, p2, p3)):
        if first:
            chunks = [(me ^ number, (0), 0, b)]
        else:
            of = core if number < 2 else 1 - core
            base = order_bits(of)
            chunks = []
            for k in range(4):
                bits = (base[0] ^ (number & 1), base[1] ^ (k >> 1), base[2] ^ (k & 1))
                sector, row = place(of, bits, quarter)
                chunks.append((sector, row, k * quarter, quarter))
        for sector, row, start, rows in chunks:
            x = piece[start:start + rows, :]
            high, low = split(x)
            vec[sector, pl.ds(row, rows), :] = x
            vh[sector, pl.ds(row, rows), :] = high
            vl[sector, pl.ds(row, rows), :] = low
            total += jnp.sum(x * x, axis=0, keepdims=True)
    inv = lax.rsqrt(jnp.broadcast_to(jnp.sum(total, axis=1, keepdims=True), (LANE_ROWS, b)) / cells + epsilon)
    inv_ref[...] = inv
    acc[...] = jnp.zeros_like(acc)

    def one_pair(p, carry):
        source = in_ref[0, p]
        target = out_ref[0, p]
        dot = functools.partial(jnp.dot, preferred_element_type=F32)
        a_h, a_l = lh[p], ll[p]
        x_h, x_l = vh[source], vl[source]
        inner = dot(a_h, x_h) + (dot(a_h, x_l) + dot(a_l, x_h))
        i_h, i_l = split(inner)
        r_h, r_l = rh[p], rl[p]
        nt = functools.partial(
            lax.dot_general, dimension_numbers=(((1,), (1,)), ((), ())), preferred_element_type=F32
        )
        acc[target] += nt(i_h, r_h) + (nt(i_h, r_l) + nt(i_l, r_h))
        return carry

    lax.fori_loop(0, count_ref[0], one_pair, 0)
    scale = inv[:1, :]
    rho = jnp.zeros((1, b), F32)
    for dest, of in ((send_ref, 1 - core), (keep_ref, core)):
        for j in range(8):
            sector, row = place(of, (j >> 2, (j >> 1) & 1, j & 1), quarter)
            x = acc[sector, pl.ds(row, quarter), :] * scale
            dest[j * quarter:(j + 1) * quarter, :] = x
            rho += jnp.sum(x * vec[sector, pl.ds(row, quarter), :], axis=0, keepdims=True)
    rho = jnp.broadcast_to(jnp.sum(rho * scale, axis=1, keepdims=True), (LANE_ROWS, b)) / cells
    send_ref[8 * quarter:, :] = rho
    keep_ref[8 * quarter:, :] = rho


def apply_pairs(first, cells, sectors, index, pieces, ops):
    pairs, b, _ = ops[0].shape
    rows = sectors * b // 2 + LANE_ROWS
    half = jax.ShapeDtypeStruct((rows, b), F32)
    return pl.pallas_call(
        functools.partial(apply_kernel, first, cells),
        in_specs=[SMEM] * 3 + [VMEM] * 8,
        out_specs=[VMEM] * 3,
        out_shape=[half, half, jax.ShapeDtypeStruct((LANE_ROWS, b), F32)],
        scratch_shapes=[
            pltpu.VMEM((sectors, b, b), F32),
            pltpu.VMEM((sectors, b, b), BF16),
            pltpu.VMEM((sectors, b, b), BF16),
            pltpu.VMEM((sectors, b, b), F32),
        ],
        compiler_params=pltpu.CompilerParams(vmem_limit_bytes=32 << 20),
    )(*index, *pieces, *ops)


def combine_kernel(step, keep_ref, recv_ref, send_ref, next_ref):
    rows = send_ref.shape[0] - LANE_ROWS
    bit = order_bits(bit_of("sector", 0))[step]
    for dest, which in ((send_ref, 1 - bit), (next_ref, bit)):
        at = pl.ds(pl.multiple_of(which * rows, 8), rows)
        dest[:rows, :] = keep_ref[at, :] + recv_ref[at, :]
        dest[rows:, :] = keep_ref[2 * rows:, :] + recv_ref[2 * rows:, :]


def combine(step, keep, recv):
    rows = (keep.shape[0] - LANE_ROWS) // 2 + LANE_ROWS
    shape = jax.ShapeDtypeStruct((rows, keep.shape[1]), F32)
    return pl.pallas_call(
        functools.partial(combine_kernel, step),
        in_specs=[VMEM] * 2,
        out_specs=[VMEM] * 2,
        out_shape=[shape] * 2,
    )(keep, recv)


def update_kernel(mine_ref, recv_ref, vec_ref, inv_ref, diag_ref, new_ref, energy_ref):
    rows = new_ref.shape[0]
    rho = mine_ref[rows:, :] + recv_ref[rows:, :]
    energy_ref[...] = rho[:, :energy_ref.shape[1]]
    rho = rho[:1, :]
    normed = vec_ref[...] * inv_ref[:1, :]
    sigma = mine_ref[:rows, :] + recv_ref[:rows, :]
    residual = sigma - rho * normed
    new_ref[...] = normed - residual / jnp.maximum(jnp.abs(diag_ref[...] - rho), 1.0)


def update(mine, recv, vec, inv, diag):
    return pl.pallas_call(
        update_kernel,
        in_specs=[VMEM] * 5,
        out_specs=[VMEM] * 2,
        out_shape=[
            jax.ShapeDtypeStruct(vec.shape, F32),
            jax.ShapeDtypeStruct((LANE_ROWS, 128), F32),
        ],
    )(mine, recv, vec, inv, diag)


def flips(mesh_shape, dims):
    terms, sectors = mesh_shape
    pairs = []
    for t in range(terms):
        for s in range(sectors):
            axis, bit = dims[s & 1]
            u, v = (t ^ (1 << bit), s) if axis == "term" else (t, s ^ (1 << bit))
            pairs.append((t * sectors + s, u * sectors + v))
    return pairs


def shards(mesh_shape, psi_start, diagonal, left_ops, right_ops, pair_in, pair_out, pair_count):
    terms, sectors = mesh_shape
    b = psi_start.shape[1]
    quarter = b // 4
    cells = float(sectors * b * b)
    index = (pair_in, pair_out, pair_count)

    def swap(x, *dims):
        return lax.ppermute(x, AXES, flips(mesh_shape, dims * 2 if len(dims) == 1 else dims))

    steps = list(zip(*ORDERS))
    core_step = ("sector", 0)
    rest = [("term", bit) for bit in range(2, terms.bit_length() - 1)]
    core = bit_of("sector", 0)
    _, row = place(core, order_bits(core), quarter)

    own = psi_start[0]
    across = swap(own, ("sector", 1))
    beside = swap(own, core_step)
    ops = prepare(left_ops, right_ops)
    corner = swap(across, core_step)
    pieces = (own, beside, across, corner)
    vec = lax.dynamic_slice(own, (row, 0), (quarter, b))
    diag = lax.dynamic_slice(diagonal[0], (row, 0), (quarter, b))
    energies = []
    for sweep in range(ITERS):
        send, keep, inv = apply_pairs(sweep == 0, cells, sectors, index, pieces, ops)
        recv = swap(send, core_step)
        for number, step in enumerate(steps):
            send, keep = combine(number, keep, recv)
            recv = swap(send, *step)
        mine = keep + recv
        for step in rest[:-1]:
            mine = mine + swap(mine, step)
        recv = swap(mine, rest[-1])
        vec, energy = update(mine, recv, vec, inv, diag)
        energies.append(energy[0, 0])
        last = sweep == ITERS - 1
        if not last:
            part = jnp.concatenate([vec, swap(vec, *steps[2])], 0)
            part = jnp.concatenate([part, swap(part, *steps[1])], 0)
            far = swap(part, *steps[0])
            pieces = (part, far, swap(part, core_step), swap(far, core_step))
    other = swap(vec, *steps[2])
    bits = order_bits(core)
    half = jnp.where(bits[2] == 0, jnp.concatenate([vec, other], 0), jnp.concatenate([other, vec], 0))
    last_step = (ORDERS[0][1], ORDERS[1][0])
    other = swap(half, *last_step)
    bit = jnp.where(core == 0, bits[1], bits[0])
    block = jnp.where(bit == 0, jnp.concatenate([half, other], 0), jnp.concatenate([other, half], 0))
    return block[None], jnp.stack(energies)


def solution(mesh):
    mesh_shape = (mesh.shape["term"], mesh.shape["sector"])
    return jax.shard_map(
        functools.partial(shards, mesh_shape),
        mesh=mesh,
        in_specs=(
            P("sector", None, None),
            P("sector", None, None),
            P(("term", "sector"), None, None),
            P(("term", "sector"), None, None),
            P(("term", "sector"), None),
            P(("term", "sector"), None),
            P(("term", "sector")),
        ),
        out_specs=(P("sector", None, None), P()),
        check_vma=False,
    )
```

```python
import functools

import jax
import jax.numpy as jnp
from jax import lax
from jax.experimental import pallas as pl
from jax.experimental.pallas import tpu as pltpu
from jax.sharding import PartitionSpec as P

ITERS = 2
AXES = ("term", "sector")
TILE = (8, 128)

epsilon = 1e-06


VMEM = pl.BlockSpec(memory_space=pltpu.VMEM)
SMEM = pl.BlockSpec(memory_space=pltpu.SMEM)
F32 = jnp.float32
BF16 = jnp.bfloat16

DIMS = (("sector", 1), ("term", 0), ("term", 1))
CORE = ("sector", 0)


def grant(mib):
    return pltpu.CompilerParams(vmem_limit_bytes=mib << 20)


def bit_of(axis, bit):
    return (lax.axis_index(axis) >> bit) & 1


def place(parity, k, quarter):
    b = [bit_of(*dim) ^ ((k >> (2 - i)) & 1) for i, dim in enumerate(DIMS)]
    return 2 * b[0] + parity, pl.multiple_of((2 * b[1] + b[2]) * quarter, 8)


def split(x):
    high = x.astype(BF16)
    return high, (x - high.astype(F32)).astype(BF16)


def prep_kernel(left_ref, right_ref, lh_ref, ll_ref, rh_ref, rl_ref):
    def one(p, carry):
        lh_ref[p], ll_ref[p] = split(left_ref[p])
        rh_ref[p], rl_ref[p] = split(right_ref[p])
        return carry

    lax.fori_loop(0, left_ref.shape[0], one, 0)


def prepare(left_ops, right_ops):
    return pl.pallas_call(
        prep_kernel,
        in_specs=[VMEM] * 2,
        out_specs=[VMEM] * 4,
        out_shape=[jax.ShapeDtypeStruct(left_ops.shape, BF16)] * 4,
        compiler_params=grant(16),
        cost_estimate=pl.CostEstimate(
            flops=4 * left_ops.size, bytes_accessed=16 * left_ops.size, transcendentals=0
        ),
    )(left_ops, right_ops)


def store_wide(dest, start, x):
    rows = x.shape[0]
    for c in range(x.shape[1] // TILE[1]):
        dest[start + c * rows:start + (c + 1) * rows, :] = x[:, c * TILE[1]:(c + 1) * TILE[1]]


def load_wide(ref, rows):
    blocks = ref.shape[0] // rows
    return jnp.concatenate([ref[c * rows:(c + 1) * rows, :] for c in range(blocks)], axis=1)


def apply_kernel(first, cells, pieces, *refs):
    in_ref, out_ref, count_ref, *refs = refs
    parts = refs[:pieces]
    lh, ll, rh, rl, send_ref, keep_ref, inv_ref, vec, vh, vl, acc = refs[pieces:]
    sectors, b, _ = vec.shape
    quarter = b // 4
    me = lax.axis_index("sector")
    core = me & 1
    total = jnp.zeros((1, b), F32)
    for number, piece in enumerate(parts):
        rows = piece.shape[0]
        if first:
            sector, row = me ^ number, 0
        else:
            sector, row = place(core ^ (number & 1), number >> 1, quarter)
        x = piece[...]
        high, low = split(x)
        vec[sector, pl.ds(row, rows), :] = x
        vh[sector, pl.ds(row, rows), :] = high
        vl[sector, pl.ds(row, rows), :] = low
        total += jnp.sum(x * x, axis=0, keepdims=True)
    inv = lax.rsqrt(jnp.broadcast_to(jnp.sum(total, axis=1, keepdims=True), (TILE[0], b)) / cells + epsilon)
    inv_ref[...] = inv
    acc[...] = jnp.zeros_like(acc)

    def one_pair(p, carry):
        source = in_ref[0, p]
        target = out_ref[0, p]
        dot = functools.partial(jnp.dot, preferred_element_type=F32)
        a_h, a_l = lh[p], ll[p]
        x_h, x_l = vh[source], vl[source]
        inner = dot(a_h, x_h) + (dot(a_h, x_l) + dot(a_l, x_h))
        i_h, i_l = split(inner)
        r_h, r_l = rh[p], rl[p]
        nt = functools.partial(
            lax.dot_general, dimension_numbers=(((1,), (1,)), ((), ())), preferred_element_type=F32
        )
        acc[target] += nt(i_h, r_h) + (nt(i_h, r_l) + nt(i_l, r_h))
        return carry

    lax.fori_loop(0, count_ref[0], one_pair, 0)
    scale = inv[:1, :]
    rho = jnp.zeros((1, b), F32)
    shard = quarter * b // TILE[1]
    for dest, parity in ((send_ref, 1 - core), (keep_ref, core)):
        for k in range(8):
            sector, row = place(parity, k, quarter)
            x = acc[sector, pl.ds(row, quarter), :] * scale
            store_wide(dest, k * shard, x)
            rho += jnp.sum(x * vec[sector, pl.ds(row, quarter), :], axis=0, keepdims=True)
    rho = jnp.broadcast_to(jnp.sum(rho * scale, axis=1, keepdims=True), TILE) / cells
    send_ref[8 * shard:, :] = rho
    keep_ref[8 * shard:, :] = rho


def apply_pairs(first, cells, sectors, index, pieces, ops):
    pairs, b, _ = ops[0].shape
    rows = sectors * b // 2 * b // TILE[1] + TILE[0]
    half = jax.ShapeDtypeStruct((rows, TILE[1]), F32)
    return pl.pallas_call(
        functools.partial(apply_kernel, first, cells, len(pieces)),
        in_specs=[SMEM] * 3 + [VMEM] * (len(pieces) + 4),
        out_specs=[VMEM] * 3,
        out_shape=[half, half, jax.ShapeDtypeStruct((TILE[0], b), F32)],
        scratch_shapes=[
            pltpu.VMEM((sectors, b, b), F32),
            pltpu.VMEM((sectors, b, b), BF16),
            pltpu.VMEM((sectors, b, b), BF16),
            pltpu.VMEM((sectors, b, b), F32),
        ],
        compiler_params=grant(24),
    )(*index, *pieces, *ops)


def combine_kernel(keep_ref, recv_ref, *slots):
    rows = slots[0].shape[0] - TILE[0]
    end = len(slots) * rows
    for k, slot in enumerate(slots):
        slot[:rows, :] = keep_ref[k * rows:(k + 1) * rows, :] + recv_ref[k * rows:(k + 1) * rows, :]
        slot[rows:, :] = keep_ref[end:, :] + recv_ref[end:, :]


def combine(keep, recv):
    shape = jax.ShapeDtypeStruct(((keep.shape[0] - TILE[0]) // 8 + TILE[0], TILE[1]), F32)
    return pl.pallas_call(
        combine_kernel,
        in_specs=[VMEM] * 2,
        out_specs=[VMEM] * 8,
        out_shape=[shape] * 8,
        compiler_params=grant(6),
    )(keep, recv)


def sum_kernel(*refs):
    *parts, out_ref = refs
    total = [ref[...] for ref in parts]
    while len(total) > 1:
        total = [total[i] + total[i + 1] for i in range(0, len(total) - 1, 2)] + total[len(total) & ~1:]
    out_ref[...] = total[0]


def sum_of(parts):
    return pl.pallas_call(
        sum_kernel,
        in_specs=[VMEM] * len(parts),
        out_specs=VMEM,
        out_shape=jax.ShapeDtypeStruct(parts[0].shape, F32),
        compiler_params=grant(4),
    )(*parts)


def update_kernel(mine_ref, recv_ref, vec_ref, inv_ref, diag_ref, new_ref, energy_ref):
    rows, b = new_ref.shape
    shard = rows * b // TILE[1]
    rho = mine_ref[shard:, :] + recv_ref[shard:, :]
    energy_ref[...] = rho
    for c in range(b // TILE[1]):
        part = slice(c * rows, (c + 1) * rows)
        lanes = slice(c * TILE[1], (c + 1) * TILE[1])
        normed = vec_ref[:, lanes] * inv_ref[:1, lanes]
        sigma = mine_ref[part, :] + recv_ref[part, :]
        residual = sigma - rho[:1, :] * normed
        gap = jnp.maximum(jnp.abs(diag_ref[:, lanes] - rho[:1, :]), 1.0)
        new_ref[:, lanes] = normed - residual / gap


def update(mine, recv, vec, inv, diag):
    return pl.pallas_call(
        update_kernel,
        in_specs=[VMEM] * 5,
        out_specs=[VMEM] * 2,
        out_shape=[jax.ShapeDtypeStruct(vec.shape, F32), jax.ShapeDtypeStruct(TILE, F32)],
        compiler_params=grant(4),
    )(mine, recv, vec, inv, diag)


def join_kernel(*refs):
    *parts, out_ref = refs
    quarter = parts[0].shape[0]
    for k, part in enumerate(parts):
        _, row = place(0, k, quarter)
        out_ref[0, pl.ds(row, quarter), :] = part[...]


def join(parts):
    quarter, b = parts[0].shape
    return pl.pallas_call(
        join_kernel,
        in_specs=[VMEM] * len(parts),
        out_specs=VMEM,
        out_shape=jax.ShapeDtypeStruct((1, 4 * quarter, b), F32),
        compiler_params=grant(4),
    )(*parts)


def flips(mesh_shape, dims):
    terms, sectors = mesh_shape
    mask = {"term": 0, "sector": 0}
    for axis, bit in dims:
        mask[axis] ^= 1 << bit
    return [
        (t * sectors + s, (t ^ mask["term"]) * sectors + (s ^ mask["sector"]))
        for t in range(terms)
        for s in range(sectors)
    ]


def shards(mesh_shape, psi_start, diagonal, left_ops, right_ops, pair_in, pair_out, pair_count):
    terms, sectors = mesh_shape
    b = psi_start.shape[1]
    quarter = b // 4
    cells = float(sectors * b * b)
    index = (pair_in, pair_out, pair_count)

    def swap(x, *dims):
        return lax.ppermute(x, AXES, flips(mesh_shape, dims))

    def dims_of(k):
        return [dim for i, dim in enumerate(DIMS) if (k >> (2 - i)) & 1]

    away = sorted(range(1, 8), key=lambda k: -len(dims_of(k)))
    rest = [("term", bit) for bit in range(2, terms.bit_length() - 1)]

    own = psi_start[0]
    across = swap(own, ("sector", 1))
    beside = swap(own, CORE)
    ops = prepare(left_ops, right_ops)
    _, row = place(0, 0, quarter)
    vec = lax.dynamic_slice(own, (row, 0), (quarter, b))
    diag = lax.dynamic_slice(diagonal[0], (row, 0), (quarter, b))
    across, ops, vec, diag = lax.optimization_barrier((across, ops, vec, diag))
    corner = swap(across, CORE)
    pieces = (own, beside, across, corner)
    energies = []
    for sweep in range(ITERS):
        send, keep, inv = apply_pairs(sweep == 0, cells, sectors, index, pieces, ops)
        slots = combine(keep, swap(send, CORE))
        got = {k: swap(slots[k], *dims_of(k)) for k in away}
        mine = sum_of([slots[0]] + [got[k] for k in range(1, 8)])
        for step in rest[:-1]:
            mine = mine + swap(mine, step)
        vec, energy = update(mine, swap(mine, rest[-1]), vec, inv, diag)
        energies.append(energy[0, 0])
        if sweep < ITERS - 1:
            got = {k: swap(vec, *dims_of(k)) for k in away}
            got[0] = vec
            pieces = []
            for k in range(8):
                pieces += [got[k], swap(got[k], CORE)]
    got = {k: swap(vec, *dims_of(k)) for k in (3, 2, 1)}
    block = join([vec, got[1], got[2], got[3]])
    return block, jnp.stack(energies)


def solution(mesh):
    mesh_shape = (mesh.shape["term"], mesh.shape["sector"])
    return jax.shard_map(
        functools.partial(shards, mesh_shape),
        mesh=mesh,
        in_specs=(
            P("sector", None, None),
            P("sector", None, None),
            P(("term", "sector"), None, None),
            P(("term", "sector"), None, None),
            P(("term", "sector"), None),
            P(("term", "sector"), None),
            P(("term", "sector")),
        ),
        out_specs=(P("sector", None, None), P()),
        check_vma=False,
    )
```

```python
import functools

import jax
import jax.numpy as jnp
from jax import lax
from jax.experimental import pallas as pl
from jax.experimental.pallas import tpu as pltpu
from jax.sharding import PartitionSpec as P


ITERS = 2
AXES = ("term", "sector")
TILE = (8, 128)
CHUNKS = 2

epsilon = 1e-06


VMEM = pl.BlockSpec(memory_space=pltpu.VMEM)
SMEM = pl.BlockSpec(memory_space=pltpu.SMEM)
F32 = jnp.float32
BF16 = jnp.bfloat16

DIMS = (("sector", 1), ("term", 0), ("term", 1))
CORE = ("sector", 0)
ORDERS = ((0, 1, 2), (2, 0, 1))


def matmul_cost(pairs, rows, b):
    return pl.CostEstimate(
        flops=6 * pairs * rows * b * b, bytes_accessed=8 * pairs * b * b, transcendentals=0
    )


def grant(mib):
    return pltpu.CompilerParams(vmem_limit_bytes=mib << 20)


def bit_of(axis, bit):
    return (lax.axis_index(axis) >> bit) & 1


def place(bits, parity, rows):
    return 2 * bits[0] + parity, pl.multiple_of((2 * bits[1] + bits[2]) * rows, 8)


def piece_place(k, parity, rows):
    return place([bit_of(*dim) ^ ((k >> (2 - i)) & 1) for i, dim in enumerate(DIMS)], parity, rows)


def slot_bits(j, order):
    flip = [0, 0, 0]
    for i, dim in enumerate(order):
        flip[dim] = (j >> (2 - i)) & 1
    return flip


def slot_place(j, parity, rows):
    a, b = slot_bits(j, ORDERS[0]), slot_bits(j, ORDERS[1])
    flip = [x if x == y else jnp.where(parity == 0, x, y) for x, y in zip(a, b)]
    return place([bit_of(*dim) ^ f for dim, f in zip(DIMS, flip)], parity, rows)


def split(x):
    high = x.astype(BF16)
    return high, (x - high.astype(F32)).astype(BF16)


def prep_kernel(left_ref, right_ref, psi_ref, diag_ref, lh_ref, ll_ref, rh_ref, rl_ref, vec_ref, mine_ref):
    def one(p, carry):
        lh_ref[p], ll_ref[p] = split(left_ref[p])
        rh_ref[p], rl_ref[p] = split(right_ref[p])
        return carry

    lax.fori_loop(0, left_ref.shape[0], one, 0)
    rows = vec_ref.shape[0] // CHUNKS
    for h in range(CHUNKS):
        _, row = piece_place(0, 0, rows)
        at = pl.ds(pl.multiple_of(row + h * 4 * rows, 8), rows)
        vec_ref[h * rows:(h + 1) * rows, :] = psi_ref[0, at, :]
        mine_ref[h * rows:(h + 1) * rows, :] = diag_ref[0, at, :]


def prepare(left_ops, right_ops, psi, diag):
    b = psi.shape[-1]
    shard = jax.ShapeDtypeStruct((b // 4, b), F32)
    return pl.pallas_call(
        prep_kernel,
        in_specs=[VMEM] * 4,
        out_specs=[VMEM] * 6,
        out_shape=[jax.ShapeDtypeStruct(left_ops.shape, BF16)] * 4 + [shard] * 2,
        compiler_params=grant(16),
        cost_estimate=pl.CostEstimate(
            flops=4 * left_ops.size, bytes_accessed=16 * left_ops.size, transcendentals=0
        ),
    )(left_ops, right_ops, psi, diag)


def store_wide(dest, start, x):
    rows = x.shape[0]
    for c in range(x.shape[1] // TILE[1]):
        dest[start + c * rows:start + (c + 1) * rows, :] = x[:, c * TILE[1]:(c + 1) * TILE[1]]


DOT_NT = functools.partial(
    lax.dot_general, dimension_numbers=(((1,), (1,)), ((), ())), preferred_element_type=F32
)
DOT = functools.partial(jnp.dot, preferred_element_type=F32)


def inner_kernel(first, cells, pieces, *refs):
    in_ref, count_ref, *refs = refs
    parts = refs[:pieces]
    rh, rl, th_ref, tl_ref, inv_ref, vh, vl = refs[pieces:]
    _, b, _ = vh.shape
    me = lax.axis_index("sector")
    core = me & 1
    total = jnp.zeros((1, b), F32)
    for number, piece in enumerate(parts):
        x = piece[...]
        high, low = split(x)
        total += jnp.sum(x * x, axis=0, keepdims=True)
        if first:
            vh[me ^ number] = high
            vl[me ^ number] = low
        else:
            rows = piece.shape[0] // CHUNKS
            sector, row = piece_place(number >> 1, core ^ (number & 1), rows)
            for h in range(CHUNKS):
                at = pl.ds(pl.multiple_of(row + h * 4 * rows, 8), rows)
                vh[sector, at, :] = high[h * rows:(h + 1) * rows, :]
                vl[sector, at, :] = low[h * rows:(h + 1) * rows, :]
    inv_ref[...] = lax.rsqrt(
        jnp.broadcast_to(jnp.sum(total, axis=1, keepdims=True), (TILE[0], b)) / cells + epsilon
    )

    def one_pair(p, carry):
        source = in_ref[0, p]
        x_h, x_l = vh[source], vl[source]
        r_h, r_l = rh[p], rl[p]
        th_ref[p], tl_ref[p] = split(DOT_NT(x_h, r_h) + (DOT_NT(x_h, r_l) + DOT_NT(x_l, r_h)))
        return carry

    lax.fori_loop(0, count_ref[0], one_pair, 0)


def inner(first, cells, sectors, pair_in, pair_count, pieces, ops):
    pairs, b, _ = ops[0].shape
    half = jax.ShapeDtypeStruct(ops[0].shape, BF16)
    return pl.pallas_call(
        functools.partial(inner_kernel, first, cells, len(pieces)),
        in_specs=[SMEM] * 2 + [VMEM] * (len(pieces) + 2),
        out_specs=[VMEM] * 3,
        out_shape=[half, half, jax.ShapeDtypeStruct((TILE[0], b), F32)],
        scratch_shapes=[pltpu.VMEM((sectors, b, b), BF16), pltpu.VMEM((sectors, b, b), BF16)],
        compiler_params=grant(16),
        cost_estimate=matmul_cost(pairs, b, b),
    )(pair_in, pair_count, *pieces, *ops)


def outer_kernel(first, chunk, cells, pieces, *refs):
    out_ref, count_ref, *refs = refs
    parts = refs[:pieces]
    lh, ll, th, tl, inv_ref, before_ref, send_ref, keep_ref, rho_ref, acc = refs[pieces:]
    _, rows, b = acc.shape
    shard = rows // 4
    core = lax.axis_index("sector") & 1
    acc[...] = jnp.zeros_like(acc)
    here = slice(chunk * rows, (chunk + 1) * rows)

    def one_pair(p, carry):
        target = out_ref[0, p]
        l_h, l_l = lh[p, here, :], ll[p, here, :]
        t_h, t_l = th[p], tl[p]
        acc[target] += DOT(l_h, t_h) + (DOT(l_h, t_l) + DOT(l_l, t_h))
        return carry

    lax.fori_loop(0, count_ref[0], one_pair, 0)
    scale = inv_ref[:1, :]
    rho = jnp.zeros((1, b), F32)
    wide = shard * b // TILE[1]
    for number in range(16):
        k, parity = number >> 1, core ^ (number & 1)
        sector, row = piece_place(k, parity, shard)
        x = acc[sector, pl.ds(row, shard), :] * scale
        if first:
            part = parts[(k >> 2) * 2 + (number & 1)]
            v = part[pl.ds(pl.multiple_of(row + chunk * rows, 8), shard), :]
        else:
            v = parts[number][chunk * shard:(chunk + 1) * shard, :]
        rho += jnp.sum(x * v, axis=0, keepdims=True)
    for dest, parity in ((send_ref, 1 - core), (keep_ref, core)):
        for j in range(8):
            sector, row = slot_place(j, parity, shard)
            store_wide(dest, j * wide, acc[sector, pl.ds(row, shard), :] * scale)
    rho = jnp.broadcast_to(jnp.sum(rho * scale, axis=1, keepdims=True), TILE) / cells + before_ref[...]
    rho_ref[...] = rho
    if chunk == CHUNKS - 1:
        send_ref[8 * wide:, :] = rho
        keep_ref[8 * wide:, :] = rho


def outer(first, chunk, cells, sectors, pair_out, pair_count, pieces, ops, inv, before):
    pairs, b, _ = ops[0].shape
    rows = b // CHUNKS
    extra = TILE[0] if chunk == CHUNKS - 1 else 0
    half = jax.ShapeDtypeStruct((sectors * rows // 2 * b // TILE[1] + extra, TILE[1]), F32)
    return pl.pallas_call(
        functools.partial(outer_kernel, first, chunk, cells, len(pieces)),
        in_specs=[SMEM] * 2 + [VMEM] * (len(pieces) + 6),
        out_specs=[VMEM] * 3,
        out_shape=[half, half, jax.ShapeDtypeStruct(TILE, F32)],
        scratch_shapes=[pltpu.VMEM((sectors, rows, b), F32)],
        compiler_params=grant(20),
        cost_estimate=matmul_cost(pairs, rows, b),
    )(pair_out, pair_count, *pieces, *ops, inv, before)


def combine_kernel(keep_ref, recv_ref, next_ref, send_ref=None):
    extra = 0 if send_ref is None else 2 * next_ref.shape[0] - keep_ref.shape[0]
    rows = next_ref.shape[0] - extra
    next_ref[:rows, :] = keep_ref[:rows, :] + recv_ref[:rows, :]
    if send_ref is None:
        return
    send_ref[:rows, :] = keep_ref[rows:2 * rows, :] + recv_ref[rows:2 * rows, :]
    if extra:
        total = keep_ref[2 * rows:, :] + recv_ref[2 * rows:, :]
        next_ref[rows:, :] = total
        send_ref[rows:, :] = total


def combine(keep, recv, extra):
    shape = jax.ShapeDtypeStruct(((keep.shape[0] - extra) // 2 + extra, TILE[1]), F32)
    return pl.pallas_call(
        combine_kernel,
        in_specs=[VMEM] * 2,
        out_specs=[VMEM] * 2,
        out_shape=[shape] * 2,
        compiler_params=grant(4),
    )(keep, recv)


def total(mine, recv):
    return pl.pallas_call(
        combine_kernel,
        in_specs=[VMEM] * 2,
        out_specs=VMEM,
        out_shape=jax.ShapeDtypeStruct(mine.shape, F32),
        compiler_params=grant(4),
    )(mine, recv)


def update_kernel(*refs):
    sums, (vec_ref, inv_ref, diag_ref, new_ref, energy_ref) = refs[:2 * CHUNKS], refs[2 * CHUNKS:]
    rows, b = new_ref.shape
    shard = rows // CHUNKS
    end = shard * b // TILE[1]
    rho = sums[-2][end:, :] + sums[-1][end:, :]
    energy_ref[...] = rho
    for h in range(CHUNKS):
        mine_ref, recv_ref = sums[2 * h:2 * h + 2]
        at = slice(h * shard, (h + 1) * shard)
        for c in range(b // TILE[1]):
            part = slice(c * shard, (c + 1) * shard)
            lanes = slice(c * TILE[1], (c + 1) * TILE[1])
            normed = vec_ref[at, lanes] * inv_ref[:1, lanes]
            sigma = mine_ref[part, :] + recv_ref[part, :]
            residual = sigma - rho[:1, :] * normed
            gap = jnp.maximum(jnp.abs(diag_ref[at, lanes] - rho[:1, :]), 1.0)
            new_ref[at, lanes] = normed - residual / gap


def update(sums, vec, inv, diag):
    return pl.pallas_call(
        update_kernel,
        in_specs=[VMEM] * (len(sums) + 3),
        out_specs=[VMEM] * 2,
        out_shape=[jax.ShapeDtypeStruct(vec.shape, F32), jax.ShapeDtypeStruct(TILE, F32)],
        compiler_params=grant(4),
    )(*sums, vec, inv, diag)


def join_kernel(*refs):
    *parts, out_ref = refs
    rows = parts[0].shape[0] // CHUNKS
    for k, part in enumerate(parts):
        _, row = piece_place(k, 0, rows)
        for h in range(CHUNKS):
            at = pl.ds(pl.multiple_of(row + h * 4 * rows, 8), rows)
            out_ref[0, at, :] = part[h * rows:(h + 1) * rows, :]


def join(parts):
    quarter, b = parts[0].shape
    return pl.pallas_call(
        join_kernel,
        in_specs=[VMEM] * len(parts),
        out_specs=VMEM,
        out_shape=jax.ShapeDtypeStruct((1, 4 * quarter, b), F32),
        compiler_params=grant(4),
    )(*parts)


def flips(mesh_shape, even, odd):
    terms, sectors = mesh_shape
    pairs = []
    for t in range(terms):
        for s in range(sectors):
            u = {"term": t, "sector": s}
            for axis, bit in odd if s & 1 else even:
                u[axis] ^= 1 << bit
            pairs.append((t * sectors + s, u["term"] * sectors + u["sector"]))
    return pairs


def rest_dims(terms):
    return [("term", bit) for bit in range(2, terms.bit_length() - 1)]


def shards(mesh_shape, psi_start, diagonal, left_ops, right_ops, pair_in, pair_out, pair_count):
    terms, sectors = mesh_shape
    b = psi_start.shape[1]
    cells = float(sectors * b * b)

    def swap(x, even, odd=None):
        return lax.ppermute(x, AXES, flips(mesh_shape, even, even if odd is None else odd))

    def dims_of(k):
        return [dim for i, dim in enumerate(DIMS) if (k >> (2 - i)) & 1]

    away = sorted(range(1, 8), key=lambda k: -len(dims_of(k)))
    rest = rest_dims(terms)

    own = psi_start[0]
    across = swap(own, [DIMS[0]])
    beside = swap(own, [CORE])
    lh, ll, rh, rl, vec, diag = prepare(left_ops, right_ops, psi_start, diagonal)
    across, lh, ll, rh, rl, vec, diag = lax.optimization_barrier((across, lh, ll, rh, rl, vec, diag))
    corner = swap(across, [CORE])
    pieces = (own, beside, across, corner)
    energies = []
    for sweep in range(ITERS):
        first = sweep == 0
        th, tl, inv = inner(first, cells, sectors, pair_in, pair_count, pieces, (rh, rl))
        rho = jnp.zeros(TILE, F32)
        keeps, recvs = [], []
        for h in range(CHUNKS):
            send, keep, rho = outer(
                first, h, cells, sectors, pair_out, pair_count, pieces, (lh, ll, th, tl), inv, rho
            )
            keeps.append(keep)
            recvs.append(swap(send, [CORE]))
        for step in zip(*ORDERS):
            for h in range(CHUNKS):
                extra = TILE[0] if h == CHUNKS - 1 else 0
                keeps[h], send = combine(keeps[h], recvs[h], extra)
                recvs[h] = swap(send, [DIMS[step[0]]], [DIMS[step[1]]])
        for step in rest:
            for h in range(CHUNKS):
                keeps[h] = total(keeps[h], recvs[h])
                recvs[h] = swap(keeps[h], [step])
        sums = [x for pair in zip(keeps, recvs) for x in pair]
        vec, energy = update(sums, vec, inv, diag)
        energies.append(energy[0, 0])
        if sweep < ITERS - 1:
            got = {k: swap(vec, dims_of(k)) for k in away}
            got[0] = vec
            pieces = []
            for k in range(8):
                pieces += [got[k], swap(got[k], [CORE])]
    got = {k: swap(vec, dims_of(k)) for k in (3, 2, 1)}
    block = join([vec, got[1], got[2], got[3]])
    return block, jnp.stack(energies)


def solution(mesh):
    mesh_shape = (mesh.shape["term"], mesh.shape["sector"])
    return jax.shard_map(
        functools.partial(shards, mesh_shape),
        mesh=mesh,
        in_specs=(
            P("sector", None, None),
            P("sector", None, None),
            P(("term", "sector"), None, None),
            P(("term", "sector"), None, None),
            P(("term", "sector"), None),
            P(("term", "sector"), None),
            P(("term", "sector")),
        ),
        out_specs=(P("sector", None, None), P()),
        check_vma=False,
    )
```

```python
import functools

import jax
import jax.numpy as jnp
from jax import lax
from jax.experimental import pallas as pl
from jax.experimental.pallas import tpu as pltpu
from jax.sharding import PartitionSpec as P


ITERS = 2
AXES = ("term", "sector")
TILE = (8, 128)
CHUNKS = 2

epsilon = 1e-06


VMEM = pl.BlockSpec(memory_space=pltpu.VMEM)
SMEM = pl.BlockSpec(memory_space=pltpu.SMEM)
F32 = jnp.float32
BF16 = jnp.bfloat16

DIMS = (("sector", 1), ("term", 0), ("term", 1))
CORE = ("sector", 0)
ORDERS = ((0, 1, 2), (2, 0, 1))
GATHER = ((0, 1, 2), (2, 1, 0))


def matmul_cost(pairs, rows, b):
    return pl.CostEstimate(
        flops=6 * pairs * rows * b * b, bytes_accessed=8 * pairs * b * b, transcendentals=0
    )


def grant(mib):
    return pltpu.CompilerParams(vmem_limit_bytes=mib << 20)


def bit_of(axis, bit):
    return (lax.axis_index(axis) >> bit) & 1


def place(bits, parity, rows):
    return 2 * bits[0] + parity, pl.multiple_of((2 * bits[1] + bits[2]) * rows, 8)


def piece_place(k, parity, rows):
    return place([bit_of(*dim) ^ ((k >> (2 - i)) & 1) for i, dim in enumerate(DIMS)], parity, rows)


def slot_bits(j, order):
    flip = [0, 0, 0]
    for i, dim in enumerate(order):
        flip[dim] = (j >> (2 - i)) & 1
    return flip


def slot_place(j, parity, rows, orders=ORDERS):
    a, b = slot_bits(j, orders[0]), slot_bits(j, orders[1])
    flip = [x if x == y else jnp.where(parity == 0, x, y) for x, y in zip(a, b)]
    return place([bit_of(*dim) ^ f for dim, f in zip(DIMS, flip)], parity, rows)


def segments(first, rows, shard):
    me = lax.axis_index("sector")
    if first:
        out = [[(h, me ^ side, h * rows, 0, rows) for h in range(CHUNKS)] for side in range(2)]
        out += [[(h, me ^ (2 + side), h * rows, 0, rows) for h in range(CHUNKS - 1)] for side in range(2)]
        for k in range(4):
            _, row = piece_place(k, 0, shard)
            out += [[(CHUNKS - 1, me ^ (2 + side), 0, row, shard)] for side in range(2)]
        return out
    out = []
    for number in range(16):
        sector, row = slot_place(number >> 1, (me & 1) ^ (number & 1), shard, GATHER)
        out.append([(h, sector, h * shard, row, shard) for h in range(CHUNKS)])
    return out


def split(x):
    high = x.astype(BF16)
    return high, (x - high.astype(F32)).astype(BF16)


def prep_kernel(left_ref, right_ref, psi_ref, diag_ref, lh_ref, ll_ref, rh_ref, rl_ref, vec_ref, mine_ref):
    def one(p, carry):
        lh_ref[p], ll_ref[p] = split(left_ref[p])
        rh_ref[p], rl_ref[p] = split(right_ref[p])
        return carry

    lax.fori_loop(0, left_ref.shape[0], one, 0)
    rows = vec_ref.shape[0] // CHUNKS
    for h in range(CHUNKS):
        _, row = piece_place(0, 0, rows)
        at = pl.ds(pl.multiple_of(row + h * 4 * rows, 8), rows)
        vec_ref[h * rows:(h + 1) * rows, :] = psi_ref[0, at, :]
        mine_ref[h * rows:(h + 1) * rows, :] = diag_ref[0, at, :]


def prepare(left_ops, right_ops, psi, diag):
    b = psi.shape[-1]
    shard = jax.ShapeDtypeStruct((b // 4, b), F32)
    return pl.pallas_call(
        prep_kernel,
        in_specs=[VMEM] * 4,
        out_specs=[VMEM] * 6,
        out_shape=[jax.ShapeDtypeStruct(left_ops.shape, BF16)] * 4 + [shard] * 2,
        compiler_params=grant(16),
        cost_estimate=pl.CostEstimate(
            flops=4 * left_ops.size, bytes_accessed=16 * left_ops.size, transcendentals=0
        ),
    )(left_ops, right_ops, psi, diag)


def store_wide(dest, start, x):
    rows = x.shape[0]
    for c in range(x.shape[1] // TILE[1]):
        dest[start + c * rows:start + (c + 1) * rows, :] = x[:, c * TILE[1]:(c + 1) * TILE[1]]


DOT_NT = functools.partial(
    lax.dot_general, dimension_numbers=(((1,), (1,)), ((), ())), preferred_element_type=F32
)
DOT = functools.partial(jnp.dot, preferred_element_type=F32)


def inner_kernel(first, cells, pieces, *refs):
    in_ref, count_ref, *refs = refs
    parts = refs[:pieces]
    rh, rl, th_ref, tl_ref, inv_ref, vh, vl = refs[pieces:]
    _, b, _ = vh.shape
    rows = b // CHUNKS
    total = jnp.zeros((1, b), F32)
    for piece, cuts in zip(parts, segments(first, rows, rows // 4)):
        for chunk, sector, start, row, size in cuts:
            x = piece[start:start + size, :]
            high, low = split(x)
            total += jnp.sum(x * x, axis=0, keepdims=True)
            at = pl.ds(pl.multiple_of(row + chunk * rows, 16), size)
            vh[sector, at, :] = high
            vl[sector, at, :] = low
    inv_ref[...] = lax.rsqrt(
        jnp.broadcast_to(jnp.sum(total, axis=1, keepdims=True), (TILE[0], b)) / cells + epsilon
    )

    def one_pair(p, carry):
        source = in_ref[0, p]
        x_h, x_l = vh[source], vl[source]
        r_h, r_l = rh[p], rl[p]
        th_ref[p], tl_ref[p] = split(DOT_NT(x_h, r_h) + (DOT_NT(x_h, r_l) + DOT_NT(x_l, r_h)))
        return carry

    lax.fori_loop(0, count_ref[0], one_pair, 0)


def inner(first, cells, sectors, pair_in, pair_count, pieces, ops):
    pairs, b, _ = ops[0].shape
    half = jax.ShapeDtypeStruct(ops[0].shape, BF16)
    return pl.pallas_call(
        functools.partial(inner_kernel, first, cells, len(pieces)),
        in_specs=[SMEM] * 2 + [VMEM] * (len(pieces) + 2),
        out_specs=[VMEM] * 3,
        out_shape=[half, half, jax.ShapeDtypeStruct((TILE[0], b), F32)],
        scratch_shapes=[pltpu.VMEM((sectors, b, b), BF16), pltpu.VMEM((sectors, b, b), BF16)],
        compiler_params=grant(16),
        cost_estimate=matmul_cost(pairs, b, b),
    )(pair_in, pair_count, *pieces, *ops)


def outer_kernel(first, chunk, cells, pieces, *refs):
    out_ref, count_ref, *refs = refs
    parts = refs[:pieces]
    lh, ll, th, tl, inv_ref, before_ref, send_ref, keep_ref, rho_ref, acc = refs[pieces:]
    _, rows, b = acc.shape
    shard = rows // 4
    core = lax.axis_index("sector") & 1
    acc[...] = jnp.zeros_like(acc)
    here = slice(chunk * rows, (chunk + 1) * rows)

    def one_pair(p, carry):
        target = out_ref[0, p]
        l_h, l_l = lh[p, here, :], ll[p, here, :]
        t_h, t_l = th[p], tl[p]
        acc[target] += DOT(l_h, t_h) + (DOT(l_h, t_l) + DOT(l_l, t_h))
        return carry

    lax.fori_loop(0, count_ref[0], one_pair, 0)
    scale = inv_ref[:1, :]
    rho = jnp.zeros((1, b), F32)
    wide = shard * b // TILE[1]
    for piece, cuts in zip(parts, segments(first, rows, shard)):
        for at, sector, start, row, size in cuts:
            if at == chunk:
                x = acc[sector, pl.ds(row, size), :] * piece[start:start + size, :]
                rho += jnp.sum(x, axis=0, keepdims=True)
    for dest, parity in ((send_ref, 1 - core), (keep_ref, core)):
        for j in range(8):
            sector, row = slot_place(j, parity, shard)
            store_wide(dest, j * wide, acc[sector, pl.ds(row, shard), :] * scale)
    rho = jnp.broadcast_to(jnp.sum(rho * scale * scale, axis=1, keepdims=True), TILE) / cells + before_ref[...]
    rho_ref[...] = rho
    if chunk == CHUNKS - 1:
        send_ref[8 * wide:, :] = rho
        keep_ref[8 * wide:, :] = rho


def outer(first, chunk, cells, sectors, pair_out, pair_count, pieces, ops, inv, before):
    pairs, b, _ = ops[0].shape
    rows = b // CHUNKS
    extra = TILE[0] if chunk == CHUNKS - 1 else 0
    half = jax.ShapeDtypeStruct((sectors * rows // 2 * b // TILE[1] + extra, TILE[1]), F32)
    return pl.pallas_call(
        functools.partial(outer_kernel, first, chunk, cells, len(pieces)),
        in_specs=[SMEM] * 2 + [VMEM] * (len(pieces) + 6),
        out_specs=[VMEM] * 3,
        out_shape=[half, half, jax.ShapeDtypeStruct(TILE, F32)],
        scratch_shapes=[pltpu.VMEM((sectors, rows, b), F32)],
        compiler_params=grant(20),
        cost_estimate=matmul_cost(pairs, rows, b),
    )(pair_out, pair_count, *pieces, *ops, inv, before)


def combine_kernel(keep_ref, recv_ref, next_ref, send_ref=None):
    extra = 0 if send_ref is None else 2 * next_ref.shape[0] - keep_ref.shape[0]
    rows = next_ref.shape[0] - extra
    next_ref[:rows, :] = keep_ref[:rows, :] + recv_ref[:rows, :]
    if send_ref is None:
        return
    send_ref[:rows, :] = keep_ref[rows:2 * rows, :] + recv_ref[rows:2 * rows, :]
    if extra:
        total = keep_ref[2 * rows:, :] + recv_ref[2 * rows:, :]
        next_ref[rows:, :] = total
        send_ref[rows:, :] = total


def combine(keep, recv, extra):
    shape = jax.ShapeDtypeStruct(((keep.shape[0] - extra) // 2 + extra, TILE[1]), F32)
    return pl.pallas_call(
        combine_kernel,
        in_specs=[VMEM] * 2,
        out_specs=[VMEM] * 2,
        out_shape=[shape] * 2,
        compiler_params=grant(4),
    )(keep, recv)


def total(mine, recv):
    return pl.pallas_call(
        combine_kernel,
        in_specs=[VMEM] * 2,
        out_specs=VMEM,
        out_shape=jax.ShapeDtypeStruct(mine.shape, F32),
        compiler_params=grant(4),
    )(mine, recv)


def update_kernel(*refs):
    sums, (vec_ref, inv_ref, diag_ref, new_ref, energy_ref) = refs[:2 * CHUNKS], refs[2 * CHUNKS:]
    rows, b = new_ref.shape
    shard = rows // CHUNKS
    end = shard * b // TILE[1]
    rho = sums[-2][end:, :] + sums[-1][end:, :]
    energy_ref[...] = rho
    for h in range(CHUNKS):
        mine_ref, recv_ref = sums[2 * h:2 * h + 2]
        at = slice(h * shard, (h + 1) * shard)
        for c in range(b // TILE[1]):
            part = slice(c * shard, (c + 1) * shard)
            lanes = slice(c * TILE[1], (c + 1) * TILE[1])
            normed = vec_ref[at, lanes] * inv_ref[:1, lanes]
            sigma = mine_ref[part, :] + recv_ref[part, :]
            residual = sigma - rho[:1, :] * normed
            gap = jnp.maximum(jnp.abs(diag_ref[at, lanes] - rho[:1, :]), 1.0)
            new_ref[at, lanes] = normed - residual / gap


def update(sums, vec, inv, diag):
    return pl.pallas_call(
        update_kernel,
        in_specs=[VMEM] * (len(sums) + 3),
        out_specs=[VMEM] * 2,
        out_shape=[jax.ShapeDtypeStruct(vec.shape, F32), jax.ShapeDtypeStruct(TILE, F32)],
        compiler_params=grant(4),
    )(*sums, vec, inv, diag)


def zero_tile():
    def kernel(out_ref):
        out_ref[...] = jnp.zeros_like(out_ref)

    return pl.pallas_call(
        kernel, out_specs=VMEM, out_shape=jax.ShapeDtypeStruct(TILE, F32), compiler_params=grant(4)
    )()


def join_kernel(*refs):
    *parts, out_ref = refs
    rows = parts[0].shape[0] // CHUNKS
    for k, part in enumerate(parts):
        _, row = piece_place(k, 0, rows)
        for h in range(CHUNKS):
            at = pl.ds(pl.multiple_of(row + h * 4 * rows, 8), rows)
            out_ref[0, at, :] = part[h * rows:(h + 1) * rows, :]


def join(parts):
    quarter, b = parts[0].shape
    return pl.pallas_call(
        join_kernel,
        in_specs=[VMEM] * len(parts),
        out_specs=VMEM,
        out_shape=jax.ShapeDtypeStruct((1, 4 * quarter, b), F32),
        compiler_params=grant(4),
    )(*parts)


def flips(mesh_shape, even, odd):
    terms, sectors = mesh_shape
    pairs = []
    for t in range(terms):
        for s in range(sectors):
            u = {"term": t, "sector": s}
            for axis, bit in odd if s & 1 else even:
                u[axis] ^= 1 << bit
            pairs.append((t * sectors + s, u["term"] * sectors + u["sector"]))
    return pairs


def rest_dims(terms):
    return [("term", bit) for bit in range(2, terms.bit_length() - 1)]


def shards(mesh_shape, psi_start, diagonal, left_ops, right_ops, pair_in, pair_out, pair_count):
    terms, sectors = mesh_shape
    b = psi_start.shape[1]
    cells = float(sectors * b * b)

    def swap(x, even, odd=None):
        return lax.ppermute(x, AXES, flips(mesh_shape, even, even if odd is None else odd))

    def dims_of(k):
        return [dim for i, dim in enumerate(DIMS) if (k >> (2 - i)) & 1]

    rest = rest_dims(terms)

    own = psi_start[0]
    shard = b // CHUNKS // 4
    _, row = piece_place(0, 0, shard)
    share = lax.dynamic_slice(own, (row + (b - b // CHUNKS), 0), (shard, b))
    share = swap(share, [DIMS[0]])
    across = swap(own[:b - b // CHUNKS], [DIMS[0]])
    beside = swap(own, [CORE])
    zero = zero_tile()
    lh, ll, rh, rl, vec, diag = prepare(left_ops, right_ops, psi_start, diagonal)
    across, lh, ll, rh, rl, vec, diag = lax.optimization_barrier((across, lh, ll, rh, rl, vec, diag))
    shares = [share, swap(share, [DIMS[2]]), swap(share, [DIMS[1]])]
    last = jnp.where(bit_of(*CORE) == 0, shares[1], shares[2])
    shares.append(swap(last, [DIMS[1]], [DIMS[2]]))
    corner = swap(across, [CORE])
    pieces = [own, beside, across, corner]
    for x in shares:
        pieces += [x, swap(x, [CORE])]
    energies = []
    for sweep in range(ITERS):
        first = sweep == 0
        th, tl, inv = inner(first, cells, sectors, pair_in, pair_count, pieces, (rh, rl))
        rho = zero
        keeps, recvs = [], []
        for h in range(CHUNKS):
            send, keep, rho = outer(first, h, cells, sectors, pair_out, pair_count, pieces, (lh, ll, th, tl), inv, rho)
            keeps.append(keep)
            recvs.append(swap(send, [CORE]))
        for step in zip(*ORDERS):
            for h in range(CHUNKS):
                extra = TILE[0] if h == CHUNKS - 1 else 0
                keeps[h], send = combine(keeps[h], recvs[h], extra)
                recvs[h] = swap(send, [DIMS[step[0]]], [DIMS[step[1]]])
        for step in rest:
            for h in range(CHUNKS):
                keeps[h] = total(keeps[h], recvs[h])
                recvs[h] = swap(keeps[h], [step])
        sums = [x for pair in zip(keeps, recvs) for x in pair]
        vec, energy = update(sums, vec, inv, diag)
        energies.append(energy[0, 0])
        if sweep < ITERS - 1:
            got = [vec] + [None] * 7
            for j in (1, 2, 4, 3, 5, 6, 7):
                over = 2 - (j.bit_length() - 1)
                source = got[j ^ (1 << (2 - over))]
                got[j] = swap(source, [DIMS[GATHER[0][over]]], [DIMS[GATHER[1][over]]])
            pieces = []
            for x in got:
                pieces += [x, swap(x, [CORE])]
    got = {k: swap(vec, dims_of(k)) for k in (3, 2, 1)}
    block = join([vec, got[1], got[2], got[3]])
    return block, jnp.stack(energies)


def solution(mesh):
    mesh_shape = (mesh.shape["term"], mesh.shape["sector"])
    return jax.shard_map(
        functools.partial(shards, mesh_shape),
        mesh=mesh,
        in_specs=(
            P("sector", None, None),
            P("sector", None, None),
            P(("term", "sector"), None, None),
            P(("term", "sector"), None, None),
            P(("term", "sector"), None),
            P(("term", "sector"), None),
            P(("term", "sector")),
        ),
        out_specs=(P("sector", None, None), P()),
        check_vma=False,
    )
```

```python
import functools

import jax
import jax.numpy as jnp
from jax import lax
from jax.experimental import pallas as pl
from jax.experimental.pallas import tpu as pltpu
from jax.sharding import PartitionSpec as P


ITERS = 2
AXES = ("term", "sector")
TILE = (8, 128)
CHUNKS = 2

epsilon = 1e-06


VMEM = pl.BlockSpec(memory_space=pltpu.VMEM)
SMEM = pl.BlockSpec(memory_space=pltpu.SMEM)
F32 = jnp.float32
BF16 = jnp.bfloat16

DIMS = (("sector", 1), ("term", 0), ("term", 1))
CORE = ("sector", 0)
ORDERS = ((0, 1, 2), (2, 1, 0))


def matmul_cost(pairs, rows, b):
    return pl.CostEstimate(
        flops=6 * pairs * rows * b * b, bytes_accessed=8 * pairs * b * b, transcendentals=0
    )


def grant(mib):
    return pltpu.CompilerParams(vmem_limit_bytes=mib << 20)


def bit_of(axis, bit):
    return (lax.axis_index(axis) >> bit) & 1


def place(bits, parity, rows):
    return 2 * bits[0] + parity, pl.multiple_of((2 * bits[1] + bits[2]) * rows, 8)


def piece_place(k, parity, rows):
    return place([bit_of(*dim) ^ ((k >> (2 - i)) & 1) for i, dim in enumerate(DIMS)], parity, rows)


def slot_bits(j, order):
    flip = [0, 0, 0]
    for i, dim in enumerate(order):
        flip[dim] = (j >> (2 - i)) & 1
    return flip


def slot_place(j, parity, rows):
    a, b = slot_bits(j, ORDERS[0]), slot_bits(j, ORDERS[1])
    flip = [x if x == y else jnp.where(parity == 0, x, y) for x, y in zip(a, b)]
    return place([bit_of(*dim) ^ f for dim, f in zip(DIMS, flip)], parity, rows)


def split(x):
    high = x.astype(BF16)
    return high, (x - high.astype(F32)).astype(BF16)


def segments(first, rows, shard):
    me = lax.axis_index("sector")
    if first:
        out = [[(h, me ^ side, h * rows, 0, rows) for h in range(CHUNKS)] for side in range(2)]
        out += [[(h, me ^ (2 + side), 0, 0, rows)] for h in range(CHUNKS) for side in range(2)]
        return out
    out = []
    for number in range(16):
        sector, row = piece_place(number >> 1, (me & 1) ^ (number & 1), shard)
        out.append([(h, sector, h * shard, row, shard) for h in range(CHUNKS)])
    return out


def prep_kernel(left_ref, right_ref, psi_ref, diag_ref, left_cat, right_cat, vec_ref, mine_ref):
    b = left_ref.shape[-1]

    def one(p, carry):
        high, low = split(left_ref[p])
        for place, x in enumerate((high, low, high)):
            left_cat[p, :, place * b:(place + 1) * b] = x
        high, low = split(right_ref[p])
        for place, x in enumerate((high, high, low)):
            right_cat[p, :, place * b:(place + 1) * b] = x
        return carry

    lax.fori_loop(0, left_ref.shape[0], one, 0)
    rows = vec_ref.shape[0] // CHUNKS
    for h in range(CHUNKS):
        _, row = piece_place(0, 0, rows)
        at = pl.ds(pl.multiple_of(row + h * 4 * rows, 8), rows)
        vec_ref[h * rows:(h + 1) * rows, :] = psi_ref[0, at, :]
        mine_ref[h * rows:(h + 1) * rows, :] = diag_ref[0, at, :]


def prepare(left_ops, right_ops, psi, diag):
    pairs, b, _ = left_ops.shape
    shard = jax.ShapeDtypeStruct((b // 4, b), F32)
    return pl.pallas_call(
        prep_kernel,
        in_specs=[VMEM] * 4,
        out_specs=[VMEM] * 4,
        out_shape=[jax.ShapeDtypeStruct((pairs, b, 3 * b), BF16)] * 2 + [shard] * 2,
        compiler_params=grant(16),
        cost_estimate=pl.CostEstimate(
            flops=4 * left_ops.size, bytes_accessed=20 * left_ops.size, transcendentals=0
        ),
    )(left_ops, right_ops, psi, diag)


def store_wide(dest, start, x):
    rows = x.shape[0]
    for c in range(x.shape[1] // TILE[1]):
        dest[start + c * rows:start + (c + 1) * rows, :] = x[:, c * TILE[1]:(c + 1) * TILE[1]]


DOT_NT = functools.partial(
    lax.dot_general, dimension_numbers=(((1,), (1,)), ((), ())), preferred_element_type=F32
)
DOT = functools.partial(jnp.dot, preferred_element_type=F32)


def inner_kernel(first, half, cells, pieces, *refs):
    in_ref, count_ref, *refs = refs
    parts = refs[:pieces]
    refs = refs[pieces:]
    if half:
        right, early_h, early_l, squares_ref, cat_ref, inv_ref, vec = refs
    else:
        right, early_h, early_l, squares_ref, vec = refs
    _, rows, _ = vec.shape
    b = right.shape[1]
    shard = rows // 4
    x_bit = bit_of(*DIMS[1])
    side = x_bit ^ half
    total = jnp.zeros((1, b), F32)
    cuts_of = segments(first, rows, shard)
    for piece, cuts in zip(parts, [cuts_of[i] for i in picked(first, half)]):
        for chunk, sector, start, row, size in cuts:
            if first and chunk != half:
                continue
            x = piece[start:start + size, :]
            high, low = split(x)
            total += jnp.sum(x * x, axis=0, keepdims=True)
            if not first:
                row = pl.multiple_of(row - side * 2 * shard + chunk * 2 * shard, 16)
            at = pl.ds(row, size)
            for place, y in enumerate((high, low, high)):
                vec[sector, at, place * b:(place + 1) * b] = y
    total = jnp.broadcast_to(jnp.sum(total, axis=1, keepdims=True), (TILE[0], b))
    if half:
        inv_ref[...] = lax.rsqrt((total + squares_ref[...]) / cells + epsilon)
    else:
        squares_ref[...] = total

    def one_pair(p, carry):
        high, low = split(DOT_NT(vec[in_ref[0, p]], right[p]))
        if not half:
            early_h[p], early_l[p] = high, low
            return carry
        for which, (h, l) in enumerate(((early_h[p], early_l[p]), (high, low))):
            if first:
                moves = [(0, rows, which * rows)]
            else:
                moves = [
                    (c * 2 * shard, 2 * shard, pl.multiple_of(c * rows + (x_bit ^ which) * 2 * shard, 16))
                    for c in range(CHUNKS)
                ]
            for start, size, row in moves:
                for place, y in enumerate((h, h, l)):
                    cat_ref[p, pl.ds(place * b + row, size), :] = y[start:start + size, :]
        return carry

    lax.fori_loop(0, count_ref[0], one_pair, 0)


def picked(first, half):
    if first:
        return [0, 1, 2 + 2 * half, 3 + 2 * half]
    return [number for number in range(16) if (number >> 2) & 1 == half]


def inner(first, half, cells, sectors, pair_in, pair_count, pieces, right, early=()):
    pairs, b, _ = right.shape
    rows = b // 2
    compact = jax.ShapeDtypeStruct((pairs, rows, b), BF16)
    row = jax.ShapeDtypeStruct((TILE[0], b), F32)
    shapes = [jax.ShapeDtypeStruct((pairs, 3 * b, b), BF16), row] if half else [compact, compact, row]
    return pl.pallas_call(
        functools.partial(inner_kernel, first, half, cells, len(pieces)),
        in_specs=[SMEM] * 2 + [VMEM] * (len(pieces) + 1 + len(early)),
        out_specs=[VMEM] * len(shapes),
        out_shape=shapes,
        scratch_shapes=[pltpu.VMEM((sectors, rows, 3 * b), BF16)],
        compiler_params=grant(16),
        cost_estimate=matmul_cost(pairs, rows, b),
    )(pair_in, pair_count, *pieces, right, *early)


def outer_kernel(first, chunk, cells, pieces, *refs):
    out_ref, count_ref, *refs = refs
    parts = refs[:pieces]
    left, cat, inv_ref, before_ref, send_ref, keep_ref, rho_ref, acc = refs[pieces:]
    _, rows, b = acc.shape
    shard = rows // 4
    core = lax.axis_index("sector") & 1
    acc[...] = jnp.zeros_like(acc)
    here = slice(chunk * rows, (chunk + 1) * rows)

    def one_pair(p, carry):
        target = out_ref[0, p]
        acc[target] += DOT(left[p, here, :], cat[p])
        return carry

    lax.fori_loop(0, count_ref[0], one_pair, 0)
    scale = inv_ref[:1, :]
    rho = jnp.zeros((1, b), F32)
    wide = shard * b // TILE[1]
    for piece, cuts in zip(parts, segments(first, rows, shard)):
        for at, sector, start, row, size in cuts:
            if at == chunk:
                x = acc[sector, pl.ds(row, size), :] * piece[start:start + size, :]
                rho += jnp.sum(x, axis=0, keepdims=True)
    for dest, parity in ((send_ref, 1 - core), (keep_ref, core)):
        for j in range(8):
            sector, row = slot_place(j, parity, shard)
            store_wide(dest, j * wide, acc[sector, pl.ds(row, shard), :] * scale)
    rho = jnp.broadcast_to(jnp.sum(rho * scale * scale, axis=1, keepdims=True), TILE) / cells + before_ref[...]
    rho_ref[...] = rho
    if chunk == CHUNKS - 1:
        send_ref[8 * wide:, :] = rho
        keep_ref[8 * wide:, :] = rho


def outer(first, chunk, cells, sectors, pair_out, pair_count, pieces, ops, inv, before):
    pairs, _, b = ops[1].shape
    rows = b // CHUNKS
    extra = TILE[0] if chunk == CHUNKS - 1 else 0
    half = jax.ShapeDtypeStruct((sectors * rows // 2 * b // TILE[1] + extra, TILE[1]), F32)
    return pl.pallas_call(
        functools.partial(outer_kernel, first, chunk, cells, len(pieces)),
        in_specs=[SMEM] * 2 + [VMEM] * (len(pieces) + 4),
        out_specs=[VMEM] * 3,
        out_shape=[half, half, jax.ShapeDtypeStruct(TILE, F32)],
        scratch_shapes=[pltpu.VMEM((sectors, rows, b), F32)],
        compiler_params=grant(20),
        cost_estimate=matmul_cost(pairs, rows, b),
    )(pair_out, pair_count, *pieces, *ops, inv, before)


def combine_kernel(keep_ref, recv_ref, next_ref, send_ref=None):
    extra = 0 if send_ref is None else 2 * next_ref.shape[0] - keep_ref.shape[0]
    rows = next_ref.shape[0] - extra
    next_ref[:rows, :] = keep_ref[:rows, :] + recv_ref[:rows, :]
    if send_ref is None:
        return
    send_ref[:rows, :] = keep_ref[rows:2 * rows, :] + recv_ref[rows:2 * rows, :]
    if extra:
        total = keep_ref[2 * rows:, :] + recv_ref[2 * rows:, :]
        next_ref[rows:, :] = total
        send_ref[rows:, :] = total


def combine(keep, recv, extra):
    shape = jax.ShapeDtypeStruct(((keep.shape[0] - extra) // 2 + extra, TILE[1]), F32)
    return pl.pallas_call(
        combine_kernel,
        in_specs=[VMEM] * 2,
        out_specs=[VMEM] * 2,
        out_shape=[shape] * 2,
        compiler_params=grant(4),
    )(keep, recv)


def total(mine, recv):
    return pl.pallas_call(
        combine_kernel,
        in_specs=[VMEM] * 2,
        out_specs=VMEM,
        out_shape=jax.ShapeDtypeStruct(mine.shape, F32),
        compiler_params=grant(4),
    )(mine, recv)


def update_kernel(*refs):
    sums, (vec_ref, inv_ref, diag_ref, new_ref, energy_ref) = refs[:2 * CHUNKS], refs[2 * CHUNKS:]
    rows, b = new_ref.shape
    shard = rows // CHUNKS
    end = shard * b // TILE[1]
    rho = sums[-2][end:, :] + sums[-1][end:, :]
    energy_ref[...] = rho
    for h in range(CHUNKS):
        mine_ref, recv_ref = sums[2 * h:2 * h + 2]
        at = slice(h * shard, (h + 1) * shard)
        for c in range(b // TILE[1]):
            part = slice(c * shard, (c + 1) * shard)
            lanes = slice(c * TILE[1], (c + 1) * TILE[1])
            normed = vec_ref[at, lanes] * inv_ref[:1, lanes]
            sigma = mine_ref[part, :] + recv_ref[part, :]
            residual = sigma - rho[:1, :] * normed
            gap = jnp.maximum(jnp.abs(diag_ref[at, lanes] - rho[:1, :]), 1.0)
            new_ref[at, lanes] = normed - residual / gap


def update(sums, vec, inv, diag):
    return pl.pallas_call(
        update_kernel,
        in_specs=[VMEM] * (len(sums) + 3),
        out_specs=[VMEM] * 2,
        out_shape=[jax.ShapeDtypeStruct(vec.shape, F32), jax.ShapeDtypeStruct(TILE, F32)],
        compiler_params=grant(4),
    )(*sums, vec, inv, diag)


def zero_tile(tile):
    def kernel(in_ref, out_ref):
        out_ref[...] = jnp.zeros_like(out_ref)

    return pl.pallas_call(
        kernel, in_specs=[VMEM], out_specs=VMEM, out_shape=jax.ShapeDtypeStruct(TILE, F32), compiler_params=grant(4)
    )(tile)


def join_kernel(*refs):
    *parts, out_ref = refs
    rows = parts[0].shape[0] // CHUNKS
    for k, part in enumerate(parts):
        _, row = piece_place(k, 0, rows)
        for h in range(CHUNKS):
            at = pl.ds(pl.multiple_of(row + h * 4 * rows, 8), rows)
            out_ref[0, at, :] = part[h * rows:(h + 1) * rows, :]


def join(parts):
    quarter, b = parts[0].shape
    return pl.pallas_call(
        join_kernel,
        in_specs=[VMEM] * len(parts),
        out_specs=VMEM,
        out_shape=jax.ShapeDtypeStruct((1, 4 * quarter, b), F32),
        compiler_params=grant(4),
    )(*parts)


def flips(mesh_shape, even, odd):
    terms, sectors = mesh_shape
    pairs = []
    for t in range(terms):
        for s in range(sectors):
            u = {"term": t, "sector": s}
            for axis, bit in odd if s & 1 else even:
                u[axis] ^= 1 << bit
            pairs.append((t * sectors + s, u["term"] * sectors + u["sector"]))
    return pairs


def rest_dims(terms):
    return [("term", bit) for bit in range(2, terms.bit_length() - 1)]


def shards(mesh_shape, psi_start, diagonal, left_ops, right_ops, pair_in, pair_out, pair_count):
    terms, sectors = mesh_shape
    b = psi_start.shape[1]
    cells = float(sectors * b * b)

    def swap(x, even, odd=None):
        return lax.ppermute(x, AXES, flips(mesh_shape, even, even if odd is None else odd))

    def dims_of(k):
        return [dim for i, dim in enumerate(DIMS) if (k >> (2 - i)) & 1]

    away = (2, 1, 4, 5, 6, 3, 7)
    rest = rest_dims(terms)

    own = psi_start[0]
    rows = b // CHUNKS
    far = []
    for h in range(CHUNKS):
        far.append(swap(own[h * rows:(h + 1) * rows], [DIMS[0]]))
    beside = swap(own, [CORE])
    left, right, vec, diag = prepare(left_ops, right_ops, psi_start, diagonal)
    far[0], left, right, vec, diag = lax.optimization_barrier((far[0], left, right, vec, diag))
    pieces = [own, beside]
    for x in far:
        pieces += [x, swap(x, [CORE])]
    zero = jnp.zeros(TILE, F32)
    energies = []
    for sweep in range(ITERS):
        first = sweep == 0
        early, late = ([pieces[i] for i in picked(first, half)] for half in range(2))
        early = inner(first, 0, cells, sectors, pair_in, pair_count, early, right)
        cat, inv = inner(first, 1, cells, sectors, pair_in, pair_count, late, right, early)
        rho = zero
        keeps, recvs = [], []
        for h in range(CHUNKS):
            send, keep, rho = outer(
                first, h, cells, sectors, pair_out, pair_count, pieces, (left, cat), inv, rho
            )
            keeps.append(keep)
            recvs.append(swap(send, [CORE]))
        for step in zip(*ORDERS):
            for h in range(CHUNKS):
                extra = TILE[0] if h == CHUNKS - 1 else 0
                keeps[h], send = combine(keeps[h], recvs[h], extra)
                recvs[h] = swap(send, [DIMS[step[0]]], [DIMS[step[1]]])
        for step in rest:
            for h in range(CHUNKS):
                keeps[h] = total(keeps[h], recvs[h])
                recvs[h] = swap(keeps[h], [step])
        sums = [x for pair in zip(keeps, recvs) for x in pair]
        vec, energy = update(sums, vec, inv, diag)
        energies.append(energy[0, 0])
        if sweep < ITERS - 1:
            got = {0: vec}
            zero = zero_tile(energy)
            for k in away:
                got[k] = swap(vec, dims_of(k))
            pieces = []
            for k in range(8):
                pieces += [got[k], swap(got[k], [CORE])]
    got = {k: swap(vec, dims_of(k)) for k in (3, 2, 1)}
    block = join([vec, got[1], got[2], got[3]])
    return block, jnp.stack(energies)


def solution(mesh):
    mesh_shape = (mesh.shape["term"], mesh.shape["sector"])
    return jax.shard_map(
        functools.partial(shards, mesh_shape),
        mesh=mesh,
        in_specs=(
            P("sector", None, None),
            P("sector", None, None),
            P(("term", "sector"), None, None),
            P(("term", "sector"), None, None),
            P(("term", "sector"), None),
            P(("term", "sector"), None),
            P(("term", "sector")),
        ),
        out_specs=(P("sector", None, None), P()),
        check_vma=False,
    )
```

```python
import functools

import jax
import jax.numpy as jnp
from jax import lax
from jax.experimental import pallas as pl
from jax.experimental.pallas import tpu as pltpu
from jax.sharding import PartitionSpec as P


ITERS = 2
AXES = ("term", "sector")
TILE = (8, 128)
CHUNKS = 2

epsilon = 1e-06


VMEM = pl.BlockSpec(memory_space=pltpu.VMEM)
SMEM = pl.BlockSpec(memory_space=pltpu.SMEM)
F32 = jnp.float32
BF16 = jnp.bfloat16

DIMS = (("sector", 1), ("term", 0), ("term", 1))
CORE = ("sector", 0)
ORDERS = ((0, 1, 2), (2, 1, 0))


def matmul_cost(pairs, rows, b):
    return pl.CostEstimate(
        flops=6 * pairs * rows * b * b, bytes_accessed=8 * pairs * b * b, transcendentals=0
    )


def grant(mib):
    return pltpu.CompilerParams(vmem_limit_bytes=mib << 20)


def bit_of(axis, bit):
    return (lax.axis_index(axis) >> bit) & 1


def place(bits, parity, rows):
    return 2 * bits[0] + parity, pl.multiple_of((2 * bits[1] + bits[2]) * rows, 8)


def piece_place(k, parity, rows):
    return place([bit_of(*dim) ^ ((k >> (2 - i)) & 1) for i, dim in enumerate(DIMS)], parity, rows)


def slot_bits(j, order):
    flip = [0, 0, 0]
    for i, dim in enumerate(order):
        flip[dim] = (j >> (2 - i)) & 1
    return flip


def slot_place(j, parity, rows):
    a, b = slot_bits(j, ORDERS[0]), slot_bits(j, ORDERS[1])
    flip = [x if x == y else jnp.where(parity == 0, x, y) for x, y in zip(a, b)]
    return place([bit_of(*dim) ^ f for dim, f in zip(DIMS, flip)], parity, rows)


def split(x):
    high = x.astype(BF16)
    return high, (x - high.astype(F32)).astype(BF16)


def segments(first, rows, shard):
    me = lax.axis_index("sector")
    if first:
        out = [[(h, me ^ side, h * rows, 0, rows) for h in range(CHUNKS)] for side in range(2)]
        out += [[(h, me ^ (2 + side), 0, 0, rows)] for h in range(CHUNKS) for side in range(2)]
        return out
    out = []
    for number in range(16):
        sector, row = piece_place(number >> 1, (me & 1) ^ (number & 1), shard)
        out.append([(h, sector, h * shard, row, shard) for h in range(CHUNKS)])
    return out


def prep_kernel(left_ref, right_ref, psi_ref, diag_ref, left_cat, right_cat, vec_ref, mine_ref):
    b = left_ref.shape[-1]

    def one(p, carry):
        high, low = split(left_ref[p])
        for place, x in enumerate((high, low, high)):
            left_cat[p, :, place * b:(place + 1) * b] = x
        high, low = split(right_ref[p])
        for place, x in enumerate((high, high, low)):
            right_cat[p, :, place * b:(place + 1) * b] = x
        return carry

    lax.fori_loop(0, left_ref.shape[0], one, 0)
    rows = vec_ref.shape[0] // CHUNKS
    for h in range(CHUNKS):
        _, row = piece_place(0, 0, rows)
        at = pl.ds(pl.multiple_of(row + h * 4 * rows, 8), rows)
        vec_ref[h * rows:(h + 1) * rows, :] = psi_ref[0, at, :]
        mine_ref[h * rows:(h + 1) * rows, :] = diag_ref[0, at, :]


def prepare(left_ops, right_ops, psi, diag):
    pairs, b, _ = left_ops.shape
    shard = jax.ShapeDtypeStruct((b // 4, b), F32)
    return pl.pallas_call(
        prep_kernel,
        in_specs=[VMEM] * 4,
        out_specs=[VMEM] * 4,
        out_shape=[jax.ShapeDtypeStruct((pairs, b, 3 * b), BF16)] * 2 + [shard] * 2,
        compiler_params=grant(16),
        cost_estimate=pl.CostEstimate(
            flops=4 * left_ops.size, bytes_accessed=20 * left_ops.size, transcendentals=0
        ),
    )(left_ops, right_ops, psi, diag)


def store_wide(dest, start, x):
    rows = x.shape[0]
    for c in range(x.shape[1] // TILE[1]):
        dest[start + c * rows:start + (c + 1) * rows, :] = x[:, c * TILE[1]:(c + 1) * TILE[1]]


DOT_NT = functools.partial(
    lax.dot_general, dimension_numbers=(((1,), (1,)), ((), ())), preferred_element_type=F32
)
DOT = functools.partial(jnp.dot, preferred_element_type=F32)


def inner_kernel(first, half, cells, pieces, *refs):
    in_ref, count_ref, *refs = refs
    parts = refs[:pieces]
    refs = refs[pieces:]
    if half == 0:
        right, early_h, early_l, squares_ref, vec = refs
    elif half == 1:
        right, early_h, early_l, squares_ref, cat_ref, inv_ref, vec = refs
    else:
        right, cat_ref, inv_ref, vec = refs
    b = right.shape[1]
    rows = b // CHUNKS
    shard = rows // 4
    total = jnp.zeros((1, b), F32)
    cuts_of = segments(first, rows, shard)
    for piece, cuts in zip(parts, [cuts_of[i] for i in picked(half, len(cuts_of))]):
        for chunk, sector, start, row, size in cuts:
            if half is not None and chunk != half:
                continue
            x = piece[start:start + size, :]
            high, low = split(x)
            total += jnp.sum(x * x, axis=0, keepdims=True)
            if half is None:
                row = pl.multiple_of(row + chunk * rows, 16)
            at = pl.ds(row, size)
            for place, y in enumerate((high, low, high)):
                vec[sector, at, place * b:(place + 1) * b] = y
    total = jnp.broadcast_to(jnp.sum(total, axis=1, keepdims=True), (TILE[0], b))
    if half == 0:
        squares_ref[...] = total
    else:
        if half == 1:
            total += squares_ref[...]
        inv_ref[...] = lax.rsqrt(total / cells + epsilon)

    def one_pair(p, carry):
        high, low = split(DOT_NT(vec[in_ref[0, p]], right[p]))
        if half == 0:
            early_h[p], early_l[p] = high, low
            return carry
        moves = [(high, low, 0)] if half is None else [(early_h[p], early_l[p], 0), (high, low, rows)]
        for h, l, row in moves:
            for place, y in enumerate((h, h, l)):
                cat_ref[p, place * b + row:place * b + row + h.shape[0], :] = y
        return carry

    lax.fori_loop(0, count_ref[0], one_pair, 0)


def picked(half, pieces):
    return list(range(pieces)) if half is None else [0, 1, 2 + 2 * half, 3 + 2 * half]


def inner(first, half, cells, sectors, pair_in, pair_count, pieces, right, early=()):
    pairs, b, _ = right.shape
    rows = b if half is None else b // CHUNKS
    compact = jax.ShapeDtypeStruct((pairs, rows, b), BF16)
    row = jax.ShapeDtypeStruct((TILE[0], b), F32)
    shapes = [compact, compact, row] if half == 0 else [jax.ShapeDtypeStruct((pairs, 3 * b, b), BF16), row]
    return pl.pallas_call(
        functools.partial(inner_kernel, first, half, cells, len(pieces)),
        in_specs=[SMEM] * 2 + [VMEM] * (len(pieces) + 1 + len(early)),
        out_specs=[VMEM] * len(shapes),
        out_shape=shapes,
        scratch_shapes=[pltpu.VMEM((sectors, rows, 3 * b), BF16)],
        compiler_params=grant(16),
        cost_estimate=matmul_cost(pairs, rows, b),
    )(pair_in, pair_count, *pieces, right, *early)


def outer_kernel(first, chunk, cells, pieces, *refs):
    out_ref, count_ref, *refs = refs
    parts = refs[:pieces]
    left, cat, inv_ref, before_ref, send_ref, keep_ref, rho_ref, acc = refs[pieces:]
    _, rows, b = acc.shape
    shard = rows // 4
    core = lax.axis_index("sector") & 1
    acc[...] = jnp.zeros_like(acc)
    here = slice(chunk * rows, (chunk + 1) * rows)

    def one_pair(p, carry):
        target = out_ref[0, p]
        acc[target] += DOT(left[p, here, :], cat[p])
        return carry

    lax.fori_loop(0, count_ref[0], one_pair, 0)
    scale = inv_ref[:1, :]
    rho = jnp.zeros((1, b), F32)
    wide = shard * b // TILE[1]
    for piece, cuts in zip(parts, segments(first, rows, shard)):
        for at, sector, start, row, size in cuts:
            if at == chunk:
                x = acc[sector, pl.ds(row, size), :] * piece[start:start + size, :]
                rho += jnp.sum(x, axis=0, keepdims=True)
    for dest, parity in ((send_ref, 1 - core), (keep_ref, core)):
        for j in range(8):
            sector, row = slot_place(j, parity, shard)
            store_wide(dest, j * wide, acc[sector, pl.ds(row, shard), :] * scale)
    rho = jnp.broadcast_to(jnp.sum(rho * scale * scale, axis=1, keepdims=True), TILE) / cells + before_ref[...]
    rho_ref[...] = rho
    if chunk == CHUNKS - 1:
        send_ref[8 * wide:, :] = rho
        keep_ref[8 * wide:, :] = rho


def outer(first, chunk, cells, sectors, pair_out, pair_count, pieces, ops, inv, before):
    pairs, _, b = ops[1].shape
    rows = b // CHUNKS
    extra = TILE[0] if chunk == CHUNKS - 1 else 0
    half = jax.ShapeDtypeStruct((sectors * rows // 2 * b // TILE[1] + extra, TILE[1]), F32)
    return pl.pallas_call(
        functools.partial(outer_kernel, first, chunk, cells, len(pieces)),
        in_specs=[SMEM] * 2 + [VMEM] * (len(pieces) + 4),
        out_specs=[VMEM] * 3,
        out_shape=[half, half, jax.ShapeDtypeStruct(TILE, F32)],
        scratch_shapes=[pltpu.VMEM((sectors, rows, b), F32)],
        compiler_params=grant(20),
        cost_estimate=matmul_cost(pairs, rows, b),
    )(pair_out, pair_count, *pieces, *ops, inv, before)


def combine_kernel(keep_ref, recv_ref, next_ref, send_ref=None):
    extra = 0 if send_ref is None else 2 * next_ref.shape[0] - keep_ref.shape[0]
    rows = next_ref.shape[0] - extra
    next_ref[:rows, :] = keep_ref[:rows, :] + recv_ref[:rows, :]
    if send_ref is None:
        return
    send_ref[:rows, :] = keep_ref[rows:2 * rows, :] + recv_ref[rows:2 * rows, :]
    if extra:
        total = keep_ref[2 * rows:, :] + recv_ref[2 * rows:, :]
        next_ref[rows:, :] = total
        send_ref[rows:, :] = total


def combine(keep, recv, extra):
    shape = jax.ShapeDtypeStruct(((keep.shape[0] - extra) // 2 + extra, TILE[1]), F32)
    return pl.pallas_call(
        combine_kernel,
        in_specs=[VMEM] * 2,
        out_specs=[VMEM] * 2,
        out_shape=[shape] * 2,
        compiler_params=grant(4),
    )(keep, recv)


def total(mine, recv):
    return pl.pallas_call(
        combine_kernel,
        in_specs=[VMEM] * 2,
        out_specs=VMEM,
        out_shape=jax.ShapeDtypeStruct(mine.shape, F32),
        compiler_params=grant(4),
    )(mine, recv)


def update_kernel(*refs):
    sums, (vec_ref, inv_ref, diag_ref, new_ref, energy_ref) = refs[:2 * CHUNKS], refs[2 * CHUNKS:]
    rows, b = new_ref.shape
    shard = rows // CHUNKS
    end = shard * b // TILE[1]
    rho = sums[-2][end:, :] + sums[-1][end:, :]
    energy_ref[...] = rho
    for h in range(CHUNKS):
        mine_ref, recv_ref = sums[2 * h:2 * h + 2]
        at = slice(h * shard, (h + 1) * shard)
        for c in range(b // TILE[1]):
            part = slice(c * shard, (c + 1) * shard)
            lanes = slice(c * TILE[1], (c + 1) * TILE[1])
            normed = vec_ref[at, lanes] * inv_ref[:1, lanes]
            sigma = mine_ref[part, :] + recv_ref[part, :]
            residual = sigma - rho[:1, :] * normed
            gap = jnp.maximum(jnp.abs(diag_ref[at, lanes] - rho[:1, :]), 1.0)
            new_ref[at, lanes] = normed - residual / gap


def update(sums, vec, inv, diag):
    return pl.pallas_call(
        update_kernel,
        in_specs=[VMEM] * (len(sums) + 3),
        out_specs=[VMEM] * 2,
        out_shape=[jax.ShapeDtypeStruct(vec.shape, F32), jax.ShapeDtypeStruct(TILE, F32)],
        compiler_params=grant(4),
    )(*sums, vec, inv, diag)


def zero_tile(tile):
    def kernel(in_ref, out_ref):
        out_ref[...] = jnp.zeros_like(out_ref)

    return pl.pallas_call(
        kernel, in_specs=[VMEM], out_specs=VMEM, out_shape=jax.ShapeDtypeStruct(TILE, F32), compiler_params=grant(4)
    )(tile)


def join_kernel(*refs):
    *parts, out_ref = refs
    rows = parts[0].shape[0] // CHUNKS
    for k, part in enumerate(parts):
        _, row = piece_place(k, 0, rows)
        for h in range(CHUNKS):
            at = pl.ds(pl.multiple_of(row + h * 4 * rows, 8), rows)
            out_ref[0, at, :] = part[h * rows:(h + 1) * rows, :]


def join(parts):
    quarter, b = parts[0].shape
    return pl.pallas_call(
        join_kernel,
        in_specs=[VMEM] * len(parts),
        out_specs=VMEM,
        out_shape=jax.ShapeDtypeStruct((1, 4 * quarter, b), F32),
        compiler_params=grant(4),
    )(*parts)


def flips(mesh_shape, even, odd):
    terms, sectors = mesh_shape
    pairs = []
    for t in range(terms):
        for s in range(sectors):
            u = {"term": t, "sector": s}
            for axis, bit in odd if s & 1 else even:
                u[axis] ^= 1 << bit
            pairs.append((t * sectors + s, u["term"] * sectors + u["sector"]))
    return pairs


def rest_dims(terms):
    return [("term", bit) for bit in range(2, terms.bit_length() - 1)]


def shards(mesh_shape, psi_start, diagonal, left_ops, right_ops, pair_in, pair_out, pair_count):
    terms, sectors = mesh_shape
    b = psi_start.shape[1]
    cells = float(sectors * b * b)

    def swap(x, even, odd=None):
        return lax.ppermute(x, AXES, flips(mesh_shape, even, even if odd is None else odd))

    def dims_of(k):
        return [dim for i, dim in enumerate(DIMS) if (k >> (2 - i)) & 1]

    away = range(1, 8)
    rest = rest_dims(terms)

    own = psi_start[0]
    rows = b // CHUNKS
    far = []
    for h in range(CHUNKS):
        far.append(swap(own[h * rows:(h + 1) * rows], [DIMS[0]]))
    beside = swap(own, [CORE])
    left, right, vec, diag = prepare(left_ops, right_ops, psi_start, diagonal)
    far[0], left, right, vec, diag = lax.optimization_barrier((far[0], left, right, vec, diag))
    pieces = [own, beside]
    for x in far:
        pieces += [x, swap(x, [CORE])]
    zero = jnp.zeros(TILE, F32)
    energies = []
    for sweep in range(ITERS):
        first = sweep == 0
        args = (cells, sectors, pair_in, pair_count)
        if first:
            early, late = ([pieces[i] for i in picked(half, len(pieces))] for half in range(2))
            early = inner(first, 0, *args, early, right)
            cat, inv = inner(first, 1, *args, late, right, early)
        else:
            cat, inv = inner(first, None, *args, pieces, right)
        rho = zero
        keeps, recvs = [], []
        for h in range(CHUNKS):
            send, keep, rho = outer(
                first, h, cells, sectors, pair_out, pair_count, pieces, (left, cat), inv, rho
            )
            keeps.append(keep)
            recvs.append(swap(send, [CORE]))
        for step in zip(*ORDERS):
            for h in range(CHUNKS):
                extra = TILE[0] if h == CHUNKS - 1 else 0
                keeps[h], send = combine(keeps[h], recvs[h], extra)
                recvs[h] = swap(send, [DIMS[step[0]]], [DIMS[step[1]]])
        for step in rest:
            for h in range(CHUNKS):
                keeps[h] = total(keeps[h], recvs[h])
                recvs[h] = swap(keeps[h], [step])
        sums = [x for pair in zip(keeps, recvs) for x in pair]
        vec, energy = update(sums, vec, inv, diag)
        energies.append(energy[0, 0])
        if sweep < ITERS - 1:
            got = {0: vec}
            zero = zero_tile(energy)
            for k in away:
                got[k] = swap(vec, dims_of(k))
            pieces = []
            for k in range(8):
                pieces += [got[k], swap(got[k], [CORE])]
    got = {k: swap(vec, dims_of(k)) for k in (3, 2, 1)}
    block = join([vec, got[1], got[2], got[3]])
    return block, jnp.stack(energies)


def solution(mesh):
    mesh_shape = (mesh.shape["term"], mesh.shape["sector"])
    return jax.shard_map(
        functools.partial(shards, mesh_shape),
        mesh=mesh,
        in_specs=(
            P("sector", None, None),
            P("sector", None, None),
            P(("term", "sector"), None, None),
            P(("term", "sector"), None, None),
            P(("term", "sector"), None),
            P(("term", "sector"), None),
            P(("term", "sector")),
        ),
        out_specs=(P("sector", None, None), P()),
        check_vma=False,
    )
```

```python
import functools

import jax
import jax.numpy as jnp
from jax import lax
from jax.experimental import pallas as pl
from jax.experimental.pallas import tpu as pltpu
from jax.sharding import PartitionSpec as P


ITERS = 2
AXES = ("term", "sector")
TILE = (8, 128)
CHUNKS = 2

epsilon = 1e-06


VMEM = pl.BlockSpec(memory_space=pltpu.VMEM)
SMEM = pl.BlockSpec(memory_space=pltpu.SMEM)
F32 = jnp.float32
BF16 = jnp.bfloat16

DIMS = (("sector", 1), ("term", 0), ("term", 1))
CORE = ("sector", 0)
ORDERS = ((0, 1, 2), (2, 1, 0))
START_ORDER = (4, 2, 1, 6, 5, 3, 7)


def matmul_cost(pairs, rows, b):
    return pl.CostEstimate(
        flops=6 * pairs * rows * b * b, bytes_accessed=8 * pairs * b * b, transcendentals=0
    )


def grant(mib):
    return pltpu.CompilerParams(vmem_limit_bytes=mib << 20)


def bit_of(axis, bit):
    return (lax.axis_index(axis) >> bit) & 1


def place(bits, parity, rows):
    return 2 * bits[0] + parity, pl.multiple_of((2 * bits[1] + bits[2]) * rows, 8)


def piece_place(k, parity, rows):
    return place([bit_of(*dim) ^ ((k >> (2 - i)) & 1) for i, dim in enumerate(DIMS)], parity, rows)


def slot_of(parity, masks):
    a, b = (sum(masks[dim] << (2 - i) for i, dim in enumerate(order)) for order in ORDERS)
    return jnp.where(parity == 0, a, b)


def split(x):
    high = x.astype(BF16)
    return high, (x - high.astype(F32)).astype(BF16)


def segments(first, rows, shard):
    me = lax.axis_index("sector")
    if first:
        out = [[(h, me ^ side, h * rows, 0, rows) for h in range(CHUNKS)] for side in range(2)]
        out += [[(h, me ^ (2 + side), 0, 0, rows)] for h in range(CHUNKS) for side in range(2)]
        return out
    out = []
    for number in range(16):
        sector, row = piece_place(number >> 1, (me & 1) ^ (number & 1), shard)
        out.append([(h, sector, h * shard, row, shard) for h in range(CHUNKS)])
    return out


def prep_kernel(left_ref, right_ref, psi_ref, diag_ref, left_cat, right_cat, vec_ref, mine_ref):
    b = left_ref.shape[-1]

    def one(p, carry):
        high, low = split(left_ref[p])
        for place, x in enumerate((high, low, high)):
            left_cat[p, :, place * b:(place + 1) * b] = x
        high, low = split(right_ref[p])
        for place, x in enumerate((high, high, low)):
            right_cat[p, :, place * b:(place + 1) * b] = x
        return carry

    lax.fori_loop(0, left_ref.shape[0], one, 0)
    rows = vec_ref.shape[0] // CHUNKS
    for h in range(CHUNKS):
        _, row = piece_place(0, 0, rows)
        at = pl.ds(pl.multiple_of(row + h * 4 * rows, 8), rows)
        vec_ref[h * rows:(h + 1) * rows, :] = psi_ref[0, at, :]
        mine_ref[h * rows:(h + 1) * rows, :] = diag_ref[0, at, :]


def prepare(left_ops, right_ops, psi, diag):
    pairs, b, _ = left_ops.shape
    shard = jax.ShapeDtypeStruct((b // 4, b), F32)
    return pl.pallas_call(
        prep_kernel,
        in_specs=[VMEM] * 4,
        out_specs=[VMEM] * 4,
        out_shape=[jax.ShapeDtypeStruct((pairs, b, 3 * b), BF16)] * 2 + [shard] * 2,
        compiler_params=grant(16),
        cost_estimate=pl.CostEstimate(
            flops=4 * left_ops.size, bytes_accessed=20 * left_ops.size, transcendentals=0
        ),
    )(left_ops, right_ops, psi, diag)


def store_wide(dest, start, x):
    rows = x.shape[0]
    for c in range(x.shape[1] // TILE[1]):
        dest[pl.ds(start + c * rows, rows), :] = x[:, c * TILE[1]:(c + 1) * TILE[1]]


DOT_NT = functools.partial(
    lax.dot_general, dimension_numbers=(((1,), (1,)), ((), ())), preferred_element_type=F32
)
DOT = functools.partial(jnp.dot, preferred_element_type=F32)


def inner_kernel(first, half, cells, pieces, *refs):
    in_ref, count_ref, *refs = refs
    parts = refs[:pieces]
    refs = refs[pieces:]
    if half == 0:
        right, early_h, early_l, squares_ref, vec = refs
    elif half == 1:
        right, early_h, early_l, squares_ref, cat_ref, inv_ref, vec = refs
    else:
        right, cat_ref, inv_ref, vec = refs
    b = right.shape[1]
    rows = b // CHUNKS
    shard = rows // 4
    total = jnp.zeros((1, b), F32)
    cuts_of = segments(first, rows, shard)
    for piece, cuts in zip(parts, [cuts_of[i] for i in picked(half, len(cuts_of))]):
        for chunk, sector, start, row, size in cuts:
            if half is not None and chunk != half:
                continue
            x = piece[start:start + size, :]
            high, low = split(x)
            total += jnp.sum(x * x, axis=0, keepdims=True)
            if half is None:
                row = pl.multiple_of(row + chunk * rows, 16)
            at = pl.ds(row, size)
            for place, y in enumerate((high, low, high)):
                vec[sector, at, place * b:(place + 1) * b] = y
    total = jnp.broadcast_to(jnp.sum(total, axis=1, keepdims=True), (TILE[0], b))
    if half == 0:
        squares_ref[...] = total
    else:
        if half == 1:
            total += squares_ref[...]
        inv_ref[...] = lax.rsqrt(total / cells + epsilon)

    def one_pair(p, carry):
        high, low = split(DOT_NT(vec[in_ref[0, p]], right[p]))
        if half == 0:
            early_h[p], early_l[p] = high, low
            return carry
        moves = [(high, low, 0)] if half is None else [(early_h[p], early_l[p], 0), (high, low, rows)]
        for h, l, row in moves:
            for place, y in enumerate((h, h, l)):
                cat_ref[p, place * b + row:place * b + row + h.shape[0], :] = y
        return carry

    lax.fori_loop(0, count_ref[0], one_pair, 0)


def picked(half, pieces):
    return list(range(pieces)) if half is None else [0, 1, 2 + 2 * half, 3 + 2 * half]


def inner(first, half, cells, sectors, pair_in, pair_count, pieces, right, early=()):
    pairs, b, _ = right.shape
    rows = b if half is None else b // CHUNKS
    compact = jax.ShapeDtypeStruct((pairs, rows, b), BF16)
    row = jax.ShapeDtypeStruct((TILE[0], b), F32)
    shapes = [compact, compact, row] if half == 0 else [jax.ShapeDtypeStruct((pairs, 3 * b, b), BF16), row]
    return pl.pallas_call(
        functools.partial(inner_kernel, first, half, cells, len(pieces)),
        in_specs=[SMEM] * 2 + [VMEM] * (len(pieces) + 1 + len(early)),
        out_specs=[VMEM] * len(shapes),
        out_shape=shapes,
        scratch_shapes=[pltpu.VMEM((sectors, rows, 3 * b), BF16)],
        compiler_params=grant(16),
        cost_estimate=matmul_cost(pairs, rows, b),
    )(pair_in, pair_count, *pieces, right, *early)


def outer_kernel(first, chunk, cells, pieces, *refs):
    out_ref, count_ref, *refs = refs
    parts = refs[:pieces]
    left, cat, inv_ref, before_ref, send_ref, keep_ref, rho_ref, acc = refs[pieces:]
    _, rows, b = acc.shape
    shard = rows // 4
    core = lax.axis_index("sector") & 1
    acc[...] = jnp.zeros_like(acc)
    here = slice(chunk * rows, (chunk + 1) * rows)

    def one_pair(p, carry):
        target = out_ref[0, p]
        acc[target] += DOT(left[p, here, :], cat[p])
        return carry

    lax.fori_loop(0, count_ref[0], one_pair, 0)
    scale = inv_ref[:1, :]
    rho = jnp.zeros((1, b), F32)
    wide = shard * b // TILE[1]
    for number, (piece, cuts) in enumerate(zip(parts, segments(first, rows, shard))):
        side = number & 1
        dest = send_ref if side else keep_ref
        for at, sector, start, row, size in cuts:
            if at != chunk:
                continue
            for q in range(size // shard):
                if first:
                    masks = (int(number > 1), (q >> 1) ^ bit_of(*DIMS[1]), (q & 1) ^ bit_of(*DIMS[2]))
                    here = pl.ds(q * shard, shard)
                else:
                    masks = tuple((number >> (3 - i)) & 1 for i in range(3))
                    here = pl.ds(row, shard)
                x = acc[sector, here, :] * scale
                slot = slot_of(core ^ side, masks)
                store_wide(dest, pl.multiple_of(slot * wide, 8), x)
                rho += jnp.sum(x * piece[start + q * shard:start + (q + 1) * shard, :], axis=0, keepdims=True)
    rho = jnp.broadcast_to(jnp.sum(rho * scale, axis=1, keepdims=True), TILE) / cells + before_ref[...]
    rho_ref[...] = rho
    if chunk == CHUNKS - 1:
        send_ref[8 * wide:, :] = rho
        keep_ref[8 * wide:, :] = rho


def outer(first, chunk, cells, sectors, pair_out, pair_count, pieces, ops, inv, before):
    pairs, _, b = ops[1].shape
    rows = b // CHUNKS
    extra = TILE[0] if chunk == CHUNKS - 1 else 0
    half = jax.ShapeDtypeStruct((sectors * rows // 2 * b // TILE[1] + extra, TILE[1]), F32)
    return pl.pallas_call(
        functools.partial(outer_kernel, first, chunk, cells, len(pieces)),
        in_specs=[SMEM] * 2 + [VMEM] * (len(pieces) + 4),
        out_specs=[VMEM] * 3,
        out_shape=[half, half, jax.ShapeDtypeStruct(TILE, F32)],
        scratch_shapes=[pltpu.VMEM((sectors, rows, b), F32)],
        compiler_params=grant(20),
        cost_estimate=matmul_cost(pairs, rows, b),
    )(pair_out, pair_count, *pieces, *ops, inv, before)


def combine_kernel(keep_ref, recv_ref, next_ref, send_ref=None):
    extra = 0 if send_ref is None else 2 * next_ref.shape[0] - keep_ref.shape[0]
    rows = next_ref.shape[0] - extra
    next_ref[:rows, :] = keep_ref[:rows, :] + recv_ref[:rows, :]
    if send_ref is None:
        return
    send_ref[:rows, :] = keep_ref[rows:2 * rows, :] + recv_ref[rows:2 * rows, :]
    if extra:
        total = keep_ref[2 * rows:, :] + recv_ref[2 * rows:, :]
        next_ref[rows:, :] = total
        send_ref[rows:, :] = total


def combine(keep, recv, extra):
    shape = jax.ShapeDtypeStruct(((keep.shape[0] - extra) // 2 + extra, TILE[1]), F32)
    return pl.pallas_call(
        combine_kernel,
        in_specs=[VMEM] * 2,
        out_specs=[VMEM] * 2,
        out_shape=[shape] * 2,
        compiler_params=grant(4),
    )(keep, recv)


def total(mine, recv):
    return pl.pallas_call(
        combine_kernel,
        in_specs=[VMEM] * 2,
        out_specs=VMEM,
        out_shape=jax.ShapeDtypeStruct(mine.shape, F32),
        compiler_params=grant(4),
    )(mine, recv)


def update_kernel(*refs):
    sums, (vec_ref, inv_ref, diag_ref, new_ref, energy_ref) = refs[:2 * CHUNKS], refs[2 * CHUNKS:]
    rows, b = new_ref.shape
    shard = rows // CHUNKS
    end = shard * b // TILE[1]
    rho = sums[-2][end:, :] + sums[-1][end:, :]
    energy_ref[...] = rho
    for h in range(CHUNKS):
        mine_ref, recv_ref = sums[2 * h:2 * h + 2]
        at = slice(h * shard, (h + 1) * shard)
        for c in range(b // TILE[1]):
            part = slice(c * shard, (c + 1) * shard)
            lanes = slice(c * TILE[1], (c + 1) * TILE[1])
            normed = vec_ref[at, lanes] * inv_ref[:1, lanes]
            sigma = mine_ref[part, :] + recv_ref[part, :]
            residual = sigma - rho[:1, :] * normed
            gap = jnp.maximum(jnp.abs(diag_ref[at, lanes] - rho[:1, :]), 1.0)
            new_ref[at, lanes] = normed - residual / gap


def update(sums, vec, inv, diag):
    return pl.pallas_call(
        update_kernel,
        in_specs=[VMEM] * (len(sums) + 3),
        out_specs=[VMEM] * 2,
        out_shape=[jax.ShapeDtypeStruct(vec.shape, F32), jax.ShapeDtypeStruct(TILE, F32)],
        compiler_params=grant(4),
    )(*sums, vec, inv, diag)


def zero_tile(tile):
    def kernel(in_ref, out_ref):
        out_ref[...] = jnp.zeros_like(out_ref)

    return pl.pallas_call(
        kernel, in_specs=[VMEM], out_specs=VMEM, out_shape=jax.ShapeDtypeStruct(TILE, F32), compiler_params=grant(4)
    )(tile)


def join_kernel(*refs):
    *parts, out_ref = refs
    rows = parts[0].shape[0] // CHUNKS
    for k, part in enumerate(parts):
        _, row = piece_place(k, 0, rows)
        for h in range(CHUNKS):
            at = pl.ds(pl.multiple_of(row + h * 4 * rows, 8), rows)
            out_ref[0, at, :] = part[h * rows:(h + 1) * rows, :]


def join(parts):
    quarter, b = parts[0].shape
    return pl.pallas_call(
        join_kernel,
        in_specs=[VMEM] * len(parts),
        out_specs=VMEM,
        out_shape=jax.ShapeDtypeStruct((1, 4 * quarter, b), F32),
        compiler_params=grant(4),
    )(*parts)


def flips(mesh_shape, even, odd):
    terms, sectors = mesh_shape
    pairs = []
    for t in range(terms):
        for s in range(sectors):
            u = {"term": t, "sector": s}
            for axis, bit in odd if s & 1 else even:
                u[axis] ^= 1 << bit
            pairs.append((t * sectors + s, u["term"] * sectors + u["sector"]))
    return pairs


def rest_dims(terms):
    return [("term", bit) for bit in range(2, terms.bit_length() - 1)]


def shards(mesh_shape, psi_start, diagonal, left_ops, right_ops, pair_in, pair_out, pair_count):
    terms, sectors = mesh_shape
    b = psi_start.shape[1]
    cells = float(sectors * b * b)

    def swap(x, even, odd=None):
        return lax.ppermute(x, AXES, flips(mesh_shape, even, even if odd is None else odd))

    def dims_of(k):
        return [dim for i, dim in enumerate(DIMS) if (k >> (2 - i)) & 1]

    away = START_ORDER
    rest = rest_dims(terms)

    own = psi_start[0]
    rows = b // CHUNKS
    far = []
    for h in range(CHUNKS):
        far.append(swap(own[h * rows:(h + 1) * rows], [DIMS[0]]))
    beside = swap(own, [CORE])
    left, right, vec, diag = prepare(left_ops, right_ops, psi_start, diagonal)
    far[0], left, right, vec, diag = lax.optimization_barrier((far[0], left, right, vec, diag))
    pieces = [own, beside]
    for x in far:
        pieces += [x, swap(x, [CORE])]
    zero = jnp.zeros(TILE, F32)
    energies = []
    for sweep in range(ITERS):
        first = sweep == 0
        args = (cells, sectors, pair_in, pair_count)
        if first:
            early, late = ([pieces[i] for i in picked(half, len(pieces))] for half in range(2))
            early = inner(first, 0, *args, early, right)
            cat, inv = inner(first, 1, *args, late, right, early)
        else:
            cat, inv = inner(first, None, *args, pieces, right)
        rho = zero
        keeps, recvs = [], []
        for h in range(CHUNKS):
            send, keep, rho = outer(first, h, cells, sectors, pair_out, pair_count, pieces, (left, cat), inv, rho)
            keeps.append(keep)
            recvs.append(swap(send, [CORE]))
        for step in zip(*ORDERS):
            for h in range(CHUNKS):
                extra = TILE[0] if h == CHUNKS - 1 else 0
                keeps[h], send = combine(keeps[h], recvs[h], extra)
                recvs[h] = swap(send, [DIMS[step[0]]], [DIMS[step[1]]])
        for step in rest:
            for h in range(CHUNKS):
                keeps[h] = total(keeps[h], recvs[h])
                recvs[h] = swap(keeps[h], [step])
        sums = [x for pair in zip(keeps, recvs) for x in pair]
        vec, energy = update(sums, vec, inv, diag)
        energies.append(energy[0, 0])
        if sweep < ITERS - 1:
            got = {0: vec}
            zero = zero_tile(energy)
            for k in away:
                got[k] = swap(vec, dims_of(k))
            pieces = []
            for k in range(8):
                pieces += [got[k], swap(got[k], [CORE])]
    got = {k: swap(vec, dims_of(k)) for k in (3, 2, 1)}
    block = join([vec, got[1], got[2], got[3]])
    return block, jnp.stack(energies)


def solution(mesh):
    mesh_shape = (mesh.shape["term"], mesh.shape["sector"])
    return jax.shard_map(
        functools.partial(shards, mesh_shape),
        mesh=mesh,
        in_specs=(
            P("sector", None, None),
            P("sector", None, None),
            P(("term", "sector"), None, None),
            P(("term", "sector"), None, None),
            P(("term", "sector"), None),
            P(("term", "sector"), None),
            P(("term", "sector")),
        ),
        out_specs=(P("sector", None, None), P()),
        check_vma=False,
    )
```

```python
import functools

import jax
import jax.numpy as jnp
from jax import lax
from jax.experimental import pallas as pl
from jax.experimental.pallas import tpu as pltpu
from jax.sharding import PartitionSpec as P


ITERS = 2
AXES = ("term", "sector")
TILE = (8, 128)
CHUNKS = 2

epsilon = 1e-06


VMEM = pl.BlockSpec(memory_space=pltpu.VMEM)
SMEM = pl.BlockSpec(memory_space=pltpu.SMEM)
F32 = jnp.float32
BF16 = jnp.bfloat16

DIMS = (("sector", 1), ("term", 0), ("term", 1))
CORE = ("sector", 0)
ORDERS = ((0, 1, 2), (2, 1, 0))
START_ORDER = (4, 2, 1, 6, 5, 3, 7)


def matmul_cost(pairs, rows, b):
    return pl.CostEstimate(
        flops=6 * pairs * rows * b * b, bytes_accessed=8 * pairs * b * b, transcendentals=0
    )


def grant(mib):
    return pltpu.CompilerParams(vmem_limit_bytes=mib << 20)


def bit_of(axis, bit):
    return (lax.axis_index(axis) >> bit) & 1


def place(bits, parity, rows):
    return 2 * bits[0] + parity, pl.multiple_of((2 * bits[1] + bits[2]) * rows, 8)


def piece_place(k, parity, rows):
    return place([bit_of(*dim) ^ ((k >> (2 - i)) & 1) for i, dim in enumerate(DIMS)], parity, rows)


def slot_of(parity, masks):
    a, b = (sum(masks[dim] << (2 - i) for i, dim in enumerate(order)) for order in ORDERS)
    return jnp.where(parity == 0, a, b)


def split(x):
    high = x.astype(BF16)
    return high, (x - high.astype(F32)).astype(BF16)


def segments(first, rows, shard):
    me = lax.axis_index("sector")
    if first:
        out = [[(h, me ^ side, h * rows, 0, rows) for h in range(CHUNKS)] for side in range(2)]
        out += [[(h, me ^ (2 + side), 0, 0, rows)] for h in range(CHUNKS) for side in range(2)]
        return out
    out = []
    for number in range(16):
        sector, row = piece_place(number >> 1, (me & 1) ^ (number & 1), shard)
        out.append([(h, sector, h * shard, row, shard) for h in range(CHUNKS)])
    return out


def prep_kernel(left_ref, right_ref, psi_ref, diag_ref, left_cat, right_cat, vec_ref, mine_ref):
    b = left_ref.shape[-1]

    def one(p, carry):
        high, low = split(left_ref[p])
        for place, x in enumerate((high, low, high)):
            left_cat[p, :, place * b:(place + 1) * b] = x
        high, low = split(right_ref[p])
        for place, x in enumerate((high, high, low)):
            right_cat[p, :, place * b:(place + 1) * b] = x
        return carry

    lax.fori_loop(0, left_ref.shape[0], one, 0)
    rows = vec_ref.shape[0] // CHUNKS
    for h in range(CHUNKS):
        _, row = piece_place(0, 0, rows)
        at = pl.ds(pl.multiple_of(row + h * 4 * rows, 8), rows)
        vec_ref[h * rows:(h + 1) * rows, :] = psi_ref[0, at, :]
        mine_ref[h * rows:(h + 1) * rows, :] = diag_ref[0, at, :]


def prepare(left_ops, right_ops, psi, diag):
    pairs, b, _ = left_ops.shape
    shard = jax.ShapeDtypeStruct((b // 4, b), F32)
    return pl.pallas_call(
        prep_kernel,
        in_specs=[VMEM] * 4,
        out_specs=[VMEM] * 4,
        out_shape=[jax.ShapeDtypeStruct((pairs, b, 3 * b), BF16)] * 2 + [shard] * 2,
        compiler_params=grant(16),
        cost_estimate=pl.CostEstimate(
            flops=4 * left_ops.size, bytes_accessed=20 * left_ops.size, transcendentals=0
        ),
    )(left_ops, right_ops, psi, diag)


def store_wide(dest, start, x):
    rows = x.shape[0]
    for c in range(x.shape[1] // TILE[1]):
        dest[pl.ds(start + c * rows, rows), :] = x[:, c * TILE[1]:(c + 1) * TILE[1]]


DOT_NT = functools.partial(
    lax.dot_general, dimension_numbers=(((1,), (1,)), ((), ())), preferred_element_type=F32
)
DOT = functools.partial(jnp.dot, preferred_element_type=F32)


def inner_kernel(first, half, cells, pieces, *refs):
    in_ref, count_ref, *refs = refs
    parts = refs[:pieces]
    refs = refs[pieces:]
    if half == 0:
        right, early_h, early_l, squares_ref, vec = refs
    elif half == 1:
        right, early_h, early_l, squares_ref, cat_ref, inv_ref, vec = refs
    else:
        right, cat_ref, inv_ref, vec = refs
    b = right.shape[1]
    rows = b // CHUNKS
    shard = rows // 4
    total = jnp.zeros((1, b), F32)
    cuts_of = segments(first, rows, shard)
    for piece, cuts in zip(parts, [cuts_of[i] for i in picked(half, len(cuts_of))]):
        for chunk, sector, start, row, size in cuts:
            if half is not None and chunk != half:
                continue
            x = piece[start:start + size, :]
            high, low = split(x)
            total += jnp.sum(x * x, axis=0, keepdims=True)
            if half is None:
                row = pl.multiple_of(row + chunk * rows, 16)
            at = pl.ds(row, size)
            for place, y in enumerate((high, low, high)):
                vec[sector, at, place * b:(place + 1) * b] = y
    total = jnp.broadcast_to(jnp.sum(total, axis=1, keepdims=True), (TILE[0], b))
    if half == 0:
        squares_ref[...] = total
    else:
        if half == 1:
            total += squares_ref[...]
        inv_ref[...] = lax.rsqrt(total / cells + epsilon)

    def one_pair(p, carry):
        high, low = split(DOT_NT(vec[in_ref[0, p]], right[p]))
        if half == 0:
            early_h[p], early_l[p] = high, low
            return carry
        moves = [(high, low, 0)] if half is None else [(early_h[p], early_l[p], 0), (high, low, rows)]
        for h, l, row in moves:
            for place, y in enumerate((h, h, l)):
                cat_ref[p, place * b + row:place * b + row + h.shape[0], :] = y
        return carry

    lax.fori_loop(0, count_ref[0], one_pair, 0)


def picked(half, pieces):
    return list(range(pieces)) if half is None else [0, 1, 2 + 2 * half, 3 + 2 * half]


def inner(first, half, cells, sectors, pair_in, pair_count, pieces, right, early=()):
    pairs, b, _ = right.shape
    rows = b if half is None else b // CHUNKS
    compact = jax.ShapeDtypeStruct((pairs, rows, b), BF16)
    row = jax.ShapeDtypeStruct((TILE[0], b), F32)
    shapes = [compact, compact, row] if half == 0 else [jax.ShapeDtypeStruct((pairs, 3 * b, b), BF16), row]
    return pl.pallas_call(
        functools.partial(inner_kernel, first, half, cells, len(pieces)),
        in_specs=[SMEM] * 2 + [VMEM] * (len(pieces) + 1 + len(early)),
        out_specs=[VMEM] * len(shapes),
        out_shape=shapes,
        scratch_shapes=[pltpu.VMEM((sectors, rows, 3 * b), BF16)],
        compiler_params=grant(16),
        cost_estimate=matmul_cost(pairs, rows, b),
    )(pair_in, pair_count, *pieces, right, *early)


def outer_kernel(first, chunk, cells, pieces, *refs):
    out_ref, count_ref, *refs = refs
    parts = refs[:pieces]
    left, cat, inv_ref, before_ref, send_ref, keep_ref, rho_ref, acc = refs[pieces:]
    _, rows, b = acc.shape
    shard = rows // 4
    core = lax.axis_index("sector") & 1
    acc[...] = jnp.zeros_like(acc)
    here = slice(chunk * rows, (chunk + 1) * rows)

    def one_pair(p, carry):
        target = out_ref[0, p]
        acc[target] += DOT(left[p, here, :], cat[p])
        return carry

    lax.fori_loop(0, count_ref[0], one_pair, 0)
    scale = inv_ref[:1, :]
    rho = jnp.zeros((1, b), F32)
    wide = shard * b // TILE[1]
    for number, (piece, cuts) in enumerate(zip(parts, segments(first, rows, shard))):
        side = number & 1
        dest = send_ref if side else keep_ref
        for at, sector, start, row, size in cuts:
            if at != chunk:
                continue
            for q in range(size // shard):
                if first:
                    masks = (int(number > 1), (q >> 1) ^ bit_of(*DIMS[1]), (q & 1) ^ bit_of(*DIMS[2]))
                    here = pl.ds(q * shard, shard)
                else:
                    masks = tuple((number >> (3 - i)) & 1 for i in range(3))
                    here = pl.ds(row, shard)
                x = acc[sector, here, :] * scale
                slot = slot_of(core ^ side, masks)
                store_wide(dest, pl.multiple_of(slot * wide, 8), x)
                rho += jnp.sum(x * piece[start + q * shard:start + (q + 1) * shard, :], axis=0, keepdims=True)
    rho = jnp.broadcast_to(jnp.sum(rho * scale, axis=1, keepdims=True), TILE) / cells + before_ref[...]
    rho_ref[...] = rho
    if chunk == CHUNKS - 1:
        send_ref[8 * wide:, :] = rho
        keep_ref[8 * wide:, :] = rho


def outer(first, chunk, cells, sectors, pair_out, pair_count, pieces, ops, inv, before):
    pairs, _, b = ops[1].shape
    rows = b // CHUNKS
    extra = TILE[0] if chunk == CHUNKS - 1 else 0
    half = jax.ShapeDtypeStruct((sectors * rows // 2 * b // TILE[1] + extra, TILE[1]), F32)
    return pl.pallas_call(
        functools.partial(outer_kernel, first, chunk, cells, len(pieces)),
        in_specs=[SMEM] * 2 + [VMEM] * (len(pieces) + 4),
        out_specs=[VMEM] * 3,
        out_shape=[half, half, jax.ShapeDtypeStruct(TILE, F32)],
        scratch_shapes=[pltpu.VMEM((sectors, rows, b), F32)],
        compiler_params=grant(20),
        cost_estimate=matmul_cost(pairs, rows, b),
    )(pair_out, pair_count, *pieces, *ops, inv, before)


def cut_kernel(extra, keep_ref, recv_ref, *slots):
    rows = slots[0].shape[0] - extra
    end = len(slots) * rows
    for k, slot in enumerate(slots):
        slot[:rows, :] = keep_ref[k * rows:(k + 1) * rows, :] + recv_ref[k * rows:(k + 1) * rows, :]
        if extra:
            slot[rows:, :] = keep_ref[end:, :] + recv_ref[end:, :]


def cut(keep, recv, extra, ways):
    shape = jax.ShapeDtypeStruct(((recv.shape[0] - extra) // ways + extra, TILE[1]), F32)
    return pl.pallas_call(
        functools.partial(cut_kernel, extra),
        in_specs=[VMEM] * 2,
        out_specs=[VMEM] * ways,
        out_shape=[shape] * ways,
        compiler_params=grant(4),
    )(keep, recv)


def sum_kernel(*refs):
    *parts, out_ref = refs
    total = parts[0][...]
    for part in parts[1:]:
        total += part[...]
    out_ref[...] = total


def sum_of(parts):
    return pl.pallas_call(
        sum_kernel,
        in_specs=[VMEM] * len(parts),
        out_specs=VMEM,
        out_shape=jax.ShapeDtypeStruct(parts[0].shape, F32),
        compiler_params=grant(4),
    )(*parts)


def update_kernel(*refs):
    sums, (vec_ref, inv_ref, diag_ref, new_ref, energy_ref) = refs[:2 * CHUNKS], refs[2 * CHUNKS:]
    rows, b = new_ref.shape
    shard = rows // CHUNKS
    end = shard * b // TILE[1]
    rho = sums[-2][end:, :] + sums[-1][end:, :]
    energy_ref[...] = rho
    for h in range(CHUNKS):
        mine_ref, recv_ref = sums[2 * h:2 * h + 2]
        at = slice(h * shard, (h + 1) * shard)
        for c in range(b // TILE[1]):
            part = slice(c * shard, (c + 1) * shard)
            lanes = slice(c * TILE[1], (c + 1) * TILE[1])
            normed = vec_ref[at, lanes] * inv_ref[:1, lanes]
            sigma = mine_ref[part, :] + recv_ref[part, :]
            residual = sigma - rho[:1, :] * normed
            gap = jnp.maximum(jnp.abs(diag_ref[at, lanes] - rho[:1, :]), 1.0)
            new_ref[at, lanes] = normed - residual / gap


def update(sums, vec, inv, diag):
    return pl.pallas_call(
        update_kernel,
        in_specs=[VMEM] * (len(sums) + 3),
        out_specs=[VMEM] * 2,
        out_shape=[jax.ShapeDtypeStruct(vec.shape, F32), jax.ShapeDtypeStruct(TILE, F32)],
        compiler_params=grant(4),
    )(*sums, vec, inv, diag)


def zero_tile(tile):
    def kernel(in_ref, out_ref):
        out_ref[...] = jnp.zeros_like(out_ref)

    return pl.pallas_call(
        kernel, in_specs=[VMEM], out_specs=VMEM, out_shape=jax.ShapeDtypeStruct(TILE, F32), compiler_params=grant(4)
    )(tile)


def join_kernel(*refs):
    *parts, out_ref = refs
    rows = parts[0].shape[0] // CHUNKS
    for k, part in enumerate(parts):
        _, row = piece_place(k, 0, rows)
        for h in range(CHUNKS):
            at = pl.ds(pl.multiple_of(row + h * 4 * rows, 8), rows)
            out_ref[0, at, :] = part[h * rows:(h + 1) * rows, :]


def join(parts):
    quarter, b = parts[0].shape
    return pl.pallas_call(
        join_kernel,
        in_specs=[VMEM] * len(parts),
        out_specs=VMEM,
        out_shape=jax.ShapeDtypeStruct((1, 4 * quarter, b), F32),
        compiler_params=grant(4),
    )(*parts)


def flips(mesh_shape, even, odd):
    terms, sectors = mesh_shape
    pairs = []
    for t in range(terms):
        for s in range(sectors):
            u = {"term": t, "sector": s}
            for axis, bit in odd if s & 1 else even:
                u[axis] ^= 1 << bit
            pairs.append((t * sectors + s, u["term"] * sectors + u["sector"]))
    return pairs


def rest_dims(terms):
    return [("term", bit) for bit in range(2, terms.bit_length() - 1)]


def shards(mesh_shape, psi_start, diagonal, left_ops, right_ops, pair_in, pair_out, pair_count):
    terms, sectors = mesh_shape
    b = psi_start.shape[1]
    cells = float(sectors * b * b)

    def swap(x, even, odd=None):
        return lax.ppermute(x, AXES, flips(mesh_shape, even, even if odd is None else odd))

    def dims_of(k):
        return [dim for i, dim in enumerate(DIMS) if (k >> (2 - i)) & 1]

    away = START_ORDER
    rest = rest_dims(terms)

    own = psi_start[0]
    rows = b // CHUNKS
    far = []
    for h in range(CHUNKS):
        far.append(swap(own[h * rows:(h + 1) * rows], [DIMS[0]]))
    beside = swap(own, [CORE])
    left, right, vec, diag = prepare(left_ops, right_ops, psi_start, diagonal)
    far[0], left, right, vec, diag = lax.optimization_barrier((far[0], left, right, vec, diag))
    pieces = [own, beside]
    for x in far:
        pieces += [x, swap(x, [CORE])]
    zero = jnp.zeros(TILE, F32)
    energies = []
    for sweep in range(ITERS):
        first = sweep == 0
        args = (cells, sectors, pair_in, pair_count)
        if first:
            early, late = ([pieces[i] for i in picked(half, len(pieces))] for half in range(2))
            early = inner(first, 0, *args, early, right)
            cat, inv = inner(first, 1, *args, late, right, early)
        else:
            cat, inv = inner(first, None, *args, pieces, right)
        rho = zero
        keeps, recvs = [], []
        for h in range(CHUNKS):
            send, keep, rho = outer(first, h, cells, sectors, pair_out, pair_count, pieces, (left, cat), inv, rho)
            keeps.append(keep)
            recvs.append(swap(send, [CORE]))
        first_dims, second, third = ([[DIMS[dim]] for dim in step] for step in zip(*ORDERS))
        for h in range(CHUNKS):
            extra = TILE[0] if h == CHUNKS - 1 else 0
            keeps[h], send = cut(keeps[h], recvs[h], extra, 2)
            recvs[h] = swap(send, *first_dims)
        both = [a + b for a, b in zip(second, third)]
        for h in range(CHUNKS):
            extra = TILE[0] if h == CHUNKS - 1 else 0
            slots = cut(keeps[h], recvs[h], extra, 4)
            parts = [slots[0]]
            for k, dims in ((3, both), (2, second), (1, third)):
                parts.append(swap(slots[k], *dims))
            keeps[h] = parts
        for number, step in enumerate(rest):
            for h in range(CHUNKS):
                keeps[h] = sum_of([keeps[h], recvs[h]] if number else keeps[h])
                recvs[h] = swap(keeps[h], [step])
        sums = [x for pair in zip(keeps, recvs) for x in pair]
        vec, energy = update(sums, vec, inv, diag)
        energies.append(energy[0, 0])
        if sweep < ITERS - 1:
            got = {0: vec}
            zero = zero_tile(energy)
            for k in away:
                got[k] = swap(vec, dims_of(k))
            pieces = []
            for k in range(8):
                pieces += [got[k], swap(got[k], [CORE])]
    got = {k: swap(vec, dims_of(k)) for k in (3, 2, 1)}
    block = join([vec, got[1], got[2], got[3]])
    return block, jnp.stack(energies)


def solution(mesh):
    mesh_shape = (mesh.shape["term"], mesh.shape["sector"])
    return jax.shard_map(
        functools.partial(shards, mesh_shape),
        mesh=mesh,
        in_specs=(
            P("sector", None, None),
            P("sector", None, None),
            P(("term", "sector"), None, None),
            P(("term", "sector"), None, None),
            P(("term", "sector"), None),
            P(("term", "sector"), None),
            P(("term", "sector")),
        ),
        out_specs=(P("sector", None, None), P()),
        check_vma=False,
    )
```

```python
import functools

import jax
import jax.numpy as jnp
from jax import lax
from jax.experimental import pallas as pl
from jax.experimental.pallas import tpu as pltpu
from jax.sharding import PartitionSpec as P


ITERS = 2
AXES = ("term", "sector")
TILE = (8, 128)
CHUNKS = 2

epsilon = 1e-06


VMEM = pl.BlockSpec(memory_space=pltpu.VMEM)
SMEM = pl.BlockSpec(memory_space=pltpu.SMEM)
F32 = jnp.float32
BF16 = jnp.bfloat16

DIMS = (("sector", 1), ("term", 0), ("term", 1))
CORE = ("sector", 0)
ORDERS = (((0, 1, 2), (2, 1, 0)), ((1, 0, 2), (1, 0, 2)))
START_ORDER = (4, 2, 1, 6, 5, 3, 7)


def matmul_cost(pairs, rows, b):
    return pl.CostEstimate(
        flops=6 * pairs * rows * b * b, bytes_accessed=8 * pairs * b * b, transcendentals=0
    )


def grant(mib):
    return pltpu.CompilerParams(vmem_limit_bytes=mib << 20)


def chunks_of(size):
    return ((0, size // 3 * 2), (size // 3 * 2, size // 3))


def bit_of(axis, bit):
    return (lax.axis_index(axis) >> bit) & 1


def place(bits, parity, rows):
    return 2 * bits[0] + parity, pl.multiple_of((2 * bits[1] + bits[2]) * rows, 8)


def piece_place(k, parity, rows):
    return place([bit_of(*dim) ^ ((k >> (2 - i)) & 1) for i, dim in enumerate(DIMS)], parity, rows)


def slot_of(chunk, parity, masks):
    a, b = (sum(masks[dim] << (2 - i) for i, dim in enumerate(order)) for order in ORDERS[chunk])
    return jnp.where(parity == 0, a, b)


def split(x):
    high = x.astype(BF16)
    return high, (x - high.astype(F32)).astype(BF16)


def segments(first, b):
    me = lax.axis_index("sector")
    whole, shard = chunks_of(b), chunks_of(b // 4)
    if first:
        out = [[(h, me ^ side, start, 0, size) for h, (start, size) in enumerate(whole)] for side in range(2)]
        out += [[(h, me ^ (2 + side), 0, 0, size)] for h, (_, size) in enumerate(whole) for side in range(2)]
        return out
    out = []
    for number in range(16):
        parity = (me & 1) ^ (number & 1)
        out.append([(h, *rows_of(number >> 1, parity, start, size)) for h, (start, size) in enumerate(shard)])
    return out


def rows_of(k, parity, start, size):
    sector, row = piece_place(k, parity, size)
    return sector, start, row, size


def each_chunk(k, b):
    for (whole, _), (start, size) in zip(chunks_of(b), chunks_of(b // 4)):
        _, row = piece_place(k, 0, size)
        yield slice(start, start + size), pl.ds(pl.multiple_of(row + whole, 8), size)


def prep_kernel(left_ref, right_ref, psi_ref, diag_ref, left_cat, right_cat, vec_ref, mine_ref):
    b = left_ref.shape[-1]

    def one(p, carry):
        high, low = split(left_ref[p])
        for place, x in enumerate((high, low, high)):
            left_cat[p, :, place * b:(place + 1) * b] = x
        high, low = split(right_ref[p])
        for place, x in enumerate((high, high, low)):
            right_cat[p, :, place * b:(place + 1) * b] = x
        return carry

    lax.fori_loop(0, left_ref.shape[0], one, 0)
    for here, there in each_chunk(0, b):
        vec_ref[here, :] = psi_ref[0, there, :]
        mine_ref[here, :] = diag_ref[0, there, :]


def prepare(left_ops, right_ops, psi, diag):
    pairs, b, _ = left_ops.shape
    shard = jax.ShapeDtypeStruct((b // 4, b), F32)
    return pl.pallas_call(
        prep_kernel,
        in_specs=[VMEM] * 4,
        out_specs=[VMEM] * 4,
        out_shape=[jax.ShapeDtypeStruct((pairs, b, 3 * b), BF16)] * 2 + [shard] * 2,
        compiler_params=grant(16),
        cost_estimate=pl.CostEstimate(
            flops=4 * left_ops.size, bytes_accessed=20 * left_ops.size, transcendentals=0
        ),
    )(left_ops, right_ops, psi, diag)


def store_wide(dest, start, x):
    rows = x.shape[0]
    for c in range(x.shape[1] // TILE[1]):
        dest[pl.ds(start + c * rows, rows), :] = x[:, c * TILE[1]:(c + 1) * TILE[1]]


DOT_NT = functools.partial(
    lax.dot_general, dimension_numbers=(((1,), (1,)), ((), ())), preferred_element_type=F32
)
DOT = functools.partial(jnp.dot, preferred_element_type=F32)


def inner_kernel(first, half, cells, pieces, *refs):
    in_ref, count_ref, *refs = refs
    parts = refs[:pieces]
    refs = refs[pieces:]
    if half == 0:
        right, early_h, early_l, squares_ref, vec = refs
    elif half == 1:
        right, early_h, early_l, squares_ref, cat_ref, inv_ref, vec = refs
    else:
        right, cat_ref, inv_ref, vec = refs
    b = right.shape[1]
    whole = chunks_of(b)
    total = jnp.zeros((1, b), F32)
    cuts_of = segments(first, b)
    for piece, cuts in zip(parts, [cuts_of[i] for i in picked(half, len(cuts_of))]):
        for chunk, sector, start, row, size in cuts:
            if half is not None and chunk != half:
                continue
            x = piece[start:start + size, :]
            high, low = split(x)
            total += jnp.sum(x * x, axis=0, keepdims=True)
            if half is None:
                row = pl.multiple_of(row + whole[chunk][0], 16)
            at = pl.ds(row, size)
            for place, y in enumerate((high, low, high)):
                vec[sector, at, place * b:(place + 1) * b] = y
    total = jnp.broadcast_to(jnp.sum(total, axis=1, keepdims=True), (TILE[0], b))
    if half == 0:
        squares_ref[...] = total
    else:
        if half == 1:
            total += squares_ref[...]
        inv_ref[...] = lax.rsqrt(total / cells + epsilon)

    def one_pair(p, carry):
        high, low = split(DOT_NT(vec[in_ref[0, p]], right[p]))
        if half == 0:
            early_h[p], early_l[p] = high, low
            return carry
        moves = [(high, low, 0)] if half is None else [(early_h[p], early_l[p], 0), (high, low, whole[1][0])]
        for h, l, row in moves:
            for place, y in enumerate((h, h, l)):
                cat_ref[p, place * b + row:place * b + row + h.shape[0], :] = y
        return carry

    lax.fori_loop(0, count_ref[0], one_pair, 0)


def picked(half, pieces):
    return list(range(pieces)) if half is None else [0, 1, 2 + 2 * half, 3 + 2 * half]


def inner(first, half, cells, sectors, pair_in, pair_count, pieces, right, early=()):
    pairs, b, _ = right.shape
    rows = b if half is None else chunks_of(b)[half][1]
    compact = jax.ShapeDtypeStruct((pairs, rows, b), BF16)
    row = jax.ShapeDtypeStruct((TILE[0], b), F32)
    shapes = [compact, compact, row] if half == 0 else [jax.ShapeDtypeStruct((pairs, 3 * b, b), BF16), row]
    return pl.pallas_call(
        functools.partial(inner_kernel, first, half, cells, len(pieces)),
        in_specs=[SMEM] * 2 + [VMEM] * (len(pieces) + 1 + len(early)),
        out_specs=[VMEM] * len(shapes),
        out_shape=shapes,
        scratch_shapes=[pltpu.VMEM((sectors, rows, 3 * b), BF16)],
        compiler_params=grant(16),
        cost_estimate=matmul_cost(pairs, rows, b),
    )(pair_in, pair_count, *pieces, right, *early)


def outer_kernel(first, chunk, cells, pieces, *refs):
    out_ref, count_ref, *refs = refs
    parts = refs[:pieces]
    left, cat, inv_ref, before_ref, send_ref, keep_ref, rho_ref, acc = refs[pieces:]
    _, rows, b = acc.shape
    shard = rows // 4
    core = lax.axis_index("sector") & 1
    acc[...] = jnp.zeros_like(acc)
    first_row = chunks_of(b)[chunk][0]
    here = slice(first_row, first_row + rows)

    def one_pair(p, carry):
        target = out_ref[0, p]
        acc[target] += DOT(left[p, here, :], cat[p])
        return carry

    lax.fori_loop(0, count_ref[0], one_pair, 0)
    scale = inv_ref[:1, :]
    rho = jnp.zeros((1, b), F32)
    wide = shard * b // TILE[1]
    for number, (piece, cuts) in enumerate(zip(parts, segments(first, b))):
        side = number & 1
        dest = send_ref if side else keep_ref
        for at, sector, start, row, size in cuts:
            if at != chunk:
                continue
            for q in range(size // shard):
                if first:
                    masks = (int(number > 1), (q >> 1) ^ bit_of(*DIMS[1]), (q & 1) ^ bit_of(*DIMS[2]))
                    here = pl.ds(q * shard, shard)
                else:
                    masks = tuple((number >> (3 - i)) & 1 for i in range(3))
                    here = pl.ds(row, shard)
                x = acc[sector, here, :] * scale
                slot = slot_of(chunk, core ^ side, masks)
                store_wide(dest, pl.multiple_of(slot * wide, 8), x)
                rho += jnp.sum(x * piece[start + q * shard:start + (q + 1) * shard, :], axis=0, keepdims=True)
    rho = jnp.broadcast_to(jnp.sum(rho * scale, axis=1, keepdims=True), TILE) / cells + before_ref[...]
    rho_ref[...] = rho
    if chunk == CHUNKS - 1:
        send_ref[8 * wide:, :] = rho
        keep_ref[8 * wide:, :] = rho


def outer(first, chunk, cells, sectors, pair_out, pair_count, pieces, ops, inv, before):
    pairs, _, b = ops[1].shape
    rows = chunks_of(b)[chunk][1]
    extra = TILE[0] if chunk == CHUNKS - 1 else 0
    half = jax.ShapeDtypeStruct((sectors * rows // 2 * b // TILE[1] + extra, TILE[1]), F32)
    return pl.pallas_call(
        functools.partial(outer_kernel, first, chunk, cells, len(pieces)),
        in_specs=[SMEM] * 2 + [VMEM] * (len(pieces) + 4),
        out_specs=[VMEM] * 3,
        out_shape=[half, half, jax.ShapeDtypeStruct(TILE, F32)],
        scratch_shapes=[pltpu.VMEM((sectors, rows, b), F32)],
        compiler_params=grant(20),
        cost_estimate=matmul_cost(pairs, rows, b),
    )(pair_out, pair_count, *pieces, *ops, inv, before)


def cut_kernel(extra, keep_ref, recv_ref, *slots):
    rows = slots[0].shape[0] - extra
    end = len(slots) * rows
    for k, slot in enumerate(slots):
        slot[:rows, :] = keep_ref[k * rows:(k + 1) * rows, :] + recv_ref[k * rows:(k + 1) * rows, :]
        if extra:
            slot[rows:, :] = keep_ref[end:, :] + recv_ref[end:, :]


def cut(keep, recv, extra, ways):
    shape = jax.ShapeDtypeStruct(((recv.shape[0] - extra) // ways + extra, TILE[1]), F32)
    return pl.pallas_call(
        functools.partial(cut_kernel, extra),
        in_specs=[VMEM] * 2,
        out_specs=[VMEM] * ways,
        out_shape=[shape] * ways,
        compiler_params=grant(4),
    )(keep, recv)


def sum_kernel(*refs):
    *parts, out_ref = refs
    total = parts[0][...]
    for part in parts[1:]:
        total += part[...]
    out_ref[...] = total


def sum_of(parts):
    return pl.pallas_call(
        sum_kernel,
        in_specs=[VMEM] * len(parts),
        out_specs=VMEM,
        out_shape=jax.ShapeDtypeStruct(parts[0].shape, F32),
        compiler_params=grant(4),
    )(*parts)


def update_kernel(*refs):
    sums, (vec_ref, inv_ref, diag_ref, new_ref, energy_ref) = refs[:2 * CHUNKS], refs[2 * CHUNKS:]
    rows, b = new_ref.shape
    end = sums[-1].shape[0] - TILE[0]
    rho = sums[-2][end:, :] + sums[-1][end:, :]
    energy_ref[...] = rho
    for h, (start, size) in enumerate(chunks_of(rows)):
        mine_ref, recv_ref = sums[2 * h:2 * h + 2]
        at = slice(start, start + size)
        for c in range(b // TILE[1]):
            part = slice(c * size, (c + 1) * size)
            lanes = slice(c * TILE[1], (c + 1) * TILE[1])
            normed = vec_ref[at, lanes] * inv_ref[:1, lanes]
            sigma = mine_ref[part, :] + recv_ref[part, :]
            residual = sigma - rho[:1, :] * normed
            gap = jnp.maximum(jnp.abs(diag_ref[at, lanes] - rho[:1, :]), 1.0)
            new_ref[at, lanes] = normed - residual / gap


def update(sums, vec, inv, diag):
    return pl.pallas_call(
        update_kernel,
        in_specs=[VMEM] * (len(sums) + 3),
        out_specs=[VMEM] * 2,
        out_shape=[jax.ShapeDtypeStruct(vec.shape, F32), jax.ShapeDtypeStruct(TILE, F32)],
        compiler_params=grant(4),
    )(*sums, vec, inv, diag)


def zero_tile(tile):
    def kernel(in_ref, out_ref):
        out_ref[...] = jnp.zeros_like(out_ref)

    return pl.pallas_call(
        kernel, in_specs=[VMEM], out_specs=VMEM, out_shape=jax.ShapeDtypeStruct(TILE, F32), compiler_params=grant(4)
    )(tile)


def join_kernel(*refs):
    *parts, out_ref = refs
    for k, part in enumerate(parts):
        for here, there in each_chunk(k, out_ref.shape[-1]):
            out_ref[0, there, :] = part[here, :]


def join(parts):
    quarter, b = parts[0].shape
    return pl.pallas_call(
        join_kernel,
        in_specs=[VMEM] * len(parts),
        out_specs=VMEM,
        out_shape=jax.ShapeDtypeStruct((1, 4 * quarter, b), F32),
        compiler_params=grant(4),
    )(*parts)


def flips(mesh_shape, even, odd):
    terms, sectors = mesh_shape
    pairs = []
    for t in range(terms):
        for s in range(sectors):
            u = {"term": t, "sector": s}
            for axis, bit in odd if s & 1 else even:
                u[axis] ^= 1 << bit
            pairs.append((t * sectors + s, u["term"] * sectors + u["sector"]))
    return pairs


def rest_dims(terms):
    return [("term", bit) for bit in range(2, terms.bit_length() - 1)]


def shards(mesh_shape, psi_start, diagonal, left_ops, right_ops, pair_in, pair_out, pair_count):
    terms, sectors = mesh_shape
    b = psi_start.shape[1]
    cells = float(sectors * b * b)

    def swap(x, even, odd=None):
        return lax.ppermute(x, AXES, flips(mesh_shape, even, even if odd is None else odd))

    def dims_of(k):
        return [dim for i, dim in enumerate(DIMS) if (k >> (2 - i)) & 1]

    away = START_ORDER
    rest = rest_dims(terms)

    own = psi_start[0]
    far = []
    for start, size in chunks_of(b):
        far.append(swap(own[start:start + size], [DIMS[0]]))
    beside = swap(own, [CORE])
    left, right, vec, diag = prepare(left_ops, right_ops, psi_start, diagonal)
    far[0], left, right, vec, diag = lax.optimization_barrier((far[0], left, right, vec, diag))
    pieces = [own, beside]
    for x in far:
        pieces += [x, swap(x, [CORE])]
    zero = jnp.zeros(TILE, F32)
    energies = []
    for sweep in range(ITERS):
        first = sweep == 0
        args = (cells, sectors, pair_in, pair_count)
        if first:
            early, late = ([pieces[i] for i in picked(half, len(pieces))] for half in range(2))
            early = inner(first, 0, *args, early, right)
            cat, inv = inner(first, 1, *args, late, right, early)
        else:
            cat, inv = inner(first, None, *args, pieces, right)
        rho = zero
        keeps, recvs = [], []
        for h in range(CHUNKS):
            send, keep, rho = outer(first, h, cells, sectors, pair_out, pair_count, pieces, (left, cat), inv, rho)
            keeps.append(keep)
            recvs.append(swap(send, [CORE]))
        orders = [[[[DIMS[dim]] for dim in step] for step in zip(*order)] for order in ORDERS]
        for h in range(CHUNKS):
            extra = TILE[0] if h == CHUNKS - 1 else 0
            keeps[h], send = cut(keeps[h], recvs[h], extra, 2)
            recvs[h] = swap(send, *orders[h][0])
        for h in range(CHUNKS):
            extra = TILE[0] if h == CHUNKS - 1 else 0
            slots = cut(keeps[h], recvs[h], extra, 4)
            parts = [slots[0]]
            _, second, third = orders[h]
            both = [a + b for a, b in zip(second, third)]
            for k, dims in ((3, both), (2, second), (1, third)):
                parts.append(swap(slots[k], *dims))
            keeps[h] = parts
        for number, step in enumerate(rest):
            for h in range(CHUNKS):
                keeps[h] = sum_of([keeps[h], recvs[h]] if number else keeps[h])
                recvs[h] = swap(keeps[h], [step])
        sums = [x for pair in zip(keeps, recvs) for x in pair]
        vec, energy = update(sums, vec, inv, diag)
        energies.append(energy[0, 0])
        if sweep < ITERS - 1:
            got = {0: vec}
            zero = zero_tile(energy)
            for k in away:
                got[k] = swap(vec, dims_of(k))
            pieces = []
            for k in range(8):
                pieces += [got[k], swap(got[k], [CORE])]
    got = {k: swap(vec, dims_of(k)) for k in (3, 2, 1)}
    block = join([vec, got[1], got[2], got[3]])
    return block, jnp.stack(energies)


def solution(mesh):
    mesh_shape = (mesh.shape["term"], mesh.shape["sector"])
    return jax.shard_map(
        functools.partial(shards, mesh_shape),
        mesh=mesh,
        in_specs=(
            P("sector", None, None),
            P("sector", None, None),
            P(("term", "sector"), None, None),
            P(("term", "sector"), None, None),
            P(("term", "sector"), None),
            P(("term", "sector"), None),
            P(("term", "sector")),
        ),
        out_specs=(P("sector", None, None), P()),
        check_vma=False,
    )
```

```python
import functools

import jax
import jax.numpy as jnp
from jax import lax
from jax.experimental import pallas as pl
from jax.experimental.pallas import tpu as pltpu
from jax.sharding import PartitionSpec as P


ITERS = 2
AXES = ("term", "sector")
TILE = (8, 128)
CHUNKS = 2

epsilon = 1e-06


VMEM = pl.BlockSpec(memory_space=pltpu.VMEM)
SMEM = pl.BlockSpec(memory_space=pltpu.SMEM)
F32 = jnp.float32
BF16 = jnp.bfloat16

DIMS = (("sector", 1), ("term", 0), ("term", 1))
CORE = ("sector", 0)
ORDERS = ((0, 1, 2), (2, 1, 0))
START_ORDER = (6, 5, 4, 2, 1, 3)


def matmul_cost(pairs, rows, b):
    return pl.CostEstimate(
        flops=6 * pairs * rows * b * b, bytes_accessed=8 * pairs * b * b, transcendentals=0
    )


def grant(mib):
    return pltpu.CompilerParams(vmem_limit_bytes=mib << 20)


def bit_of(axis, bit):
    return (lax.axis_index(axis) >> bit) & 1


def place(bits, parity, rows):
    return 2 * bits[0] + parity, pl.multiple_of((2 * bits[1] + bits[2]) * rows, 8)


def piece_place(k, parity, rows):
    return place([bit_of(*dim) ^ ((k >> (2 - i)) & 1) for i, dim in enumerate(DIMS)], parity, rows)


def slot_of(parity, masks):
    a, b = (sum(masks[dim] << (2 - i) for i, dim in enumerate(order)) for order in ORDERS)
    return jnp.where(parity == 0, a, b)


def split(x):
    high = x.astype(BF16)
    return high, (x - high.astype(F32)).astype(BF16)


def segments(first, rows, shard):
    me = lax.axis_index("sector")
    if first:
        out = [[(h, me ^ side, h * rows, 0, rows) for h in range(CHUNKS)] for side in range(2)]
        out += [[(h, me ^ (2 + side), 0, 0, rows)] for h in range(CHUNKS) for side in range(2)]
        return out
    out = []
    for number in range(16):
        sector, row = piece_place(number >> 1, (me & 1) ^ (number & 1), shard)
        out.append([(h, sector, h * shard, row, shard) for h in range(CHUNKS)])
    return out


def prep_kernel(left_ref, right_ref, psi_ref, diag_ref, left_cat, right_cat, vec_ref, mine_ref):
    b = left_ref.shape[-1]

    def one(p, carry):
        high, low = split(left_ref[p])
        for place, x in enumerate((high, low, high)):
            left_cat[p, :, place * b:(place + 1) * b] = x
        high, low = split(right_ref[p])
        for place, x in enumerate((high, high, low)):
            right_cat[p, :, place * b:(place + 1) * b] = x
        return carry

    lax.fori_loop(0, left_ref.shape[0], one, 0)
    rows = vec_ref.shape[0] // CHUNKS
    for h in range(CHUNKS):
        _, row = piece_place(0, 0, rows)
        at = pl.ds(pl.multiple_of(row + h * 4 * rows, 8), rows)
        vec_ref[h * rows:(h + 1) * rows, :] = psi_ref[0, at, :]
        mine_ref[h * rows:(h + 1) * rows, :] = diag_ref[0, at, :]


def prepare(left_ops, right_ops, psi, diag):
    pairs, b, _ = left_ops.shape
    shard = jax.ShapeDtypeStruct((b // 4, b), F32)
    return pl.pallas_call(
        prep_kernel,
        in_specs=[VMEM] * 4,
        out_specs=[VMEM] * 4,
        out_shape=[jax.ShapeDtypeStruct((pairs, b, 3 * b), BF16)] * 2 + [shard] * 2,
        compiler_params=grant(16),
        cost_estimate=pl.CostEstimate(
            flops=4 * left_ops.size, bytes_accessed=20 * left_ops.size, transcendentals=0
        ),
    )(left_ops, right_ops, psi, diag)


def store_wide(dest, start, x):
    rows = x.shape[0]
    for c in range(x.shape[1] // TILE[1]):
        dest[pl.ds(start + c * rows, rows), :] = x[:, c * TILE[1]:(c + 1) * TILE[1]]


DOT_NT = functools.partial(
    lax.dot_general, dimension_numbers=(((1,), (1,)), ((), ())), preferred_element_type=F32
)
DOT = functools.partial(jnp.dot, preferred_element_type=F32)


def inner_kernel(first, half, cells, pieces, *refs):
    in_ref, count_ref, *refs = refs
    parts = refs[:pieces]
    refs = refs[pieces:]
    if half == 0:
        right, early_h, early_l, squares_ref, vec = refs
    elif half == 1:
        right, early_h, early_l, squares_ref, cat_ref, inv_ref, vec = refs
    else:
        right, cat_ref, inv_ref, vec = refs
    b = right.shape[1]
    rows = b // CHUNKS
    shard = rows // 4
    total = jnp.zeros((1, b), F32)
    cuts_of = segments(first, rows, shard)
    for piece, cuts in zip(parts, [cuts_of[i] for i in picked(half, len(cuts_of))]):
        for chunk, sector, start, row, size in cuts:
            if half is not None and chunk != half:
                continue
            x = piece[start:start + size, :]
            high, low = split(x)
            total += jnp.sum(x * x, axis=0, keepdims=True)
            if half is None:
                row = pl.multiple_of(row + chunk * rows, 16)
            at = pl.ds(row, size)
            for place, y in enumerate((high, low, high)):
                vec[sector, at, place * b:(place + 1) * b] = y
    total = jnp.broadcast_to(jnp.sum(total, axis=1, keepdims=True), (TILE[0], b))
    if half == 0:
        squares_ref[...] = total
    else:
        if half == 1:
            total += squares_ref[...]
        inv_ref[...] = lax.rsqrt(total / cells + epsilon)

    def one_pair(p, carry):
        high, low = split(DOT_NT(vec[in_ref[0, p]], right[p]))
        if half == 0:
            early_h[p], early_l[p] = high, low
            return carry
        moves = [(high, low, 0)] if half is None else [(early_h[p], early_l[p], 0), (high, low, rows)]
        for h, l, row in moves:
            for place, y in enumerate((h, h, l)):
                cat_ref[p, place * b + row:place * b + row + h.shape[0], :] = y
        return carry

    lax.fori_loop(0, count_ref[0], one_pair, 0)


def picked(half, pieces):
    return list(range(pieces)) if half is None else [0, 1, 2 + 2 * half, 3 + 2 * half]


def inner(first, half, cells, sectors, pair_in, pair_count, pieces, right, early=()):
    pairs, b, _ = right.shape
    rows = b if half is None else b // CHUNKS
    compact = jax.ShapeDtypeStruct((pairs, rows, b), BF16)
    row = jax.ShapeDtypeStruct((TILE[0], b), F32)
    shapes = [compact, compact, row] if half == 0 else [jax.ShapeDtypeStruct((pairs, 3 * b, b), BF16), row]
    return pl.pallas_call(
        functools.partial(inner_kernel, first, half, cells, len(pieces)),
        in_specs=[SMEM] * 2 + [VMEM] * (len(pieces) + 1 + len(early)),
        out_specs=[VMEM] * len(shapes),
        out_shape=shapes,
        scratch_shapes=[pltpu.VMEM((sectors, rows, 3 * b), BF16)],
        compiler_params=grant(16),
        cost_estimate=matmul_cost(pairs, rows, b),
    )(pair_in, pair_count, *pieces, right, *early)


def outer_kernel(first, chunk, cells, pieces, *refs):
    out_ref, count_ref, *refs = refs
    parts = refs[:pieces]
    left, cat, inv_ref, before_ref, send_ref, keep_ref, rho_ref, acc = refs[pieces:]
    _, rows, b = acc.shape
    shard = rows // 4
    core = lax.axis_index("sector") & 1
    acc[...] = jnp.zeros_like(acc)
    here = slice(chunk * rows, (chunk + 1) * rows)

    def one_pair(p, carry):
        target = out_ref[0, p]
        acc[target] += DOT(left[p, here, :], cat[p])
        return carry

    lax.fori_loop(0, count_ref[0], one_pair, 0)
    scale = inv_ref[:1, :]
    rho = jnp.zeros((1, b), F32)
    wide = shard * b // TILE[1]
    for number, (piece, cuts) in enumerate(zip(parts, segments(first, rows, shard))):
        side = number & 1
        dest = send_ref if side else keep_ref
        for at, sector, start, row, size in cuts:
            if at != chunk:
                continue
            for q in range(size // shard):
                if first:
                    masks = (int(number > 1), (q >> 1) ^ bit_of(*DIMS[1]), (q & 1) ^ bit_of(*DIMS[2]))
                    here = pl.ds(q * shard, shard)
                else:
                    masks = tuple((number >> (3 - i)) & 1 for i in range(3))
                    here = pl.ds(row, shard)
                x = acc[sector, here, :] * scale
                slot = slot_of(core ^ side, masks)
                store_wide(dest, pl.multiple_of(slot * wide, 8), x)
                rho += jnp.sum(x * piece[start + q * shard:start + (q + 1) * shard, :], axis=0, keepdims=True)
    rho = jnp.broadcast_to(jnp.sum(rho * scale, axis=1, keepdims=True), TILE) / cells + before_ref[...]
    rho_ref[...] = rho
    if chunk == CHUNKS - 1:
        send_ref[8 * wide:, :] = rho
        keep_ref[8 * wide:, :] = rho


def outer(first, chunk, cells, sectors, pair_out, pair_count, pieces, ops, inv, before):
    pairs, _, b = ops[1].shape
    rows = b // CHUNKS
    extra = TILE[0] if chunk == CHUNKS - 1 else 0
    half = jax.ShapeDtypeStruct((sectors * rows // 2 * b // TILE[1] + extra, TILE[1]), F32)
    return pl.pallas_call(
        functools.partial(outer_kernel, first, chunk, cells, len(pieces)),
        in_specs=[SMEM] * 2 + [VMEM] * (len(pieces) + 4),
        out_specs=[VMEM] * 3,
        out_shape=[half, half, jax.ShapeDtypeStruct(TILE, F32)],
        scratch_shapes=[pltpu.VMEM((sectors, rows, b), F32)],
        compiler_params=grant(20),
        cost_estimate=matmul_cost(pairs, rows, b),
    )(pair_out, pair_count, *pieces, *ops, inv, before)


def cut_kernel(extra, keep_ref, recv_ref, *slots):
    rows = slots[0].shape[0] - extra
    end = len(slots) * rows
    for k, slot in enumerate(slots):
        slot[:rows, :] = keep_ref[k * rows:(k + 1) * rows, :] + recv_ref[k * rows:(k + 1) * rows, :]
        if extra:
            slot[rows:, :] = keep_ref[end:, :] + recv_ref[end:, :]


def cut(keep, recv, extra, ways):
    shape = jax.ShapeDtypeStruct(((recv.shape[0] - extra) // ways + extra, TILE[1]), F32)
    return pl.pallas_call(
        functools.partial(cut_kernel, extra),
        in_specs=[VMEM] * 2,
        out_specs=[VMEM] * ways,
        out_shape=[shape] * ways,
        compiler_params=grant(4),
    )(keep, recv)


def sum_kernel(*refs):
    *parts, out_ref = refs
    total = parts[0][...]
    for part in parts[1:]:
        total += part[...]
    out_ref[...] = total


def sum_of(parts):
    return pl.pallas_call(
        sum_kernel,
        in_specs=[VMEM] * len(parts),
        out_specs=VMEM,
        out_shape=jax.ShapeDtypeStruct(parts[0].shape, F32),
        compiler_params=grant(4),
    )(*parts)


def pick_kernel(even_ref, odd_ref, out_ref):
    out_ref[...] = jnp.where(bit_of(*CORE) == 0, even_ref[...], odd_ref[...])


def pick(even, odd):
    return pl.pallas_call(
        pick_kernel,
        in_specs=[VMEM] * 2,
        out_specs=VMEM,
        out_shape=jax.ShapeDtypeStruct(even.shape, F32),
        compiler_params=grant(4),
    )(even, odd)


def update_kernel(*refs):
    sums, (vec_ref, inv_ref, diag_ref, new_ref, energy_ref) = refs[:2 * CHUNKS], refs[2 * CHUNKS:]
    rows, b = new_ref.shape
    shard = rows // CHUNKS
    end = shard * b // TILE[1]
    rho = sums[-2][end:, :] + sums[-1][end:, :]
    energy_ref[...] = rho
    for h in range(CHUNKS):
        mine_ref, recv_ref = sums[2 * h:2 * h + 2]
        at = slice(h * shard, (h + 1) * shard)
        for c in range(b // TILE[1]):
            part = slice(c * shard, (c + 1) * shard)
            lanes = slice(c * TILE[1], (c + 1) * TILE[1])
            normed = vec_ref[at, lanes] * inv_ref[:1, lanes]
            sigma = mine_ref[part, :] + recv_ref[part, :]
            residual = sigma - rho[:1, :] * normed
            gap = jnp.maximum(jnp.abs(diag_ref[at, lanes] - rho[:1, :]), 1.0)
            new_ref[at, lanes] = normed - residual / gap


def update(sums, vec, inv, diag):
    return pl.pallas_call(
        update_kernel,
        in_specs=[VMEM] * (len(sums) + 3),
        out_specs=[VMEM] * 2,
        out_shape=[jax.ShapeDtypeStruct(vec.shape, F32), jax.ShapeDtypeStruct(TILE, F32)],
        compiler_params=grant(4),
    )(*sums, vec, inv, diag)


def zero_tile(tile):
    def kernel(in_ref, out_ref):
        out_ref[...] = jnp.zeros_like(out_ref)

    return pl.pallas_call(
        kernel, in_specs=[VMEM], out_specs=VMEM, out_shape=jax.ShapeDtypeStruct(TILE, F32), compiler_params=grant(4)
    )(tile)


def join_kernel(*refs):
    *parts, out_ref = refs
    rows = parts[0].shape[0] // CHUNKS
    for k, part in enumerate(parts):
        _, row = piece_place(k, 0, rows)
        for h in range(CHUNKS):
            at = pl.ds(pl.multiple_of(row + h * 4 * rows, 8), rows)
            out_ref[0, at, :] = part[h * rows:(h + 1) * rows, :]


def join(parts):
    quarter, b = parts[0].shape
    return pl.pallas_call(
        join_kernel,
        in_specs=[VMEM] * len(parts),
        out_specs=VMEM,
        out_shape=jax.ShapeDtypeStruct((1, 4 * quarter, b), F32),
        compiler_params=grant(4),
    )(*parts)


def flips(mesh_shape, even, odd):
    terms, sectors = mesh_shape
    pairs = []
    for t in range(terms):
        for s in range(sectors):
            u = {"term": t, "sector": s}
            for axis, bit in odd if s & 1 else even:
                u[axis] ^= 1 << bit
            pairs.append((t * sectors + s, u["term"] * sectors + u["sector"]))
    return pairs


def rest_dims(terms):
    return [("term", bit) for bit in range(2, terms.bit_length() - 1)]


def shards(mesh_shape, psi_start, diagonal, left_ops, right_ops, pair_in, pair_out, pair_count):
    terms, sectors = mesh_shape
    b = psi_start.shape[1]
    cells = float(sectors * b * b)

    def swap(x, even, odd=None):
        return lax.ppermute(x, AXES, flips(mesh_shape, even, even if odd is None else odd))

    def dims_of(k):
        return [dim for i, dim in enumerate(DIMS) if (k >> (2 - i)) & 1]

    away = START_ORDER
    rest = rest_dims(terms)

    own = psi_start[0]
    rows = b // CHUNKS
    far = []
    for h in range(CHUNKS):
        far.append(swap(own[h * rows:(h + 1) * rows], [DIMS[0]]))
    beside = swap(own, [CORE])
    left, right, vec, diag = prepare(left_ops, right_ops, psi_start, diagonal)
    far[0], left, right, vec, diag = lax.optimization_barrier((far[0], left, right, vec, diag))
    pieces = [own, beside]
    for x in far:
        pieces += [x, swap(x, [CORE])]
    zero = jnp.zeros(TILE, F32)
    energies = []
    for sweep in range(ITERS):
        first = sweep == 0
        args = (cells, sectors, pair_in, pair_count)
        if first:
            early, late = ([pieces[i] for i in picked(half, len(pieces))] for half in range(2))
            early = inner(first, 0, *args, early, right)
            cat, inv = inner(first, 1, *args, late, right, early)
        else:
            cat, inv = inner(first, None, *args, pieces, right)
        rho = zero
        keeps, recvs = [], []
        for h in range(CHUNKS):
            send, keep, rho = outer(first, h, cells, sectors, pair_out, pair_count, pieces, (left, cat), inv, rho)
            keeps.append(keep)
            recvs.append(swap(send, [CORE]))
        first_dims, second, third = ([[DIMS[dim]] for dim in step] for step in zip(*ORDERS))
        for h in range(CHUNKS):
            extra = TILE[0] if h == CHUNKS - 1 else 0
            keeps[h], send = cut(keeps[h], recvs[h], extra, 2)
            recvs[h] = swap(send, *first_dims)
        both = [a + b for a, b in zip(second, third)]
        for h in range(CHUNKS):
            extra = TILE[0] if h == CHUNKS - 1 else 0
            slots = cut(keeps[h], recvs[h], extra, 4)
            parts = [slots[0]]
            for k, dims in ((3, both), (2, second), (1, third)):
                parts.append(swap(slots[k], *dims))
            keeps[h] = parts
        for number, step in enumerate(rest):
            for h in range(CHUNKS):
                keeps[h] = sum_of([keeps[h], recvs[h]] if number else keeps[h])
                recvs[h] = swap(keeps[h], [step])
        sums = [x for pair in zip(keeps, recvs) for x in pair]
        vec, energy = update(sums, vec, inv, diag)
        energies.append(energy[0, 0])
        if sweep < ITERS - 1:
            got = {0: vec}
            zero = zero_tile(energy)
            for k in away:
                got[k] = swap(vec, dims_of(k))
            near = pick(got[5], got[6])
            got[7] = swap(near, [DIMS[1]], [DIMS[2]])
            pieces = []
            for k in range(8):
                pieces += [got[k], swap(got[k], [CORE])]
    got = {k: swap(vec, dims_of(k)) for k in (3, 2, 1)}
    block = join([vec, got[1], got[2], got[3]])
    return block, jnp.stack(energies)


def solution(mesh):
    mesh_shape = (mesh.shape["term"], mesh.shape["sector"])
    return jax.shard_map(
        functools.partial(shards, mesh_shape),
        mesh=mesh,
        in_specs=(
            P("sector", None, None),
            P("sector", None, None),
            P(("term", "sector"), None, None),
            P(("term", "sector"), None, None),
            P(("term", "sector"), None),
            P(("term", "sector"), None),
            P(("term", "sector")),
        ),
        out_specs=(P("sector", None, None), P()),
        check_vma=False,
    )
```

```python
import functools

import jax
import jax.numpy as jnp
from jax import lax
from jax.experimental import pallas as pl
from jax.experimental.pallas import tpu as pltpu
from jax.sharding import PartitionSpec as P


ITERS = 2
AXES = ("term", "sector")
TILE = (8, 128)
CHUNKS = 2

epsilon = 1e-06


VMEM = pl.BlockSpec(memory_space=pltpu.VMEM)
SMEM = pl.BlockSpec(memory_space=pltpu.SMEM)
F32 = jnp.float32
BF16 = jnp.bfloat16

DIMS = (("sector", 1), ("term", 0), ("term", 1))
CORE = ("sector", 0)
ORDERS = (((0, 1, 2), (2, 1, 0)), ((1, 0, 2), (2, 1, 0)))
START_ORDER = (6, 5, 4, 2, 1, 3)


def matmul_cost(pairs, rows, b):
    return pl.CostEstimate(
        flops=6 * pairs * rows * b * b, bytes_accessed=8 * pairs * b * b, transcendentals=0
    )


def grant(mib):
    return pltpu.CompilerParams(vmem_limit_bytes=mib << 20)


def bit_of(axis, bit):
    return (lax.axis_index(axis) >> bit) & 1


def place(bits, parity, rows):
    return 2 * bits[0] + parity, pl.multiple_of((2 * bits[1] + bits[2]) * rows, 8)


def piece_place(k, parity, rows):
    return place([bit_of(*dim) ^ ((k >> (2 - i)) & 1) for i, dim in enumerate(DIMS)], parity, rows)


def slot_of(chunk, parity, masks):
    a, b = (sum(masks[dim] << (2 - i) for i, dim in enumerate(order)) for order in ORDERS[chunk])
    return jnp.where(parity == 0, a, b)


def split(x):
    high = x.astype(BF16)
    return high, (x - high.astype(F32)).astype(BF16)


def segments(first, rows, shard):
    me = lax.axis_index("sector")
    if first:
        out = [[(h, me ^ side, h * rows, 0, rows) for h in range(CHUNKS)] for side in range(2)]
        out += [[(h, me ^ (2 + side), 0, 0, rows)] for h in range(CHUNKS) for side in range(2)]
        return out
    out = []
    for number in range(16):
        sector, row = piece_place(number >> 1, (me & 1) ^ (number & 1), shard)
        out.append([(h, sector, h * shard, row, shard) for h in range(CHUNKS)])
    return out


def prep_kernel(left_ref, right_ref, psi_ref, diag_ref, left_cat, right_cat, vec_ref, mine_ref):
    b = left_ref.shape[-1]

    def one(p, carry):
        high, low = split(left_ref[p])
        for place, x in enumerate((high, low, high)):
            left_cat[p, :, place * b:(place + 1) * b] = x
        high, low = split(right_ref[p])
        for place, x in enumerate((high, high, low)):
            right_cat[p, :, place * b:(place + 1) * b] = x
        return carry

    lax.fori_loop(0, left_ref.shape[0], one, 0)
    rows = vec_ref.shape[0] // CHUNKS
    for h in range(CHUNKS):
        _, row = piece_place(0, 0, rows)
        at = pl.ds(pl.multiple_of(row + h * 4 * rows, 8), rows)
        vec_ref[h * rows:(h + 1) * rows, :] = psi_ref[0, at, :]
        mine_ref[h * rows:(h + 1) * rows, :] = diag_ref[0, at, :]


def prepare(left_ops, right_ops, psi, diag):
    pairs, b, _ = left_ops.shape
    shard = jax.ShapeDtypeStruct((b // 4, b), F32)
    return pl.pallas_call(
        prep_kernel,
        in_specs=[VMEM] * 4,
        out_specs=[VMEM] * 4,
        out_shape=[jax.ShapeDtypeStruct((pairs, b, 3 * b), BF16)] * 2 + [shard] * 2,
        compiler_params=grant(16),
        cost_estimate=pl.CostEstimate(
            flops=4 * left_ops.size, bytes_accessed=20 * left_ops.size, transcendentals=0
        ),
    )(left_ops, right_ops, psi, diag)


def store_wide(dest, start, x):
    rows = x.shape[0]
    for c in range(x.shape[1] // TILE[1]):
        dest[pl.ds(start + c * rows, rows), :] = x[:, c * TILE[1]:(c + 1) * TILE[1]]


DOT_NT = functools.partial(
    lax.dot_general, dimension_numbers=(((1,), (1,)), ((), ())), preferred_element_type=F32
)
DOT = functools.partial(jnp.dot, preferred_element_type=F32)


def inner_kernel(first, half, cells, pieces, *refs):
    in_ref, count_ref, *refs = refs
    parts = refs[:pieces]
    refs = refs[pieces:]
    if half == 0:
        right, early_h, early_l, squares_ref, vec = refs
    elif half == 1:
        right, early_h, early_l, squares_ref, cat_ref, inv_ref, vec = refs
    else:
        right, cat_ref, inv_ref, vec = refs
    b = right.shape[1]
    rows = b // CHUNKS
    shard = rows // 4
    total = jnp.zeros((1, b), F32)
    cuts_of = segments(first, rows, shard)
    for piece, cuts in zip(parts, [cuts_of[i] for i in picked(half, len(cuts_of))]):
        for chunk, sector, start, row, size in cuts:
            if half is not None and chunk != half:
                continue
            x = piece[start:start + size, :]
            high, low = split(x)
            total += jnp.sum(x * x, axis=0, keepdims=True)
            if half is None:
                row = pl.multiple_of(row + chunk * rows, 16)
            at = pl.ds(row, size)
            for place, y in enumerate((high, low, high)):
                vec[sector, at, place * b:(place + 1) * b] = y
    total = jnp.broadcast_to(jnp.sum(total, axis=1, keepdims=True), (TILE[0], b))
    if half == 0:
        squares_ref[...] = total
    else:
        if half == 1:
            total += squares_ref[...]
        inv_ref[...] = lax.rsqrt(total / cells + epsilon)

    def one_pair(p, carry):
        high, low = split(DOT_NT(vec[in_ref[0, p]], right[p]))
        if half == 0:
            early_h[p], early_l[p] = high, low
            return carry
        moves = [(high, low, 0)] if half is None else [(early_h[p], early_l[p], 0), (high, low, rows)]
        for h, l, row in moves:
            for place, y in enumerate((h, h, l)):
                cat_ref[p, place * b + row:place * b + row + h.shape[0], :] = y
        return carry

    lax.fori_loop(0, count_ref[0], one_pair, 0)


def picked(half, pieces):
    return list(range(pieces)) if half is None else [0, 1, 2 + 2 * half, 3 + 2 * half]


def inner(first, half, cells, sectors, pair_in, pair_count, pieces, right, early=()):
    pairs, b, _ = right.shape
    rows = b if half is None else b // CHUNKS
    compact = jax.ShapeDtypeStruct((pairs, rows, b), BF16)
    row = jax.ShapeDtypeStruct((TILE[0], b), F32)
    shapes = [compact, compact, row] if half == 0 else [jax.ShapeDtypeStruct((pairs, 3 * b, b), BF16), row]
    return pl.pallas_call(
        functools.partial(inner_kernel, first, half, cells, len(pieces)),
        in_specs=[SMEM] * 2 + [VMEM] * (len(pieces) + 1 + len(early)),
        out_specs=[VMEM] * len(shapes),
        out_shape=shapes,
        scratch_shapes=[pltpu.VMEM((sectors, rows, 3 * b), BF16)],
        compiler_params=grant(16),
        cost_estimate=matmul_cost(pairs, rows, b),
    )(pair_in, pair_count, *pieces, right, *early)


def outer_kernel(first, chunk, cells, pieces, *refs):
    out_ref, count_ref, *refs = refs
    parts = refs[:pieces]
    left, cat, inv_ref, before_ref, send_ref, keep_ref, rho_ref, acc = refs[pieces:]
    _, rows, b = acc.shape
    shard = rows // 4
    core = lax.axis_index("sector") & 1
    acc[...] = jnp.zeros_like(acc)
    here = slice(chunk * rows, (chunk + 1) * rows)

    def one_pair(p, carry):
        target = out_ref[0, p]
        acc[target] += DOT(left[p, here, :], cat[p])
        return carry

    lax.fori_loop(0, count_ref[0], one_pair, 0)
    scale = inv_ref[:1, :]
    rho = jnp.zeros((1, b), F32)
    wide = shard * b // TILE[1]
    for number, (piece, cuts) in enumerate(zip(parts, segments(first, rows, shard))):
        side = number & 1
        dest = send_ref if side else keep_ref
        for at, sector, start, row, size in cuts:
            if at != chunk:
                continue
            for q in range(size // shard):
                if first:
                    masks = (int(number > 1), (q >> 1) ^ bit_of(*DIMS[1]), (q & 1) ^ bit_of(*DIMS[2]))
                    here = pl.ds(q * shard, shard)
                else:
                    masks = tuple((number >> (3 - i)) & 1 for i in range(3))
                    here = pl.ds(row, shard)
                x = acc[sector, here, :] * scale
                slot = slot_of(chunk, core ^ side, masks)
                store_wide(dest, pl.multiple_of(slot * wide, 8), x)
                rho += jnp.sum(x * piece[start + q * shard:start + (q + 1) * shard, :], axis=0, keepdims=True)
    rho = jnp.broadcast_to(jnp.sum(rho * scale, axis=1, keepdims=True), TILE) / cells + before_ref[...]
    rho_ref[...] = rho
    if chunk == CHUNKS - 1:
        send_ref[8 * wide:, :] = rho
        keep_ref[8 * wide:, :] = rho


def outer(first, chunk, cells, sectors, pair_out, pair_count, pieces, ops, inv, before):
    pairs, _, b = ops[1].shape
    rows = b // CHUNKS
    extra = TILE[0] if chunk == CHUNKS - 1 else 0
    half = jax.ShapeDtypeStruct((sectors * rows // 2 * b // TILE[1] + extra, TILE[1]), F32)
    return pl.pallas_call(
        functools.partial(outer_kernel, first, chunk, cells, len(pieces)),
        in_specs=[SMEM] * 2 + [VMEM] * (len(pieces) + 4),
        out_specs=[VMEM] * 3,
        out_shape=[half, half, jax.ShapeDtypeStruct(TILE, F32)],
        scratch_shapes=[pltpu.VMEM((sectors, rows, b), F32)],
        compiler_params=grant(20),
        cost_estimate=matmul_cost(pairs, rows, b),
    )(pair_out, pair_count, *pieces, *ops, inv, before)


def cut_kernel(extra, keep_ref, recv_ref, *slots):
    rows = slots[0].shape[0] - extra
    end = len(slots) * rows
    for k, slot in enumerate(slots):
        slot[:rows, :] = keep_ref[k * rows:(k + 1) * rows, :] + recv_ref[k * rows:(k + 1) * rows, :]
        if extra:
            slot[rows:, :] = keep_ref[end:, :] + recv_ref[end:, :]


def cut(keep, recv, extra, ways):
    shape = jax.ShapeDtypeStruct(((recv.shape[0] - extra) // ways + extra, TILE[1]), F32)
    return pl.pallas_call(
        functools.partial(cut_kernel, extra),
        in_specs=[VMEM] * 2,
        out_specs=[VMEM] * ways,
        out_shape=[shape] * ways,
        compiler_params=grant(4),
    )(keep, recv)


def sum_kernel(*refs):
    *parts, out_ref = refs
    total = parts[0][...]
    for part in parts[1:]:
        total += part[...]
    out_ref[...] = total


def sum_of(parts):
    return pl.pallas_call(
        sum_kernel,
        in_specs=[VMEM] * len(parts),
        out_specs=VMEM,
        out_shape=jax.ShapeDtypeStruct(parts[0].shape, F32),
        compiler_params=grant(4),
    )(*parts)


def pick_kernel(even_ref, odd_ref, out_ref):
    out_ref[...] = jnp.where(bit_of(*CORE) == 0, even_ref[...], odd_ref[...])


def pick(even, odd):
    return pl.pallas_call(
        pick_kernel,
        in_specs=[VMEM] * 2,
        out_specs=VMEM,
        out_shape=jax.ShapeDtypeStruct(even.shape, F32),
        compiler_params=grant(4),
    )(even, odd)


def update_kernel(*refs):
    sums, (vec_ref, inv_ref, diag_ref, new_ref, energy_ref) = refs[:2 * CHUNKS], refs[2 * CHUNKS:]
    rows, b = new_ref.shape
    shard = rows // CHUNKS
    end = shard * b // TILE[1]
    rho = sums[-2][end:, :] + sums[-1][end:, :]
    energy_ref[...] = rho
    for h in range(CHUNKS):
        mine_ref, recv_ref = sums[2 * h:2 * h + 2]
        at = slice(h * shard, (h + 1) * shard)
        for c in range(b // TILE[1]):
            part = slice(c * shard, (c + 1) * shard)
            lanes = slice(c * TILE[1], (c + 1) * TILE[1])
            normed = vec_ref[at, lanes] * inv_ref[:1, lanes]
            sigma = mine_ref[part, :] + recv_ref[part, :]
            residual = sigma - rho[:1, :] * normed
            gap = jnp.maximum(jnp.abs(diag_ref[at, lanes] - rho[:1, :]), 1.0)
            new_ref[at, lanes] = normed - residual / gap


def update(sums, vec, inv, diag):
    return pl.pallas_call(
        update_kernel,
        in_specs=[VMEM] * (len(sums) + 3),
        out_specs=[VMEM] * 2,
        out_shape=[jax.ShapeDtypeStruct(vec.shape, F32), jax.ShapeDtypeStruct(TILE, F32)],
        compiler_params=grant(4),
    )(*sums, vec, inv, diag)


def take_kernel(first, x_ref, out_ref, sem):
    copy = pltpu.make_async_copy(x_ref.at[0, pl.ds(first, out_ref.shape[0]), :], out_ref, sem)
    copy.start()
    copy.wait()


def take(x, first, rows):
    return pl.pallas_call(
        functools.partial(take_kernel, first),
        in_specs=[pl.BlockSpec(memory_space=pl.ANY)],
        out_specs=VMEM,
        out_shape=jax.ShapeDtypeStruct((rows, x.shape[-1]), x.dtype),
        scratch_shapes=[pltpu.SemaphoreType.DMA],
        compiler_params=grant(4),
    )(x)


def zero_tile(tile):
    def kernel(in_ref, out_ref):
        out_ref[...] = jnp.zeros_like(out_ref)

    return pl.pallas_call(
        kernel, in_specs=[VMEM], out_specs=VMEM, out_shape=jax.ShapeDtypeStruct(TILE, F32), compiler_params=grant(4)
    )(tile)


def join_kernel(*refs):
    *parts, out_ref = refs
    rows = parts[0].shape[0] // CHUNKS
    for k, part in enumerate(parts):
        _, row = piece_place(k, 0, rows)
        for h in range(CHUNKS):
            at = pl.ds(pl.multiple_of(row + h * 4 * rows, 8), rows)
            out_ref[0, at, :] = part[h * rows:(h + 1) * rows, :]


def join(parts):
    quarter, b = parts[0].shape
    return pl.pallas_call(
        join_kernel,
        in_specs=[VMEM] * len(parts),
        out_specs=VMEM,
        out_shape=jax.ShapeDtypeStruct((1, 4 * quarter, b), F32),
        compiler_params=grant(4),
    )(*parts)


def flips(mesh_shape, even, odd):
    terms, sectors = mesh_shape
    pairs = []
    for t in range(terms):
        for s in range(sectors):
            u = {"term": t, "sector": s}
            for axis, bit in odd if s & 1 else even:
                u[axis] ^= 1 << bit
            pairs.append((t * sectors + s, u["term"] * sectors + u["sector"]))
    return pairs


def rest_dims(terms):
    return [("term", bit) for bit in range(2, terms.bit_length() - 1)]


def shards(mesh_shape, psi_start, diagonal, left_ops, right_ops, pair_in, pair_out, pair_count):
    terms, sectors = mesh_shape
    b = psi_start.shape[1]
    cells = float(sectors * b * b)

    def swap(x, even, odd=None):
        return lax.ppermute(x, AXES, flips(mesh_shape, even, even if odd is None else odd))

    def dims_of(k):
        return [dim for i, dim in enumerate(DIMS) if (k >> (2 - i)) & 1]

    away = START_ORDER
    rest = rest_dims(terms)

    own = psi_start[0]
    rows = b // CHUNKS
    far = []
    for h in range(CHUNKS):
        far.append(swap(take(psi_start, h * rows, rows), [DIMS[0]]))
    beside = swap(own, [CORE])
    left, right, vec, diag = prepare(left_ops, right_ops, psi_start, diagonal)
    far[0], left, right, vec, diag = lax.optimization_barrier((far[0], left, right, vec, diag))
    pieces = [own, beside]
    for x in far:
        pieces += [x, swap(x, [CORE])]
    zero = jnp.zeros(TILE, F32)
    energies = []
    for sweep in range(ITERS):
        first = sweep == 0
        args = (cells, sectors, pair_in, pair_count)
        if first:
            early, late = ([pieces[i] for i in picked(half, len(pieces))] for half in range(2))
            early = inner(first, 0, *args, early, right)
            cat, inv = inner(first, 1, *args, late, right, early)
        else:
            cat, inv = inner(first, None, *args, pieces, right)
        rho = zero
        keeps, recvs = [], []
        for h in range(CHUNKS):
            send, keep, rho = outer(first, h, cells, sectors, pair_out, pair_count, pieces, (left, cat), inv, rho)
            keeps.append(keep)
            recvs.append(swap(send, [CORE]))
        orders = [[[[DIMS[dim]] for dim in step] for step in zip(*order)] for order in ORDERS]
        for h in range(CHUNKS):
            extra = TILE[0] if h == CHUNKS - 1 else 0
            keeps[h], send = cut(keeps[h], recvs[h], extra, 2)
            recvs[h] = swap(send, *orders[h][0])
        for h in range(CHUNKS):
            extra = TILE[0] if h == CHUNKS - 1 else 0
            slots = cut(keeps[h], recvs[h], extra, 4)
            parts = [slots[0]]
            _, second, third = orders[h]
            both = [a + b for a, b in zip(second, third)]
            for k, dims in ((3, both), (2, second), (1, third)):
                parts.append(swap(slots[k], *dims))
            keeps[h] = parts
        for number, step in enumerate(rest):
            for h in range(CHUNKS):
                keeps[h] = sum_of([keeps[h], recvs[h]] if number else keeps[h])
                recvs[h] = swap(keeps[h], [step])
        sums = [x for pair in zip(keeps, recvs) for x in pair]
        vec, energy = update(sums, vec, inv, diag)
        energies.append(energy[0, 0])
        if sweep < ITERS - 1:
            got = {0: vec}
            zero = zero_tile(energy)
            for k in away:
                got[k] = swap(vec, dims_of(k))
            near = pick(got[5], got[6])
            got[7] = swap(near, [DIMS[1]], [DIMS[2]])
            pieces = []
            for k in range(8):
                pieces += [got[k], swap(got[k], [CORE])]
    got = {k: swap(vec, dims_of(k)) for k in (3, 2, 1)}
    block = join([vec, got[1], got[2], got[3]])
    return block, jnp.stack(energies)


def solution(mesh):
    mesh_shape = (mesh.shape["term"], mesh.shape["sector"])
    return jax.shard_map(
        functools.partial(shards, mesh_shape),
        mesh=mesh,
        in_specs=(
            P("sector", None, None),
            P("sector", None, None),
            P(("term", "sector"), None, None),
            P(("term", "sector"), None, None),
            P(("term", "sector"), None),
            P(("term", "sector"), None),
            P(("term", "sector")),
        ),
        out_specs=(P("sector", None, None), P()),
        check_vma=False,
    )
```

```python
import functools

import jax
import jax.numpy as jnp
from jax import lax
from jax.experimental import pallas as pl
from jax.experimental.pallas import tpu as pltpu
from jax.sharding import PartitionSpec as P


ITERS = 2
AXES = ("term", "sector")
TILE = (8, 128)
CHUNKS = 2

epsilon = 1e-06


VMEM = pl.BlockSpec(memory_space=pltpu.VMEM)
SMEM = pl.BlockSpec(memory_space=pltpu.SMEM)
F32 = jnp.float32
BF16 = jnp.bfloat16

DIMS = (("sector", 1), ("term", 0), ("term", 1))
CORE = ("sector", 0)
ORDERS = (((0, 1, 2), (2, 1, 0)), ((1, 0, 2), (2, 1, 0)))
START_ORDER = (6, 5, 4, 2, 1, 3)


def matmul_cost(pairs, rows, b):
    return pl.CostEstimate(
        flops=6 * pairs * rows * b * b, bytes_accessed=8 * pairs * b * b, transcendentals=0
    )


def grant(mib):
    return pltpu.CompilerParams(vmem_limit_bytes=mib << 20)


def bit_of(axis, bit):
    return (lax.axis_index(axis) >> bit) & 1


def place(bits, parity, rows):
    return 2 * bits[0] + parity, pl.multiple_of((2 * bits[1] + bits[2]) * rows, 8)


def piece_place(k, parity, rows):
    return place([bit_of(*dim) ^ ((k >> (2 - i)) & 1) for i, dim in enumerate(DIMS)], parity, rows)


def slot_of(chunk, parity, masks):
    a, b = (sum(masks[dim] << (2 - i) for i, dim in enumerate(order)) for order in ORDERS[chunk])
    return jnp.where(parity == 0, a, b)


def split(x):
    high = x.astype(BF16)
    return high, (x - high.astype(F32)).astype(BF16)


def segments(first, rows, shard):
    me = lax.axis_index("sector")
    if first:
        out = [[(h, me ^ side, h * rows, 0, rows) for h in range(CHUNKS)] for side in range(2)]
        out += [[(h, me ^ (2 + side), 0, 0, rows)] for h in range(CHUNKS) for side in range(2)]
        return out
    out = []
    for number in range(16):
        sector, row = piece_place(number >> 1, (me & 1) ^ (number & 1), shard)
        out.append([(h, sector, h * shard, row, shard) for h in range(CHUNKS)])
    return out


def prep_kernel(left_ref, right_ref, psi_ref, diag_ref, left_cat, right_cat, vec_ref, mine_ref):
    b = left_ref.shape[-1]

    def one(p, carry):
        high, low = split(left_ref[p])
        for place, x in enumerate((high, low, high)):
            left_cat[p, :, place * b:(place + 1) * b] = x
        high, low = split(right_ref[p])
        for place, x in enumerate((high, high, low)):
            right_cat[p, :, place * b:(place + 1) * b] = x
        return carry

    lax.fori_loop(0, left_ref.shape[0], one, 0)
    rows = vec_ref.shape[0] // CHUNKS
    for h in range(CHUNKS):
        _, row = piece_place(0, 0, rows)
        at = pl.ds(pl.multiple_of(row + h * 4 * rows, 8), rows)
        vec_ref[h * rows:(h + 1) * rows, :] = psi_ref[0, at, :]
        mine_ref[h * rows:(h + 1) * rows, :] = diag_ref[0, at, :]


def prepare(left_ops, right_ops, psi, diag):
    pairs, b, _ = left_ops.shape
    shard = jax.ShapeDtypeStruct((b // 4, b), F32)
    return pl.pallas_call(
        prep_kernel,
        in_specs=[VMEM] * 4,
        out_specs=[VMEM] * 4,
        out_shape=[jax.ShapeDtypeStruct((pairs, b, 3 * b), BF16)] * 2 + [shard] * 2,
        compiler_params=grant(16),
        cost_estimate=pl.CostEstimate(
            flops=4 * left_ops.size, bytes_accessed=20 * left_ops.size, transcendentals=0
        ),
    )(left_ops, right_ops, psi, diag)


def store_wide(dest, start, x):
    rows = x.shape[0]
    for c in range(x.shape[1] // TILE[1]):
        dest[pl.ds(start + c * rows, rows), :] = x[:, c * TILE[1]:(c + 1) * TILE[1]]


DOT_NT = functools.partial(
    lax.dot_general, dimension_numbers=(((1,), (1,)), ((), ())), preferred_element_type=F32
)
DOT = functools.partial(jnp.dot, preferred_element_type=F32)


def inner_kernel(first, half, cells, pieces, *refs):
    in_ref, count_ref, *refs = refs
    parts = refs[:pieces]
    refs = refs[pieces:]
    if half == 0:
        right, early_h, early_l, squares_ref, vec = refs
    elif half == 1:
        right, early_h, early_l, squares_ref, cat_ref, inv_ref, vec = refs
    else:
        right, cat_ref, inv_ref, vec = refs
    b = right.shape[1]
    rows = b // CHUNKS
    shard = rows // 4
    total = jnp.zeros((1, b), F32)
    cuts_of = segments(first, rows, shard)
    for piece, cuts in zip(parts, [cuts_of[i] for i in picked(half, len(cuts_of))]):
        for chunk, sector, start, row, size in cuts:
            if half is not None and chunk != half:
                continue
            x = piece[start:start + size, :]
            high, low = split(x)
            total += jnp.sum(x * x, axis=0, keepdims=True)
            if half is None:
                row = pl.multiple_of(row + chunk * rows, 16)
            at = pl.ds(row, size)
            for place, y in enumerate((high, low, high)):
                vec[sector, at, place * b:(place + 1) * b] = y
    total = jnp.broadcast_to(jnp.sum(total, axis=1, keepdims=True), (TILE[0], b))
    if half == 0:
        squares_ref[...] = total
    else:
        if half == 1:
            total += squares_ref[...]
        inv_ref[...] = lax.rsqrt(total / cells + epsilon)

    def one_pair(p, carry):
        high, low = split(DOT_NT(vec[in_ref[0, p]], right[p]))
        if half == 0:
            early_h[p], early_l[p] = high, low
            return carry
        moves = [(high, low, 0)] if half is None else [(early_h[p], early_l[p], 0), (high, low, rows)]
        for h, l, row in moves:
            for place, y in enumerate((h, h, l)):
                cat_ref[p, place * b + row:place * b + row + h.shape[0], :] = y
        return carry

    lax.fori_loop(0, count_ref[0], one_pair, 0)


def picked(half, pieces):
    return list(range(pieces)) if half is None else [0, 1, 2 + 2 * half, 3 + 2 * half]


def inner(first, half, cells, sectors, pair_in, pair_count, pieces, right, early=()):
    pairs, b, _ = right.shape
    rows = b if half is None else b // CHUNKS
    compact = jax.ShapeDtypeStruct((pairs, rows, b), BF16)
    row = jax.ShapeDtypeStruct((TILE[0], b), F32)
    shapes = [compact, compact, row] if half == 0 else [jax.ShapeDtypeStruct((pairs, 3 * b, b), BF16), row]
    return pl.pallas_call(
        functools.partial(inner_kernel, first, half, cells, len(pieces)),
        in_specs=[SMEM] * 2 + [VMEM] * (len(pieces) + 1 + len(early)),
        out_specs=[VMEM] * len(shapes),
        out_shape=shapes,
        scratch_shapes=[pltpu.VMEM((sectors, rows, 3 * b), BF16)],
        compiler_params=grant(16),
        cost_estimate=matmul_cost(pairs, rows, b),
    )(pair_in, pair_count, *pieces, right, *early)


def outer_kernel(first, chunk, cells, pieces, *refs):
    out_ref, count_ref, *refs = refs
    parts = refs[:pieces]
    left, cat, inv_ref, before_ref, send_ref, keep_ref, rho_ref, acc = refs[pieces:]
    _, rows, b = acc.shape
    shard = rows // 4
    core = lax.axis_index("sector") & 1
    acc[...] = jnp.zeros_like(acc)
    here = slice(chunk * rows, (chunk + 1) * rows)

    def one_pair(p, carry):
        target = out_ref[0, p]
        acc[target] += DOT(left[p, here, :], cat[p])
        return carry

    lax.fori_loop(0, count_ref[0], one_pair, 0)
    scale = inv_ref[:1, :]
    rho = jnp.zeros((1, b), F32)
    wide = shard * b // TILE[1]
    for number, (piece, cuts) in enumerate(zip(parts, segments(first, rows, shard))):
        side = number & 1
        dest = send_ref if side else keep_ref
        for at, sector, start, row, size in cuts:
            if at != chunk:
                continue
            for q in range(size // shard):
                if first:
                    masks = (int(number > 1), (q >> 1) ^ bit_of(*DIMS[1]), (q & 1) ^ bit_of(*DIMS[2]))
                    here = pl.ds(q * shard, shard)
                else:
                    masks = tuple((number >> (3 - i)) & 1 for i in range(3))
                    here = pl.ds(row, shard)
                x = acc[sector, here, :] * scale
                slot = slot_of(chunk, core ^ side, masks)
                store_wide(dest, pl.multiple_of(slot * wide, 8), x)
                rho += jnp.sum(x * piece[start + q * shard:start + (q + 1) * shard, :], axis=0, keepdims=True)
    rho = jnp.broadcast_to(jnp.sum(rho * scale, axis=1, keepdims=True), TILE) / cells + before_ref[...]
    rho_ref[...] = rho
    if chunk == CHUNKS - 1:
        send_ref[8 * wide:, :] = rho
        keep_ref[8 * wide:, :] = rho


def outer(first, chunk, cells, sectors, pair_out, pair_count, pieces, ops, inv, before):
    pairs, _, b = ops[1].shape
    rows = b // CHUNKS
    extra = TILE[0] if chunk == CHUNKS - 1 else 0
    half = jax.ShapeDtypeStruct((sectors * rows // 2 * b // TILE[1] + extra, TILE[1]), F32)
    return pl.pallas_call(
        functools.partial(outer_kernel, first, chunk, cells, len(pieces)),
        in_specs=[SMEM] * 2 + [VMEM] * (len(pieces) + 4),
        out_specs=[VMEM] * 3,
        out_shape=[half, half, jax.ShapeDtypeStruct(TILE, F32)],
        scratch_shapes=[pltpu.VMEM((sectors, rows, b), F32)],
        compiler_params=grant(20),
        cost_estimate=matmul_cost(pairs, rows, b),
    )(pair_out, pair_count, *pieces, *ops, inv, before)


def cut_kernel(extra, keep_ref, recv_ref, *slots):
    rows = slots[0].shape[0] - extra
    end = len(slots) * rows
    for k, slot in enumerate(slots):
        slot[:rows, :] = keep_ref[k * rows:(k + 1) * rows, :] + recv_ref[k * rows:(k + 1) * rows, :]
        if extra:
            slot[rows:, :] = keep_ref[end:, :] + recv_ref[end:, :]


def cut(keep, recv, extra, ways):
    shape = jax.ShapeDtypeStruct(((recv.shape[0] - extra) // ways + extra, TILE[1]), F32)
    return pl.pallas_call(
        functools.partial(cut_kernel, extra),
        in_specs=[VMEM] * 2,
        out_specs=[VMEM] * ways,
        out_shape=[shape] * ways,
        compiler_params=grant(4),
    )(keep, recv)


def sum_kernel(*refs):
    *parts, out_ref = refs
    total = parts[0][...]
    for part in parts[1:]:
        total += part[...]
    out_ref[...] = total


def sum_of(parts):
    return pl.pallas_call(
        sum_kernel,
        in_specs=[VMEM] * len(parts),
        out_specs=VMEM,
        out_shape=jax.ShapeDtypeStruct(parts[0].shape, F32),
        compiler_params=grant(4),
    )(*parts)


def pick_kernel(even_ref, odd_ref, out_ref):
    out_ref[...] = jnp.where(bit_of(*CORE) == 0, even_ref[...], odd_ref[...])


def pick(even, odd):
    return pl.pallas_call(
        pick_kernel,
        in_specs=[VMEM] * 2,
        out_specs=VMEM,
        out_shape=jax.ShapeDtypeStruct(even.shape, F32),
        compiler_params=grant(4),
    )(even, odd)


def update_kernel(*refs):
    sums, (vec_ref, inv_ref, diag_ref, new_ref, energy_ref) = refs[:2 * CHUNKS], refs[2 * CHUNKS:]
    rows, b = new_ref.shape
    shard = rows // CHUNKS
    end = shard * b // TILE[1]
    rho = sums[-2][end:, :] + sums[-1][end:, :]
    energy_ref[...] = rho
    for h in range(CHUNKS):
        mine_ref, recv_ref = sums[2 * h:2 * h + 2]
        at = slice(h * shard, (h + 1) * shard)
        for c in range(b // TILE[1]):
            part = slice(c * shard, (c + 1) * shard)
            lanes = slice(c * TILE[1], (c + 1) * TILE[1])
            normed = vec_ref[at, lanes] * inv_ref[:1, lanes]
            sigma = mine_ref[part, :] + recv_ref[part, :]
            residual = sigma - rho[:1, :] * normed
            gap = jnp.maximum(jnp.abs(diag_ref[at, lanes] - rho[:1, :]), 1.0)
            new_ref[at, lanes] = normed - residual / gap


def update(sums, vec, inv, diag):
    return pl.pallas_call(
        update_kernel,
        in_specs=[VMEM] * (len(sums) + 3),
        out_specs=[VMEM] * 2,
        out_shape=[jax.ShapeDtypeStruct(vec.shape, F32), jax.ShapeDtypeStruct(TILE, F32)],
        compiler_params=grant(4),
    )(*sums, vec, inv, diag)


def zero_tile(tile):
    def kernel(in_ref, out_ref):
        out_ref[...] = jnp.zeros_like(out_ref)

    return pl.pallas_call(
        kernel, in_specs=[VMEM], out_specs=VMEM, out_shape=jax.ShapeDtypeStruct(TILE, F32), compiler_params=grant(4)
    )(tile)


def join_kernel(*refs):
    *parts, out_ref = refs
    rows = parts[0].shape[0] // CHUNKS
    for k, part in enumerate(parts):
        _, row = piece_place(k, 0, rows)
        for h in range(CHUNKS):
            at = pl.ds(pl.multiple_of(row + h * 4 * rows, 8), rows)
            out_ref[0, at, :] = part[h * rows:(h + 1) * rows, :]


def join(parts):
    quarter, b = parts[0].shape
    return pl.pallas_call(
        join_kernel,
        in_specs=[VMEM] * len(parts),
        out_specs=VMEM,
        out_shape=jax.ShapeDtypeStruct((1, 4 * quarter, b), F32),
        compiler_params=grant(4),
    )(*parts)


def flips(mesh_shape, even, odd):
    terms, sectors = mesh_shape
    pairs = []
    for t in range(terms):
        for s in range(sectors):
            u = {"term": t, "sector": s}
            for axis, bit in odd if s & 1 else even:
                u[axis] ^= 1 << bit
            pairs.append((t * sectors + s, u["term"] * sectors + u["sector"]))
    return pairs


def rest_dims(terms):
    return [("term", bit) for bit in range(2, terms.bit_length() - 1)]


def shards(mesh_shape, psi_start, diagonal, left_ops, right_ops, pair_in, pair_out, pair_count):
    terms, sectors = mesh_shape
    b = psi_start.shape[1]
    cells = float(sectors * b * b)

    def swap(x, even, odd=None):
        return lax.ppermute(x, AXES, flips(mesh_shape, even, even if odd is None else odd))

    def dims_of(k):
        return [dim for i, dim in enumerate(DIMS) if (k >> (2 - i)) & 1]

    away = START_ORDER
    rest = rest_dims(terms)

    own = psi_start[0]
    rows = b // CHUNKS
    far = []
    for h in range(CHUNKS):
        block = own if h == 0 else lax.optimization_barrier(own)
        far.append(swap(block[h * rows:(h + 1) * rows], [DIMS[0]]))
    beside = swap(own, [CORE])
    left, right, vec, diag = prepare(left_ops, right_ops, psi_start, diagonal)
    far[0], left, right, vec, diag = lax.optimization_barrier((far[0], left, right, vec, diag))
    pieces = [own, beside]
    for x in far:
        pieces += [x, swap(x, [CORE])]
    zero = jnp.zeros(TILE, F32)
    energies = []
    for sweep in range(ITERS):
        first = sweep == 0
        args = (cells, sectors, pair_in, pair_count)
        if first:
            early, late = ([pieces[i] for i in picked(half, len(pieces))] for half in range(2))
            early = inner(first, 0, *args, early, right)
            cat, inv = inner(first, 1, *args, late, right, early)
        else:
            cat, inv = inner(first, None, *args, pieces, right)
        rho = zero
        keeps, recvs = [], []
        for h in range(CHUNKS):
            send, keep, rho = outer(first, h, cells, sectors, pair_out, pair_count, pieces, (left, cat), inv, rho)
            keeps.append(keep)
            recvs.append(swap(send, [CORE]))
        orders = [[[[DIMS[dim]] for dim in step] for step in zip(*order)] for order in ORDERS]
        for h in range(CHUNKS):
            extra = TILE[0] if h == CHUNKS - 1 else 0
            keeps[h], send = cut(keeps[h], recvs[h], extra, 2)
            recvs[h] = swap(send, *orders[h][0])
        for h in range(CHUNKS):
            extra = TILE[0] if h == CHUNKS - 1 else 0
            slots = cut(keeps[h], recvs[h], extra, 4)
            parts = [slots[0]]
            _, second, third = orders[h]
            both = [a + b for a, b in zip(second, third)]
            for k, dims in ((3, both), (2, second), (1, third)):
                parts.append(swap(slots[k], *dims))
            keeps[h] = parts
        for number, step in enumerate(rest):
            for h in range(CHUNKS):
                keeps[h] = sum_of([keeps[h], recvs[h]] if number else keeps[h])
                recvs[h] = swap(keeps[h], [step])
        sums = [x for pair in zip(keeps, recvs) for x in pair]
        vec, energy = update(sums, vec, inv, diag)
        energies.append(energy[0, 0])
        if sweep < ITERS - 1:
            got = {0: vec}
            zero = zero_tile(energy)
            for k in away:
                got[k] = swap(vec, dims_of(k))
            near = pick(got[5], got[6])
            got[7] = swap(near, [DIMS[1]], [DIMS[2]])
            pieces = []
            for k in range(8):
                pieces += [got[k], swap(got[k], [CORE])]
    got = {k: swap(vec, dims_of(k)) for k in (3, 2, 1)}
    block = join([vec, got[1], got[2], got[3]])
    return block, jnp.stack(energies)


def solution(mesh):
    mesh_shape = (mesh.shape["term"], mesh.shape["sector"])
    return jax.shard_map(
        functools.partial(shards, mesh_shape),
        mesh=mesh,
        in_specs=(
            P("sector", None, None),
            P("sector", None, None),
            P(("term", "sector"), None, None),
            P(("term", "sector"), None, None),
            P(("term", "sector"), None),
            P(("term", "sector"), None),
            P(("term", "sector")),
        ),
        out_specs=(P("sector", None, None), P()),
        check_vma=False,
    )
```

```python
import functools

import jax
import jax.numpy as jnp
from jax import lax
from jax.experimental import pallas as pl
from jax.experimental.pallas import tpu as pltpu
from jax.sharding import PartitionSpec as P


ITERS = 2
AXES = ("term", "sector")
TILE = (8, 128)
CHUNKS = 2

epsilon = 1e-06


VMEM = pl.BlockSpec(memory_space=pltpu.VMEM)
SMEM = pl.BlockSpec(memory_space=pltpu.SMEM)
F32 = jnp.float32
BF16 = jnp.bfloat16

DIMS = (("sector", 1), ("term", 0), ("term", 1))
CORE = ("sector", 0)
ORDERS = (((0, 1, 2), (2, 1, 0)), ((1, 0, 2), (2, 1, 0)))
START_ORDER = (6, 5, 4, 2, 1, 3)


def matmul_cost(pairs, rows, b):
    return pl.CostEstimate(
        flops=6 * pairs * rows * b * b, bytes_accessed=8 * pairs * b * b, transcendentals=0
    )


def grant(mib):
    return pltpu.CompilerParams(vmem_limit_bytes=mib << 20)


def bit_of(axis, bit):
    return (lax.axis_index(axis) >> bit) & 1


def place(bits, parity, rows):
    return 2 * bits[0] + parity, pl.multiple_of((2 * bits[1] + bits[2]) * rows, 8)


def piece_place(k, parity, rows):
    return place([bit_of(*dim) ^ ((k >> (2 - i)) & 1) for i, dim in enumerate(DIMS)], parity, rows)


def slot_of(chunk, parity, masks):
    a, b = (sum(masks[dim] << (2 - i) for i, dim in enumerate(order)) for order in ORDERS[chunk])
    return jnp.where(parity == 0, a, b)


def split(x):
    high = x.astype(BF16)
    return high, (x - high.astype(F32)).astype(BF16)


def segments(first, rows, shard):
    me = lax.axis_index("sector")
    if first:
        out = [[(h, me ^ side, h * rows, 0, rows) for h in range(CHUNKS)] for side in range(2)]
        out += [[(h, me ^ (2 + side), 0, 0, rows)] for h in range(CHUNKS) for side in range(2)]
        return out
    out = []
    for number in range(16):
        sector, row = piece_place(number >> 1, (me & 1) ^ (number & 1), shard)
        out.append([(h, sector, h * shard, row, shard) for h in range(CHUNKS)])
    return out


def prep_kernel(left_ref, right_ref, psi_ref, diag_ref, left_cat, right_cat, vec_ref, mine_ref):
    b = left_ref.shape[-1]

    def one(p, carry):
        high, low = split(left_ref[p])
        for place, x in enumerate((high, low, high)):
            left_cat[p, :, place * b:(place + 1) * b] = x
        high, low = split(right_ref[p])
        for place, x in enumerate((high, high, low)):
            right_cat[p, :, place * b:(place + 1) * b] = x
        return carry

    lax.fori_loop(0, left_ref.shape[0], one, 0)
    rows = vec_ref.shape[0] // CHUNKS
    for h in range(CHUNKS):
        _, row = piece_place(0, 0, rows)
        at = pl.ds(pl.multiple_of(row + h * 4 * rows, 8), rows)
        vec_ref[h * rows:(h + 1) * rows, :] = psi_ref[0, at, :]
        mine_ref[h * rows:(h + 1) * rows, :] = diag_ref[0, at, :]


def prepare(left_ops, right_ops, psi, diag):
    pairs, b, _ = left_ops.shape
    shard = jax.ShapeDtypeStruct((b // 4, b), F32)
    return pl.pallas_call(
        prep_kernel,
        in_specs=[VMEM] * 4,
        out_specs=[VMEM] * 4,
        out_shape=[jax.ShapeDtypeStruct((pairs, b, 3 * b), BF16)] * 2 + [shard] * 2,
        compiler_params=grant(16),
        cost_estimate=pl.CostEstimate(
            flops=4 * left_ops.size, bytes_accessed=20 * left_ops.size, transcendentals=0
        ),
    )(left_ops, right_ops, psi, diag)


def store_wide(dest, start, x):
    rows = x.shape[0]
    for c in range(x.shape[1] // TILE[1]):
        dest[pl.ds(start + c * rows, rows), :] = x[:, c * TILE[1]:(c + 1) * TILE[1]]


DOT_NT = functools.partial(
    lax.dot_general, dimension_numbers=(((1,), (1,)), ((), ())), preferred_element_type=F32
)
DOT = functools.partial(jnp.dot, preferred_element_type=F32)


def inner_kernel(first, half, cells, pieces, *refs):
    in_ref, count_ref, *refs = refs
    parts = refs[:pieces]
    refs = refs[pieces:]
    if half == 0:
        right, early_h, early_l, squares_ref, vec = refs
    elif half == 1:
        right, early_h, early_l, squares_ref, cat_ref, inv_ref, vec = refs
    else:
        right, cat_ref, inv_ref, vec = refs
    b = right.shape[1]
    rows = b // CHUNKS
    shard = rows // 4
    total = jnp.zeros((1, b), F32)
    cuts_of = segments(first, rows, shard)
    for piece, cuts in zip(parts, [cuts_of[i] for i in picked(half, len(cuts_of))]):
        for chunk, sector, start, row, size in cuts:
            if half is not None and chunk != half:
                continue
            x = piece[start:start + size, :]
            high, low = split(x)
            total += jnp.sum(x * x, axis=0, keepdims=True)
            if half is None:
                row = pl.multiple_of(row + chunk * rows, 16)
            at = pl.ds(row, size)
            for place, y in enumerate((high, low, high)):
                vec[sector, at, place * b:(place + 1) * b] = y
    total = jnp.broadcast_to(jnp.sum(total, axis=1, keepdims=True), (TILE[0], b))
    if half == 0:
        squares_ref[...] = total
    else:
        if half == 1:
            total += squares_ref[...]
        inv_ref[...] = lax.rsqrt(total / cells + epsilon)

    def one_pair(p, carry):
        high, low = split(DOT_NT(vec[in_ref[0, p]], right[p]))
        if half == 0:
            early_h[p], early_l[p] = high, low
            return carry
        moves = [(high, low, 0)] if half is None else [(early_h[p], early_l[p], 0), (high, low, rows)]
        for h, l, row in moves:
            for place, y in enumerate((h, h, l)):
                cat_ref[p, place * b + row:place * b + row + h.shape[0], :] = y
        return carry

    lax.fori_loop(0, count_ref[0], one_pair, 0)


def picked(half, pieces):
    return list(range(pieces)) if half is None else [0, 1, 2 + 2 * half, 3 + 2 * half]


def inner(first, half, cells, sectors, pair_in, pair_count, pieces, right, early=()):
    pairs, b, _ = right.shape
    rows = b if half is None else b // CHUNKS
    compact = jax.ShapeDtypeStruct((pairs, rows, b), BF16)
    row = jax.ShapeDtypeStruct((TILE[0], b), F32)
    shapes = [compact, compact, row] if half == 0 else [jax.ShapeDtypeStruct((pairs, 3 * b, b), BF16), row]
    return pl.pallas_call(
        functools.partial(inner_kernel, first, half, cells, len(pieces)),
        in_specs=[SMEM] * 2 + [VMEM] * (len(pieces) + 1 + len(early)),
        out_specs=[VMEM] * len(shapes),
        out_shape=shapes,
        scratch_shapes=[pltpu.VMEM((sectors, rows, 3 * b), BF16)],
        compiler_params=grant(16),
        cost_estimate=matmul_cost(pairs, rows, b),
    )(pair_in, pair_count, *pieces, right, *early)


def outer_kernel(first, chunk, cells, pieces, *refs):
    out_ref, count_ref, *refs = refs
    parts = refs[:pieces]
    left, cat, inv_ref, before_ref, send_ref, keep_ref, rho_ref, acc = refs[pieces:]
    _, rows, b = acc.shape
    shard = rows // 4
    core = lax.axis_index("sector") & 1
    acc[...] = jnp.zeros_like(acc)
    here = slice(chunk * rows, (chunk + 1) * rows)

    def one_pair(p, carry):
        target = out_ref[0, p]
        acc[target] += DOT(left[p, here, :], cat[p])
        return carry

    lax.fori_loop(0, count_ref[0], one_pair, 0)
    scale = inv_ref[:1, :]
    rho = jnp.zeros((1, b), F32)
    wide = shard * b // TILE[1]
    for number, (piece, cuts) in enumerate(zip(parts, segments(first, rows, shard))):
        side = number & 1
        dest = send_ref if side else keep_ref
        for at, sector, start, row, size in cuts:
            if at != chunk:
                continue
            for q in range(size // shard):
                if first:
                    masks = (int(number > 1), (q >> 1) ^ bit_of(*DIMS[1]), (q & 1) ^ bit_of(*DIMS[2]))
                    here = pl.ds(q * shard, shard)
                else:
                    masks = tuple((number >> (3 - i)) & 1 for i in range(3))
                    here = pl.ds(row, shard)
                x = acc[sector, here, :] * scale
                slot = slot_of(chunk, core ^ side, masks)
                store_wide(dest, pl.multiple_of(slot * wide, 8), x)
                rho += jnp.sum(x * piece[start + q * shard:start + (q + 1) * shard, :], axis=0, keepdims=True)
    rho = jnp.broadcast_to(jnp.sum(rho * scale, axis=1, keepdims=True), TILE) / cells + before_ref[...]
    rho_ref[...] = rho
    if chunk == CHUNKS - 1:
        send_ref[8 * wide:, :] = rho
        keep_ref[8 * wide:, :] = rho


def outer(first, chunk, cells, sectors, pair_out, pair_count, pieces, ops, inv, before):
    pairs, _, b = ops[1].shape
    rows = b // CHUNKS
    extra = TILE[0] if chunk == CHUNKS - 1 else 0
    half = jax.ShapeDtypeStruct((sectors * rows // 2 * b // TILE[1] + extra, TILE[1]), F32)
    return pl.pallas_call(
        functools.partial(outer_kernel, first, chunk, cells, len(pieces)),
        in_specs=[SMEM] * 2 + [VMEM] * (len(pieces) + 4),
        out_specs=[VMEM] * 3,
        out_shape=[half, half, jax.ShapeDtypeStruct(TILE, F32)],
        scratch_shapes=[pltpu.VMEM((sectors, rows, b), F32)],
        compiler_params=grant(20),
        cost_estimate=matmul_cost(pairs, rows, b),
    )(pair_out, pair_count, *pieces, *ops, inv, before)


def cut_kernel(extra, keep_ref, recv_ref, *slots):
    rows = slots[0].shape[0] - extra
    end = len(slots) * rows
    for k, slot in enumerate(slots):
        slot[:rows, :] = keep_ref[k * rows:(k + 1) * rows, :] + recv_ref[k * rows:(k + 1) * rows, :]
        if extra:
            slot[rows:, :] = keep_ref[end:, :] + recv_ref[end:, :]


def cut(keep, recv, extra, ways):
    shape = jax.ShapeDtypeStruct(((recv.shape[0] - extra) // ways + extra, TILE[1]), F32)
    return pl.pallas_call(
        functools.partial(cut_kernel, extra),
        in_specs=[VMEM] * 2,
        out_specs=[VMEM] * ways,
        out_shape=[shape] * ways,
        compiler_params=grant(4),
    )(keep, recv)


def sum_kernel(*refs):
    *parts, out_ref = refs
    total = parts[0][...]
    for part in parts[1:]:
        total += part[...]
    out_ref[...] = total


def sum_of(parts):
    return pl.pallas_call(
        sum_kernel,
        in_specs=[VMEM] * len(parts),
        out_specs=VMEM,
        out_shape=jax.ShapeDtypeStruct(parts[0].shape, F32),
        compiler_params=grant(4),
    )(*parts)


def pick_kernel(even_ref, odd_ref, out_ref):
    out_ref[...] = jnp.where(bit_of(*CORE) == 0, even_ref[...], odd_ref[...])


def pick(even, odd):
    return pl.pallas_call(
        pick_kernel,
        in_specs=[VMEM] * 2,
        out_specs=VMEM,
        out_shape=jax.ShapeDtypeStruct(even.shape, F32),
        compiler_params=grant(4),
    )(even, odd)


def update_kernel(*refs):
    sums, (vec_ref, inv_ref, diag_ref, new_ref, energy_ref) = refs[:2 * CHUNKS], refs[2 * CHUNKS:]
    rows, b = new_ref.shape
    shard = rows // CHUNKS
    end = shard * b // TILE[1]
    rho = sums[-2][end:, :] + sums[-1][end:, :]
    energy_ref[...] = rho
    for h in range(CHUNKS):
        mine_ref, recv_ref = sums[2 * h:2 * h + 2]
        at = slice(h * shard, (h + 1) * shard)
        for c in range(b // TILE[1]):
            part = slice(c * shard, (c + 1) * shard)
            lanes = slice(c * TILE[1], (c + 1) * TILE[1])
            normed = vec_ref[at, lanes] * inv_ref[:1, lanes]
            sigma = mine_ref[part, :] + recv_ref[part, :]
            residual = sigma - rho[:1, :] * normed
            gap = jnp.maximum(jnp.abs(diag_ref[at, lanes] - rho[:1, :]), 1.0)
            new_ref[at, lanes] = normed - residual / gap


def update(sums, vec, inv, diag):
    return pl.pallas_call(
        update_kernel,
        in_specs=[VMEM] * (len(sums) + 3),
        out_specs=[VMEM] * 2,
        out_shape=[jax.ShapeDtypeStruct(vec.shape, F32), jax.ShapeDtypeStruct(TILE, F32)],
        compiler_params=grant(4),
    )(*sums, vec, inv, diag)


def zero_tile(tile):
    def kernel(in_ref, out_ref):
        out_ref[...] = jnp.zeros_like(out_ref)

    return pl.pallas_call(
        kernel, in_specs=[VMEM], out_specs=VMEM, out_shape=jax.ShapeDtypeStruct(TILE, F32), compiler_params=grant(4)
    )(tile)


def join_kernel(*refs):
    *parts, out_ref = refs
    rows = parts[0].shape[0] // CHUNKS
    for k, part in enumerate(parts):
        _, row = piece_place(k, 0, rows)
        for h in range(CHUNKS):
            at = pl.ds(pl.multiple_of(row + h * 4 * rows, 8), rows)
            out_ref[0, at, :] = part[h * rows:(h + 1) * rows, :]


def join(parts):
    quarter, b = parts[0].shape
    return pl.pallas_call(
        join_kernel,
        in_specs=[VMEM] * len(parts),
        out_specs=VMEM,
        out_shape=jax.ShapeDtypeStruct((1, 4 * quarter, b), F32),
        compiler_params=grant(4),
    )(*parts)


def flips(mesh_shape, even, odd):
    terms, sectors = mesh_shape
    pairs = []
    for t in range(terms):
        for s in range(sectors):
            u = {"term": t, "sector": s}
            for axis, bit in odd if s & 1 else even:
                u[axis] ^= 1 << bit
            pairs.append((t * sectors + s, u["term"] * sectors + u["sector"]))
    return pairs


def rest_dims(terms):
    return [("term", bit) for bit in range(2, terms.bit_length() - 1)]


def shards(mesh_shape, psi_start, diagonal, left_ops, right_ops, pair_in, pair_out, pair_count):
    terms, sectors = mesh_shape
    b = psi_start.shape[1]
    cells = float(sectors * b * b)

    def swap(x, even, odd=None):
        return lax.ppermute(x, AXES, flips(mesh_shape, even, even if odd is None else odd))

    def dims_of(k):
        return [dim for i, dim in enumerate(DIMS) if (k >> (2 - i)) & 1]

    away = START_ORDER
    rest = rest_dims(terms)

    own = psi_start[0]
    rows = b // CHUNKS
    far = []
    for h in range(CHUNKS):
        far.append(swap(own[h * rows:(h + 1) * rows], [DIMS[0]]))
    beside = swap(own, [CORE])
    left, right, vec, diag = prepare(left_ops, right_ops, psi_start, diagonal)
    far[0], left, right, vec, diag = lax.optimization_barrier((far[0], left, right, vec, diag))
    pieces = [own, beside]
    for x in far:
        pieces += [x, swap(x, [CORE])]
    zero = jnp.zeros(TILE, F32)
    energies = []
    for sweep in range(ITERS):
        first = sweep == 0
        args = (cells, sectors, pair_in, pair_count)
        if first:
            early, late = ([pieces[i] for i in picked(half, len(pieces))] for half in range(2))
            early = inner(first, 0, *args, early, right)
            cat, inv = inner(first, 1, *args, late, right, early)
        else:
            cat, inv = inner(first, None, *args, pieces, right)
        rho = zero
        keeps, recvs = [], []
        for h in range(CHUNKS):
            send, keep, rho = outer(first, h, cells, sectors, pair_out, pair_count, pieces, (left, cat), inv, rho)
            keeps.append(keep)
            recvs.append(swap(send, [CORE]))
        orders = [[[[DIMS[dim]] for dim in step] for step in zip(*order)] for order in ORDERS]
        for h in range(CHUNKS):
            extra = TILE[0] if h == CHUNKS - 1 else 0
            keeps[h], send = cut(keeps[h], recvs[h], extra, 2)
            recvs[h] = swap(send, *orders[h][0])
        for h in range(CHUNKS):
            extra = TILE[0] if h == CHUNKS - 1 else 0
            slots = cut(keeps[h], recvs[h], extra, 4)
            parts = [slots[0]]
            _, second, third = orders[h]
            both = [a + b for a, b in zip(second, third)]
            for k, dims in ((3, both), (2, second), (1, third)):
                parts.append(swap(slots[k], *dims))
            keeps[h] = parts
        for number, step in enumerate(rest):
            for h in range(CHUNKS):
                keeps[h] = sum_of([keeps[h], recvs[h]] if number else keeps[h])
                recvs[h] = swap(keeps[h], [step])
        sums = [x for pair in zip(keeps, recvs) for x in pair]
        vec, energy = update(sums, vec, inv, diag)
        energies.append(energy[0, 0])
        if sweep < ITERS - 1:
            got = {0: vec}
            zero = zero_tile(energy)
            for k in away:
                got[k] = swap(vec, dims_of(k))
            near = pick(got[5], got[6])
            got[7] = swap(near, [DIMS[1]], [DIMS[2]])
            pieces = []
            for k in range(8):
                pieces += [got[k], swap(got[k], [CORE])]
    got = {k: swap(vec, dims_of(k)) for k in (2, 3, 1)}
    block = join([vec, got[1], got[2], got[3]])
    return block, jnp.stack(energies)


def solution(mesh):
    mesh_shape = (mesh.shape["term"], mesh.shape["sector"])
    return jax.shard_map(
        functools.partial(shards, mesh_shape),
        mesh=mesh,
        in_specs=(
            P("sector", None, None),
            P("sector", None, None),
            P(("term", "sector"), None, None),
            P(("term", "sector"), None, None),
            P(("term", "sector"), None),
            P(("term", "sector"), None),
            P(("term", "sector")),
        ),
        out_specs=(P("sector", None, None), P()),
        check_vma=False,
    )
```
